256 devices in a mesh: rollout: 2 (over core), context: 32 (over z, x), head: 4 (over y).
Axes of the slice: x: 4, y: 4, z: 8, core: 2. Of those that a mesh axis runs over, the one named last changes fastest.
Arguments:
- inner_raw: bfloat16 [16384, 8192], P(('rollout', 'context', 'head')), parts along dimension 0, may hold values from -6 to 6
- pairs_raw: bfloat16 [16384, 8, 2, 128], P(('rollout', 'context', 'head')), parts along dimension 0, may hold values from -2.5 to 2.5
- gate_raw: bfloat16 [16384, 8192], P(('rollout', 'context'), 'head'), parts along dimension 0, may hold values from -6 to 6
- step_raw: bfloat16 [16384, 128], P(('rollout', 'context'), 'head'), parts along dimension 0, may hold values from -3 to 3
- step_bias: float32 [128], P('head'), may hold values from -0.5 to 0.5
- rate_log: float32 [128], P('head'), may hold values from -13.5 to -2.8, as said below
- skip_gain: float32 [128], P('head'), may hold values from 0.5 to 2
- conv_inner: float32 [5, 8192], replicated, may hold values from -2.5 to 2.5
- conv_pairs: float32 [5, 8, 2, 128], replicated, may hold values from -2.5 to 2.5
- norm_gain: float32 [8192], P('head'), may hold values from 0.5 to 1.5
Outputs:
- mixer_out: bfloat16 [16384, 8192], P(('rollout', 'context', 'head')), parts along dimension 0
The draws below stay inside these ranges and needn't reach their ends.
There are 2 independent parts, one for each index of `rollout`. The reference program is written for one: setup_inputs(seed, part) draws one part's arguments, and reference() takes and returns one part's arrays. A program takes and returns all parts, laid end to end along the dimension named above; an argument that names none is the same for every part. Nothing has to cross between parts.
Inputs may be any that keep to these rules, and one draw needn't show every extreme that they name: `rate_log`: one value a head.
All inputs are finite; a program needn't handle non-finite values.
Results may differ from the reference program's by a relative error of at most 0.012.
The reference program's roundings to bfloat16 on the way (of `inner_conv`) count: a program that leaves them out, or rounds other values in their place, can miss the bound.
Values may be sent and summed in bfloat16 or wider, within the bound.
No kernel may reach another device: no remote copies, remote signals or barrier semaphores. Data moves between devices by JAX's collectives and lax.ppermute only.
A program may use at most 128 MiB of HBM per device.

```python
import jax
import jax.numpy as jnp
from jax import lax

D_INNER = 8192
HEADS = 128
HEAD_DIM = 64
STATE = 128
GROUPS = 8
CONV = 4
BLOCK = 256
SEQ = 8192


def draw_rate_log(key, part):
    pick_key = jax.random.fold_in(key, 11)
    level_key = jax.random.fold_in(key, 12)
    slow_share = 0.5
    slow_heads = jax.random.uniform(pick_key, (HEADS,), jnp.float32) < slow_share
    level = jax.random.uniform(level_key, (HEADS,), jnp.float32)
    slow_rate = jnp.log(0.2 / SEQ) + level * jnp.log(5.0)
    fast_rate = jnp.log(0.02) + level * jnp.log(3.0)
    return jnp.where(slow_heads, slow_rate, fast_rate).astype(jnp.float32)


def levels(key, shape, pieces, smallest, largest):
    def one(position, shards_of):
        steps = jax.random.uniform(jax.random.fold_in(jax.random.fold_in(key, 6), position), (shards_of,), jnp.float32, smallest / len(pieces), largest / len(pieces))
        return jnp.repeat(jnp.exp(steps), shape[position] // shards_of).reshape((-1,) + (1,) * (len(shape) - position - 1))

    gain = one(*pieces[0])
    for cut in pieces[1:]:
        gain = gain * one(*cut)
    return gain


def noise(rng, shape, width, reach, shards=(), dtype=jnp.bfloat16):
    array = jax.random.normal(rng, shape, jnp.float32) * width
    if len(shards) > 0:
        array = levels(rng, shape, shards, -0.22, 0.18) * array
    return jnp.clip(array, min=-reach, max=reach).astype(dtype)


def setup_inputs(seed: int = 0, part: int = 0) -> dict:
    streams_of = jax.random.split(jax.random.key(seed), 11)
    part_keys = jax.random.split(jax.random.fold_in(streams_of[10], part), 11)
    inner_raw = noise(part_keys[0], (SEQ, D_INNER), 1.0, 6.0, ((0, 128),))
    pairs_raw = noise(part_keys[1], (SEQ, GROUPS, 2, STATE), 0.35, 2.5, ((0, 128),))
    gate_raw = noise(part_keys[2], (SEQ, D_INNER), 1.0, 6.0, ((0, 32), (1, 4)))
    step_raw = noise(part_keys[3], (SEQ, HEADS), 0.5, 3.0, ((0, 32), (1, 4)))
    step_bias = jnp.clip(jax.random.uniform(streams_of[4], (HEADS,), jnp.float32, -0.5, 0.5) * levels(streams_of[4], (HEADS,), ((0, 4),), -0.4, 0.0), -0.5, 0.5)
    rate_log = draw_rate_log(jax.random.fold_in(streams_of[10], 71), part)
    skip_gain = jnp.clip(0.5 + 1.5 * jax.random.uniform(streams_of[6], (HEADS,), jnp.float32) ** levels(streams_of[6], (HEADS,), ((0, 4),), -0.2, 0.2), 0.5, 2.0)
    conv_inner = noise(streams_of[7], (CONV + 1, D_INNER), 0.5, 2.5, (), jnp.float32)
    conv_pairs = noise(streams_of[8], (CONV + 1, GROUPS, 2, STATE), 0.5, 2.5, (), jnp.float32)
    norm_gain = jnp.clip(1.0 + 0.1 * jax.random.normal(streams_of[9], (D_INNER,), jnp.float32), 0.5, 1.5)
    return dict(inner_raw=inner_raw, pairs_raw=pairs_raw, gate_raw=gate_raw, step_raw=step_raw, step_bias=step_bias, rate_log=rate_log, skip_gain=skip_gain, conv_inner=conv_inner, conv_pairs=conv_pairs, norm_gain=norm_gain)


def convolve(raw_rows, before, weight):
    tap_count = weight.shape[0] - 1
    row_count = raw_rows.shape[0]
    extended = jnp.concatenate([before, raw_rows], axis=0).astype(jnp.float32)
    summed = weight[tap_count][None, :] + weight[0][None, :] * extended[0:row_count]
    for offset in range(1, tap_count):
        summed = summed + weight[offset][None, :] * extended[offset:offset + row_count]
    return jax.nn.silu(summed).astype(jnp.bfloat16)

def block_intra(inner_conv, pairs_conv, step_size, log_cum, groups):
    block_len, head_count = step_size.shape
    per_group = head_count // groups
    head_width = inner_conv.shape[1] // head_count
    pair_view = pairs_conv.reshape(block_len, groups, 2, -1).astype(jnp.float32)
    scores = jnp.einsum('ign,jgn->gij', pair_view[:, :, 1], pair_view[:, :, 0])
    lower_tri = lax.broadcasted_iota(jnp.int32, (block_len, block_len), 0) >= lax.broadcasted_iota(jnp.int32, (block_len, block_len), 1)
    cum_t = log_cum.T
    log_gap = jnp.minimum(cum_t[:, :, None] - cum_t[:, None, :], 0.0)
    decay_mat = jnp.where(lower_tri[None], jnp.exp(log_gap), 0.0) * step_size.T[:, None, :]
    weights = (scores[:, None] * decay_mat.reshape(groups, per_group, block_len, block_len)).astype(jnp.bfloat16)
    inner_view = inner_conv.reshape(block_len, groups, per_group, head_width).astype(jnp.float32)
    intra_out = jnp.einsum('gkij,jgkp->igkp', weights.astype(jnp.float32), inner_view)
    return intra_out.reshape(block_len, head_count * head_width)

def block_state(inner_conv, pairs_conv, step_size, log_cum, groups):
    block_len, head_count = step_size.shape
    per_group = head_count // groups
    head_width = inner_conv.shape[1] // head_count
    tail_w = jnp.exp(log_cum[-1][None, :] - log_cum) * step_size
    weighted = (inner_conv.reshape(block_len, head_count, head_width).astype(jnp.float32) * tail_w[:, :, None]).astype(jnp.bfloat16)
    weighted = weighted.reshape(block_len, groups, per_group, head_width)
    bmat = pairs_conv.reshape(block_len, groups, 2, -1)[:, :, 0]
    local_state = jnp.einsum('jgn,jgkp->gknp', bmat.astype(jnp.float32), weighted.astype(jnp.float32))
    return (local_state.reshape(head_count, -1, head_width), jnp.exp(log_cum[-1]))

def finish(inner_conv, pairs_conv, gate_rows, intra_out, carry_state, log_cum, skip_gain, norm_gain, groups):
    block_len, head_count = log_cum.shape
    per_group = head_count // groups
    head_width = inner_conv.shape[1] // head_count
    cmat = pairs_conv.reshape(block_len, groups, 2, -1)[:, :, 1]
    held = carry_state.astype(jnp.bfloat16).reshape(groups, per_group, -1, head_width)
    carried = jnp.einsum('ign,gknp->igkp', cmat.astype(jnp.float32), held.astype(jnp.float32))
    carried = carried.reshape(block_len, head_count, head_width) * jnp.exp(log_cum)[:, :, None]
    mixed = intra_out + carried.reshape(block_len, -1) + jnp.repeat(skip_gain, head_width)[None, :] * inner_conv.astype(jnp.float32)
    gated_out = mixed * jax.nn.silu(gate_rows.astype(jnp.float32))
    grouped = gated_out.reshape(block_len, groups, -1)
    inv_rms = lax.rsqrt(lax.optimization_barrier(jnp.mean(grouped * grouped, axis=2, keepdims=True)) + 1e-05)
    return ((grouped * inv_rms).reshape(block_len, -1) * norm_gain[None, :]).astype(jnp.bfloat16)

def reference(inner_raw, pairs_raw, gate_raw, step_raw, step_bias, rate_log, skip_gain, conv_inner, conv_pairs, norm_gain):
    tap_count = conv_inner.shape[0] - 1
    block_count = SEQ // BLOCK
    pairs_flat = pairs_raw.reshape(SEQ, -1)
    conv_flat = conv_pairs.reshape(tap_count + 1, -1)
    blocks = (inner_raw.reshape(block_count, BLOCK, D_INNER), pairs_flat.reshape(block_count, BLOCK, -1), gate_raw.reshape(block_count, BLOCK, D_INNER), step_raw.reshape(block_count, BLOCK, HEADS))

    def advance(running, element):
        carry_state, tail_inner, tail_pairs = running
        inner_rows, pair_rows, gate_rows, step_rows = element
        inner_conv = convolve(inner_rows, tail_inner, conv_inner)
        pairs_conv = convolve(pair_rows, tail_pairs, conv_flat)
        step_size = jax.nn.softplus(step_rows.astype(jnp.float32) + step_bias[None, :])
        log_cum = jnp.cumsum(-jnp.exp(rate_log)[None, :] * step_size, axis=0)
        intra_out = block_intra(inner_conv, pairs_conv, step_size, log_cum, GROUPS)
        local_state, block_decay = block_state(inner_conv, pairs_conv, step_size, log_cum, GROUPS)
        result = finish(inner_conv, pairs_conv, gate_rows, intra_out, carry_state, log_cum, skip_gain, norm_gain, GROUPS)
        carry_state = block_decay[:, None, None] * carry_state + local_state
        return ((carry_state, inner_rows[BLOCK - tap_count:], pair_rows[BLOCK - tap_count:]), result)
    start = (jnp.zeros((HEADS, STATE, HEAD_DIM), jnp.float32), jnp.zeros((tap_count, D_INNER), jnp.bfloat16), jnp.zeros((tap_count, pairs_flat.shape[1]), jnp.bfloat16))
    _, results = lax.scan(advance, start, blocks)
    return results.reshape(SEQ, D_INNER)
```

```python
import functools

import jax
import jax.numpy as jnp
from jax import lax
from jax.experimental import pallas as pl
from jax.experimental.pallas import tpu as pltpu
from jax.sharding import PartitionSpec as P

BLOCK = 256
HIGH = lax.Precision.HIGHEST
F32 = jnp.float32
BF16 = jnp.bfloat16
LANES = 128
ANY = pl.BlockSpec(memory_space=pl.ANY)
VMEM = pl.BlockSpec(memory_space=pltpu.VMEM)
SMEM = pl.BlockSpec(memory_space=pltpu.SMEM)
PARAMS = pltpu.CompilerParams(vmem_limit_bytes=48 * 1024 * 1024)


def cost(flops, bytes_accessed, transcendentals=0):
    return pl.CostEstimate(
        flops=flops, bytes_accessed=bytes_accessed, transcendentals=transcendentals
    )


def group_of(member):
    return 2 * (member % 4) + member // 4


def iota(shape, dim):
    return lax.broadcasted_iota(jnp.int32, shape, dim)


def spread(rows, channels, head_width):
    return (iota((rows, channels), 1) // head_width == iota((rows, channels), 0)).astype(F32)


def silu(v):
    return v / (1.0 + jnp.exp(-v))


def pack_kernel(inner, pairs, out, sem):
    wide = inner.shape[1] // 8
    narrow = pairs.shape[1] // 8
    copies = []
    for member in range(8):
        group = group_of(member)
        copies.append(
            pltpu.make_async_copy(
                inner.at[:, pl.ds(group * wide, wide)],
                out.at[member, :, pl.ds(0, wide)],
                sem.at[2 * member],
            )
        )
        copies.append(
            pltpu.make_async_copy(
                pairs.at[:, pl.ds(group * narrow, narrow)],
                out.at[member, :, pl.ds(wide, narrow)],
                sem.at[2 * member + 1],
            )
        )
    for copy in copies:
        copy.start()
    for copy in copies:
        copy.wait()


def pack(inner, pairs):
    rows = inner.shape[0]
    width = (inner.shape[1] + pairs.shape[1]) // 8
    return pl.pallas_call(
        pack_kernel,
        out_shape=jax.ShapeDtypeStruct((8, rows, width), BF16),
        in_specs=[ANY, ANY],
        out_specs=ANY,
        scratch_shapes=[pltpu.SemaphoreType.DMA((16,))],
        compiler_params=PARAMS,
        cost_estimate=cost(0, 4 * 8 * rows * width),
        name="pack",
    )(inner, pairs)


def unpack_kernel(slabs, out, sem):
    wide = slabs.shape[2]
    copies = [
        pltpu.make_async_copy(
            slabs.at[member], out.at[:, pl.ds(group_of(member) * wide, wide)], sem.at[member]
        )
        for member in range(8)
    ]
    for copy in copies:
        copy.start()
    for copy in copies:
        copy.wait()


def unpack(slabs):
    _, rows, wide = slabs.shape
    return pl.pallas_call(
        unpack_kernel,
        out_shape=jax.ShapeDtypeStruct((rows, 8 * wide), BF16),
        in_specs=[ANY],
        out_specs=ANY,
        scratch_shapes=[pltpu.SemaphoreType.DMA((8,))],
        compiler_params=PARAMS,
        cost_estimate=cost(0, 4 * 8 * rows * wide),
        name="unpack",
    )(slabs)


def prep_kernel(side_ref, own, got, bias, rate, lc, dt, lc_t, dt_t):
    side = side_ref[0]
    own_heads = own.shape[1]
    heads = own_heads // 2
    mine = own[...].astype(F32)
    theirs = got[...].astype(F32)
    low = jnp.where(side == 0, mine, theirs)
    high = jnp.where(side == 0, theirs, mine)
    column = iota((own_heads, LANES), 1)
    pick = ((iota((own_heads, LANES), 0) == column + heads * side) & (column < heads)).astype(F32)
    tri = (iota((BLOCK, BLOCK), 0) >= iota((BLOCK, BLOCK), 1)).astype(F32)
    neg_rate = -jnp.exp(rate[...])
    for b, raw in enumerate((low, high)):
        v = raw + bias[...]
        step = jnp.maximum(v, 0.0) + jnp.log1p(jnp.exp(-jnp.abs(v)))
        picked = jnp.dot(step, pick, precision=HIGH, preferred_element_type=F32)
        logs = jnp.dot(step * neg_rate, pick, precision=HIGH, preferred_element_type=F32)
        cum = jnp.dot(tri, logs, precision=HIGH, preferred_element_type=F32)
        lc[b] = cum
        dt[b] = picked
        lc_t[b] = cum.T[:heads]
        dt_t[b] = picked.T[:heads]


def prep(side, own, got, bias, rate):
    heads = own.shape[1] // 2
    tall = jax.ShapeDtypeStruct((2, BLOCK, LANES), F32)
    flat = jax.ShapeDtypeStruct((2, heads, BLOCK), F32)
    return pl.pallas_call(
        prep_kernel,
        out_shape=(tall, tall, flat, flat),
        in_specs=[SMEM, VMEM, VMEM, VMEM, VMEM],
        out_specs=(VMEM,) * 4,
        compiler_params=PARAMS,
        cost_estimate=cost(2 * 10**8, 10**6, 10**5),
        name="prep",
    )(side, own, got, bias, rate)


def taps(ext, row, rows, cols, weight):
    window = ext[pl.ds(row, rows + 8), cols]
    total = weight[4:5] + weight[0:1] * window[4 : 4 + rows]
    for k in range(1, 4):
        total = total + weight[k : k + 1] * window[4 + k : 4 + k + rows]
    return silu(total).astype(BF16)


def conv_kernel(group, recv, w_inner, w_pairs, xc, bc, ext):
    members, rows, width = recv.shape
    wide = xc.shape[1]
    ext[0:8] = jnp.zeros((8, width), F32)
    for m in range(members):
        ext[8 + m * rows : 8 + (m + 1) * rows] = recv[m].astype(F32)

    def chunk(m, _):
        row = pl.multiple_of(m * rows, rows)
        for start in range(0, wide, 128):
            cols = slice(start, start + 128)
            xc[pl.ds(row, rows), cols] = taps(ext, row, rows, cols, w_inner[:, cols])
        for start in range(0, width - wide, 128):
            bc[pl.ds(row, rows), start : start + 128] = taps(
                ext,
                row,
                rows,
                slice(wide + start, wide + start + 128),
                w_pairs[:, start : start + 128],
            )
        return 0

    lax.fori_loop(0, members, chunk, 0)


def conv(group, recv, conv_inner, conv_pairs):
    members, rows, width = recv.shape
    wide = conv_inner.shape[1] // 8
    narrow = width - wide
    total = members * rows
    return pl.pallas_call(
        conv_kernel,
        out_shape=(
            jax.ShapeDtypeStruct((total, wide), BF16),
            jax.ShapeDtypeStruct((total, narrow), BF16),
        ),
        grid_spec=pltpu.PrefetchScalarGridSpec(
            num_scalar_prefetch=1,
            grid=(1,),
            in_specs=[
                pl.BlockSpec((members, rows, width), lambda i, g: (0, 0, 0)),
                pl.BlockSpec((5, wide), lambda i, g: (0, g[0])),
                pl.BlockSpec((5, narrow), lambda i, g: (0, g[0])),
            ],
            out_specs=(
                pl.BlockSpec((total, wide), lambda i, g: (0, 0)),
                pl.BlockSpec((total, narrow), lambda i, g: (0, 0)),
            ),
            scratch_shapes=[pltpu.VMEM((8 + total, width), F32)],
        ),
        compiler_params=PARAMS,
        cost_estimate=cost(20 * total * width, 4 * total * width, 2 * total * width),
        name="conv",
    )(group, recv, conv_inner, conv_pairs)


def state_kernel(
    group, first, halo, w_inner, w_pairs, xc0, bc0, lc, dt, xc, bc, first_state, payload, ext
):
    fix = first.shape[0]
    wide = xc.shape[1]
    narrow = bc.shape[1]
    ext[0:8] = halo[fix - 8 : fix].astype(F32)
    ext[8 : 8 + fix] = first[...].astype(F32)
    xc[...] = xc0[...]
    bc[...] = bc0[...]
    for start in range(0, wide, 128):
        cols = slice(start, start + 128)
        xc[0:fix, cols] = taps(ext, 0, fix, cols, w_inner[:, cols])
    for start in range(0, narrow, 128):
        bc[0:fix, start : start + 128] = taps(
            ext, 0, fix, slice(wide + start, wide + start + 128), w_pairs[:, start : start + 128]
        )
    heads = wide // 64
    one_hot = spread(LANES, wide, wide // heads)
    states = []
    for b in range(2):
        rows = slice(b * BLOCK, (b + 1) * BLOCK)
        cum = lc[b]
        tail = jnp.exp(cum[BLOCK - 1 : BLOCK] - cum) * dt[b]
        tail = jnp.dot(tail, one_hot, precision=HIGH, preferred_element_type=F32)
        weighted = (xc[rows].astype(F32) * tail).astype(BF16)
        states.append(
            lax.dot_general(
                bc[rows, 0:128],
                weighted,
                (((0,), (0,)), ((), ())),
                preferred_element_type=F32,
            )
        )
    last = [lc[b, BLOCK - 1 : BLOCK] for b in range(2)]
    decay = jnp.dot(
        jnp.broadcast_to(jnp.exp(last[1]), (8, LANES)),
        one_hot,
        precision=HIGH,
        preferred_element_type=F32,
    )
    first_state[...] = states[0]
    total = decay[0:1] * states[0] + states[1]
    parts = payload.shape[0]
    payload[:, :, 0:wide] = total.reshape(parts, -1, wide)
    depth = payload.shape[1]
    log_decay = jnp.broadcast_to(last[0] + last[1], (depth, LANES))
    for part in range(parts):
        payload[part, :, wide : wide + LANES] = log_decay


def state(group, first, halo, conv_inner, conv_pairs, xc0, bc0, lc, dt, parts):
    fix, width = first.shape
    total, wide = xc0.shape
    narrow = width - wide
    state_rows = narrow // 2

    def whole(shape):
        return pl.BlockSpec(shape, lambda i, g: (0,) * len(shape))

    payload_shape = (parts, state_rows // parts, wide + LANES)
    return pl.pallas_call(
        state_kernel,
        out_shape=(
            jax.ShapeDtypeStruct((total, wide), BF16),
            jax.ShapeDtypeStruct((total, narrow), BF16),
            jax.ShapeDtypeStruct((state_rows, wide), F32),
            jax.ShapeDtypeStruct(payload_shape, F32),
        ),
        grid_spec=pltpu.PrefetchScalarGridSpec(
            num_scalar_prefetch=1,
            grid=(1,),
            in_specs=[
                whole((fix, width)),
                whole((fix, width)),
                pl.BlockSpec((5, wide), lambda i, g: (0, g[0])),
                pl.BlockSpec((5, narrow), lambda i, g: (0, g[0])),
                whole((total, wide)),
                whole((total, narrow)),
                whole(lc.shape),
                whole(dt.shape),
            ],
            out_specs=(
                whole((total, wide)),
                whole((total, narrow)),
                whole((state_rows, wide)),
                whole(payload_shape),
            ),
            scratch_shapes=[pltpu.VMEM((8 + fix, width), F32)],
        ),
        compiler_params=PARAMS,
        cost_estimate=cost(4 * total * wide * 128, 8 * total * wide),
        name="state",
    )(group, first, halo, conv_inner, conv_pairs, xc0, bc0, lc, dt)


def intra_kernel(side_ref, xc, bc, lc, lc_t, dt_t, skip, out):
    side = side_ref[0]
    wide = xc.shape[1]
    heads = lc_t.shape[1]
    head_width = wide // heads
    state_rows = bc.shape[1] // 2
    scores = lax.dot_general(
        bc[:, state_rows:],
        bc[:, 0:state_rows],
        (((1,), (1,)), ((), ())),
        preferred_element_type=F32,
    )
    lower = iota((BLOCK, BLOCK), 0) >= iota((BLOCK, BLOCK), 1)
    own_heads = skip.shape[1]
    row = iota((own_heads, wide), 0)
    gain = jnp.dot(
        jnp.broadcast_to(skip[...], (8, own_heads)),
        (iota((own_heads, wide), 1) // head_width + heads * side == row).astype(F32),
        precision=HIGH,
        preferred_element_type=F32,
    )[0:1]
    cum = lc[0]
    for pair in range(heads // 2):
        outs = []
        for h in (2 * pair, 2 * pair + 1):
            gap = cum[:, h : h + 1] - lc_t[0, h : h + 1]
            decay = jnp.exp(jnp.where(lower, gap, -jnp.inf))
            weights = (scores * (decay * dt_t[0, h : h + 1])).astype(BF16)
            outs.append(
                jnp.dot(
                    weights,
                    xc[:, h * head_width : (h + 1) * head_width],
                    preferred_element_type=F32,
                )
            )
        cols = slice(2 * pair * head_width, 2 * (pair + 1) * head_width)
        out[:, cols] = jnp.concatenate(outs, axis=1) + gain[:, cols] * xc[:, cols].astype(F32)


def intra(side, xc, bc, lc, lc_t, dt_t, skip):
    total, wide = xc.shape
    narrow = bc.shape[1]
    heads = lc_t.shape[1]
    return pl.pallas_call(
        intra_kernel,
        out_shape=jax.ShapeDtypeStruct((total, wide), F32),
        grid_spec=pltpu.PrefetchScalarGridSpec(
            num_scalar_prefetch=1,
            grid=(total // BLOCK,),
            in_specs=[
                pl.BlockSpec((BLOCK, wide), lambda b, s: (b, 0)),
                pl.BlockSpec((BLOCK, narrow), lambda b, s: (b, 0)),
                pl.BlockSpec((1, BLOCK, LANES), lambda b, s: (b, 0, 0)),
                pl.BlockSpec((1, heads, BLOCK), lambda b, s: (b, 0, 0)),
                pl.BlockSpec((1, heads, BLOCK), lambda b, s: (b, 0, 0)),
                pl.BlockSpec(skip.shape, lambda b, s: (0, 0)),
            ],
            out_specs=pl.BlockSpec((BLOCK, wide), lambda b, s: (b, 0)),
        ),
        compiler_params=PARAMS,
        cost_estimate=cost(2 * total * BLOCK * wide * 4, 8 * total * wide, heads * total * BLOCK),
        name="intra",
    )(side, xc, bc, lc, lc_t, dt_t, skip)


def scan_kernel(recv, out):
    chunks, rows, width = recv.shape
    wide = out.shape[2]
    one_hot = spread(LANES, wide, 64)
    logs = jnp.concatenate([recv[k, 0:1, wide:width] for k in range(chunks)], axis=0)
    decay = jnp.dot(jnp.exp(logs), one_hot, precision=HIGH, preferred_element_type=F32)
    carry = jnp.zeros((rows, wide), F32)
    for k in range(chunks):
        out[k] = carry
        carry = decay[k : k + 1] * carry + recv[k, :, 0:wide]


def scan(recv):
    chunks, rows, width = recv.shape
    return pl.pallas_call(
        scan_kernel,
        out_shape=jax.ShapeDtypeStruct((chunks, rows, width - LANES), F32),
        in_specs=[VMEM],
        out_specs=VMEM,
        compiler_params=PARAMS,
        cost_estimate=cost(4 * chunks * rows * width, 4 * chunks * rows * width),
        name="scan",
    )(recv)


def finish_kernel(side_ref, carry, first_state, bc, lc, lc0, mixed, own, got, gain, out):
    side = side_ref[0]
    b = pl.program_id(0)
    wide = mixed.shape[1]
    state_rows = bc.shape[1] // 2
    one_hot = spread(LANES, wide, 64)
    start = carry[...].reshape(state_rows, wide)
    decay = jnp.dot(
        jnp.broadcast_to(jnp.exp(lc0[0, BLOCK - 1 : BLOCK]), (8, LANES)),
        one_hot,
        precision=HIGH,
        preferred_element_type=F32,
    )[0:1]
    start = jnp.where(b == 0, start, decay * start + first_state[...]).astype(BF16)
    carried = jnp.dot(bc[:, state_rows:], start, preferred_element_type=F32)
    scale = jnp.dot(jnp.exp(lc[0]), one_hot, precision=HIGH, preferred_element_type=F32)
    gate = jnp.where(b == side, own[...].astype(F32), got[...].astype(F32))
    gated = (mixed[...] + carried * scale) * silu(gate)
    inv = lax.rsqrt(jnp.mean(gated * gated, axis=1, keepdims=True) + 1e-5)
    result = (gated * inv * gain[...]).astype(BF16)
    out[...] = result.reshape(out.shape)


def finish(side, carry, first_state, bc, lc, mixed, gate, got, gain):
    total, wide = mixed.shape
    narrow = bc.shape[1]

    def whole(shape):
        return pl.BlockSpec(shape, lambda b, s: (0,) * len(shape))

    return pl.pallas_call(
        finish_kernel,
        out_shape=jax.ShapeDtypeStruct((8, total // 8, wide), BF16),
        grid_spec=pltpu.PrefetchScalarGridSpec(
            num_scalar_prefetch=1,
            grid=(total // BLOCK,),
            in_specs=[
                whole(carry.shape),
                whole(first_state.shape),
                pl.BlockSpec((BLOCK, narrow), lambda b, s: (b, 0)),
                pl.BlockSpec((1, BLOCK, LANES), lambda b, s: (b, 0, 0)),
                pl.BlockSpec((1, BLOCK, LANES), lambda b, s: (0, 0, 0)),
                pl.BlockSpec((BLOCK, wide), lambda b, s: (b, 0)),
                pl.BlockSpec((BLOCK, wide), lambda b, s: (0, s[0])),
                whole(got.shape),
                pl.BlockSpec((1, wide), lambda b, s: (0, s[0])),
            ],
            out_specs=pl.BlockSpec((4, total // 8, wide), lambda b, s: (b, 0, 0)),
        ),
        compiler_params=PARAMS,
        cost_estimate=cost(2 * total * wide * 200, 10 * total * wide, total * wide),
        name="finish",
    )(side, carry, first_state, bc, lc, lc, mixed, gate, got, gain)


def on_device(
    inner_raw,
    pairs_raw,
    gate_raw,
    step_raw,
    step_bias,
    rate_log,
    skip_gain,
    conv_inner,
    conv_pairs,
    norm_gain,
):
    places = lax.axis_size("context")
    shards = lax.axis_size("head")
    chunks = places // 2
    side = lax.axis_index("context") % 2
    group = (2 * lax.axis_index("head") + side).astype(jnp.int32).reshape(1)
    side = side.astype(jnp.int32)
    side_arr = side.reshape(1)
    rows = inner_raw.shape[0]
    partner = [(c, c ^ 1) for c in range(places)]
    after = [(c, c + 2) for c in range(places - 2)]
    teams = [list(range(8 * k, 8 * k + 8)) for k in range(places * shards // 8)]
    lines = [[2 * k + s for k in range(chunks)] for s in range(2)]

    packed = pack(inner_raw, pairs_raw.reshape(rows, -1))
    step_got = lax.ppermute(step_raw, "context", partner)
    recv = lax.all_to_all(
        packed, ("context", "head"), split_axis=0, concat_axis=0, axis_index_groups=teams
    )
    halo = lax.ppermute(recv[7, rows - 16 :], "context", after)
    half = gate_raw.shape[1] // 2
    gate_out = lax.dynamic_slice_in_dim(gate_raw, (1 - side) * half, half, 1)
    gate_out, recv = lax.optimization_barrier((gate_out, recv))
    gate_got = lax.ppermute(gate_out, "context", partner)

    lc, dt, lc_t, dt_t = prep(
        side_arr, step_raw, step_got, step_bias.reshape(1, -1), rate_log.reshape(1, -1)
    )
    pair_taps = conv_pairs.reshape(conv_pairs.shape[0], -1)
    xc0, bc0 = conv(group, recv, conv_inner, pair_taps)
    xc, bc, first_state, payload = state(
        group, recv[0, :16], halo, conv_inner, pair_taps, xc0, bc0, lc, dt, chunks
    )
    states = lax.all_to_all(
        payload, "context", split_axis=0, concat_axis=0, axis_index_groups=lines
    )
    mixed = intra(side_arr, xc, bc, lc, lc_t, dt_t, skip_gain.reshape(1, -1))
    carries = scan(states)
    carry = lax.all_to_all(
        carries, "context", split_axis=0, concat_axis=0, axis_index_groups=lines
    )
    slabs = finish(
        side_arr, carry, first_state, bc, lc, mixed, gate_raw, gate_got, norm_gain.reshape(1, -1)
    )
    slabs = lax.all_to_all(
        slabs, ("context", "head"), split_axis=0, concat_axis=0, axis_index_groups=teams
    )
    return unpack(slabs)


def solution(mesh):
    placed = (
        P(("rollout", "context", "head"), None),
        P(("rollout", "context", "head"), None, None, None),
        P(("rollout", "context"), "head"),
        P(("rollout", "context"), "head"),
        P("head"),
        P("head"),
        P("head"),
        P(),
        P(),
        P("head"),
    )
    return jax.shard_map(
        on_device,
        mesh=mesh,
        in_specs=placed,
        out_specs=P(("rollout", "context", "head"), None),
        check_vma=False,
    )
```

```python
import functools

import jax
import jax.numpy as jnp
from jax import lax
from jax.experimental import pallas as pl
from jax.experimental.pallas import tpu as pltpu
from jax.sharding import PartitionSpec as P

BLOCK = 256
HIGH = lax.Precision.HIGHEST
F32 = jnp.float32
BF16 = jnp.bfloat16
LANES = 128
ANY = pl.BlockSpec(memory_space=pl.ANY)
VMEM = pl.BlockSpec(memory_space=pltpu.VMEM)
SMEM = pl.BlockSpec(memory_space=pltpu.SMEM)
PARAMS = pltpu.CompilerParams(vmem_limit_bytes=24 * 1024 * 1024)


def cost(flops, bytes_accessed, transcendentals=0):
    return pl.CostEstimate(
        flops=flops, bytes_accessed=bytes_accessed, transcendentals=transcendentals
    )


def group_of(member):
    return 2 * (member % 4) + member // 4


def iota(shape, dim):
    return lax.broadcasted_iota(jnp.int32, shape, dim)


def spread(rows, channels, head_width):
    return (iota((rows, channels), 1) // head_width == iota((rows, channels), 0)).astype(F32)


def silu(v):
    return v / (1.0 + jnp.exp(-v))


def taps(ext, rows, cols, weight):
    window = ext[0 : rows + 8, cols]
    total = weight[4:5] + weight[0:1] * window[4 : 4 + rows]
    for k in range(1, 4):
        total = total + weight[k : k + 1] * window[4 + k : 4 + k + rows]
    return silu(total).astype(BF16)


def conv_kernel(inner, pairs, w_inner, w_pairs, out, ext):
    rows, wide = inner.shape
    width = out.shape[2]
    ext[0:8] = jnp.zeros((8, width), F32)
    ext[8:, 0:wide] = inner[...].astype(F32)
    ext[8:, wide:width] = pairs[...].astype(F32)
    for start in range(0, width, LANES):
        cols = slice(start, start + LANES)
        weight = w_inner[:, cols] if start < wide else w_pairs[:, start - wide : start - wide + LANES]
        out[0, :, cols] = taps(ext, rows, cols, weight)


def conv(inner, pairs, w_inner, w_pairs):
    rows = inner.shape[0]
    wide, narrow = inner.shape[1] // 8, pairs.shape[1] // 8
    width = wide + narrow

    def column(member):
        return (0, 2 * lax.rem(member, 4) + lax.div(member, 4))

    return pl.pallas_call(
        conv_kernel,
        out_shape=jax.ShapeDtypeStruct((8, rows, width), BF16),
        grid=(8,),
        in_specs=[
            pl.BlockSpec((rows, wide), column),
            pl.BlockSpec((rows, narrow), column),
            pl.BlockSpec((5, wide), column),
            pl.BlockSpec((5, narrow), column),
        ],
        out_specs=pl.BlockSpec((1, rows, width), lambda m: (m, 0, 0)),
        scratch_shapes=[pltpu.VMEM((8 + rows, width), F32)],
        compiler_params=PARAMS,
        cost_estimate=cost(160 * rows * width, 32 * rows * width, 16 * rows * width),
        name="conv",
    )(inner, pairs, w_inner, w_pairs)


FIX = 16


def fix_kernel(inner, pairs, halo_inner, halo_pairs, w_inner, w_pairs, _, out, ext):
    full = inner.shape[1]
    wide, narrow = full // 8, pairs.shape[1] // 8
    ext[0:8, 0:full] = halo_inner[...].astype(F32)
    ext[8:, 0:full] = inner[...].astype(F32)
    ext[0:8, full:] = halo_pairs[...].astype(F32)
    ext[8:, full:] = pairs[...].astype(F32)
    for member in range(8):
        group = group_of(member)
        for start in range(0, wide, LANES):
            at = group * wide + start
            cols = slice(at, at + LANES)
            out[member, :, start : start + LANES] = taps(ext, FIX, cols, w_inner[:, cols])
        for start in range(0, narrow, LANES):
            at = group * narrow + start
            out[member, :, wide + start : wide + start + LANES] = taps(
                ext, FIX, slice(full + at, full + at + LANES), w_pairs[:, at : at + LANES]
            )


def fix(inner, pairs, halo_inner, halo_pairs, w_inner, w_pairs, packed):
    full, pairs_full = inner.shape[1], pairs.shape[1]

    def whole(shape):
        return pl.BlockSpec(shape, lambda i: (0,) * len(shape))

    return pl.pallas_call(
        fix_kernel,
        out_shape=jax.ShapeDtypeStruct(packed.shape, BF16),
        grid=(1,),
        in_specs=[
            whole((FIX, full)),
            whole((FIX, pairs_full)),
            whole(halo_inner.shape),
            whole(halo_pairs.shape),
            whole(w_inner.shape),
            whole(w_pairs.shape),
            ANY,
        ],
        out_specs=whole((8, FIX, packed.shape[2])),
        scratch_shapes=[pltpu.VMEM((8 + FIX, full + pairs_full), F32)],
        input_output_aliases={6: 0},
        compiler_params=PARAMS,
        cost_estimate=cost(20 * FIX * (full + pairs_full), 8 * FIX * (full + pairs_full)),
        name="fix",
    )(inner, pairs, halo_inner, halo_pairs, w_inner, w_pairs, packed)


def unpack_kernel(slabs, out, sem):
    wide = slabs.shape[2]
    copies = [
        pltpu.make_async_copy(
            slabs.at[member], out.at[:, pl.ds(group_of(member) * wide, wide)], sem.at[member]
        )
        for member in range(8)
    ]
    for copy in copies:
        copy.start()
    for copy in copies:
        copy.wait()


def unpack(slabs):
    _, rows, wide = slabs.shape
    return pl.pallas_call(
        unpack_kernel,
        out_shape=jax.ShapeDtypeStruct((rows, 8 * wide), BF16),
        in_specs=[ANY],
        out_specs=ANY,
        scratch_shapes=[pltpu.SemaphoreType.DMA((8,))],
        compiler_params=PARAMS,
        cost_estimate=cost(0, 4 * 8 * rows * wide),
        name="unpack",
    )(slabs)


def widen(value, one_hot):
    return jnp.dot(value, one_hot, precision=HIGH, preferred_element_type=F32)


def prep_kernel(side_ref, own, got, bias, rate, lc, lc_t, dt_t, tail, scale, last):
    side = side_ref[0]
    own_heads = own.shape[1]
    heads = own_heads // 2
    wide = tail.shape[2]
    mine = own[...].astype(F32)
    theirs = got[...].astype(F32)
    low = jnp.where(side == 0, mine, theirs)
    high = jnp.where(side == 0, theirs, mine)
    column = iota((own_heads, LANES), 1)
    pick = ((iota((own_heads, LANES), 0) == column + heads * side) & (column < heads)).astype(F32)
    tri = (iota((BLOCK, BLOCK), 0) >= iota((BLOCK, BLOCK), 1)).astype(F32)
    one_hot = spread(LANES, wide, wide // heads)
    neg_rate = -jnp.exp(rate[...])
    for b, raw in enumerate((low, high)):
        v = raw + bias[...]
        step = jnp.maximum(v, 0.0) + jnp.log1p(jnp.exp(-jnp.abs(v)))
        picked = widen(step, pick)
        cum = widen(tri, widen(step * neg_rate, pick))
        end = cum[BLOCK - 1 : BLOCK]
        lc[b] = cum
        lc_t[b] = cum.T[:heads]
        dt_t[b] = picked.T[:heads]
        tail[b] = widen(jnp.exp(end - cum) * picked, one_hot)
        scale[b] = widen(jnp.exp(cum), one_hot)
        last[b] = jnp.broadcast_to(end, (8, LANES))


def prep(side, own, got, bias, rate, wide):
    heads = own.shape[1] // 2
    tall = jax.ShapeDtypeStruct((2, BLOCK, LANES), F32)
    flat = jax.ShapeDtypeStruct((2, heads, BLOCK), F32)
    full = jax.ShapeDtypeStruct((2, BLOCK, wide), F32)
    last = jax.ShapeDtypeStruct((2, 8, LANES), F32)
    return pl.pallas_call(
        prep_kernel,
        out_shape=(tall, flat, flat, full, full, last),
        in_specs=[SMEM, VMEM, VMEM, VMEM, VMEM],
        out_specs=(VMEM,) * 6,
        compiler_params=PARAMS,
        cost_estimate=cost(2 * 10**9, 6 * 10**6, 10**5),
        name="prep",
    )(side, own, got, bias, rate)


def state_kernel(recv, tail, last, first_state, payload):
    members, rows, width = recv.shape
    wide = tail.shape[2]
    half = members // 2
    heads = wide // 64
    states = []
    for b in range(2):
        block = recv[b * half : (b + 1) * half].reshape(half * rows, width)
        weighted = (block[:, 0:wide].astype(F32) * tail[b]).astype(BF16)
        states.append(
            lax.dot_general(
                block[:, wide : wide + LANES],
                weighted,
                (((0,), (0,)), ((), ())),
                preferred_element_type=F32,
            )
        )
    decay = widen(jnp.exp(last[1]), spread(LANES, wide, wide // heads))
    first_state[...] = states[0]
    total = decay[0:1] * states[0] + states[1]
    parts, depth, _ = payload.shape
    payload[:, :, 0:wide] = total.reshape(parts, depth, wide)
    log_decay = jnp.broadcast_to(last[0, 0:1] + last[1, 0:1], (depth, LANES))
    for part in range(parts):
        payload[part, :, wide : wide + LANES] = log_decay


def state(recv, tail, last, parts):
    members, rows, width = recv.shape
    wide = tail.shape[2]
    state_rows = (width - wide) // 2
    return pl.pallas_call(
        state_kernel,
        out_shape=(
            jax.ShapeDtypeStruct((state_rows, wide), F32),
            jax.ShapeDtypeStruct((parts, state_rows // parts, wide + LANES), F32),
        ),
        in_specs=[VMEM, VMEM, VMEM],
        out_specs=(VMEM, VMEM),
        compiler_params=PARAMS,
        cost_estimate=cost(2 * members * rows * wide * 128, 8 * members * rows * wide),
        name="state",
    )(recv, tail, last)


def intra_kernel(side_ref, recv, lc, lc_t, dt_t, skip, scale, own, got, out, factor):
    side = side_ref[0]
    half, rows, width = recv.shape
    wide = out.shape[1]
    heads = lc_t.shape[1]
    head_width = wide // heads
    block = recv[...].reshape(half * rows, width)
    xc = block[:, 0:wide]
    scores = lax.dot_general(
        block[:, wide + LANES : wide + 2 * LANES],
        block[:, wide : wide + LANES],
        (((1,), (1,)), ((), ())),
        preferred_element_type=F32,
    )
    lower = iota((BLOCK, BLOCK), 0) >= iota((BLOCK, BLOCK), 1)
    own_heads = skip.shape[1]
    row = iota((own_heads, wide), 0)
    gain = widen(
        jnp.broadcast_to(skip[...], (8, own_heads)),
        (iota((own_heads, wide), 1) // head_width + heads * side == row).astype(F32),
    )[0:1]
    gate = jnp.where(pl.program_id(0) == side, own[...].astype(F32), got[...].astype(F32))
    gate = silu(gate)
    factor[...] = gate * scale[0]
    cum = lc[0]
    for pair in range(heads // 2):
        outs = []
        for h in (2 * pair, 2 * pair + 1):
            gap = cum[:, h : h + 1] - lc_t[0, h : h + 1]
            decay = jnp.exp(jnp.where(lower, gap, -jnp.inf))
            weights = (scores * (decay * dt_t[0, h : h + 1])).astype(BF16)
            outs.append(
                jnp.dot(
                    weights,
                    xc[:, h * head_width : (h + 1) * head_width],
                    preferred_element_type=F32,
                )
            )
        cols = slice(2 * pair * head_width, 2 * (pair + 1) * head_width)
        mixed = jnp.concatenate(outs, axis=1) + gain[:, cols] * xc[:, cols].astype(F32)
        out[:, cols] = mixed * gate[:, cols]


def intra(side, recv, lc, lc_t, dt_t, skip, scale, gate, got):
    members, rows, width = recv.shape
    wide = scale.shape[2]
    total = members * rows
    heads = lc_t.shape[1]
    half = members // 2
    return pl.pallas_call(
        intra_kernel,
        out_shape=(jax.ShapeDtypeStruct((total, wide), F32),) * 2,
        grid_spec=pltpu.PrefetchScalarGridSpec(
            num_scalar_prefetch=1,
            grid=(2,),
            in_specs=[
                pl.BlockSpec((half, rows, width), lambda b, s: (b, 0, 0)),
                pl.BlockSpec((1, BLOCK, LANES), lambda b, s: (b, 0, 0)),
                pl.BlockSpec((1, heads, BLOCK), lambda b, s: (b, 0, 0)),
                pl.BlockSpec((1, heads, BLOCK), lambda b, s: (b, 0, 0)),
                pl.BlockSpec(skip.shape, lambda b, s: (0, 0)),
                pl.BlockSpec((1, BLOCK, wide), lambda b, s: (b, 0, 0)),
                pl.BlockSpec((BLOCK, wide), lambda b, s: (0, s[0])),
                pl.BlockSpec(got.shape, lambda b, s: (0, 0)),
            ],
            out_specs=(pl.BlockSpec((BLOCK, wide), lambda b, s: (b, 0)),) * 2,
        ),
        compiler_params=PARAMS,
        cost_estimate=cost(2 * total * BLOCK * wide * 4, 12 * total * wide, heads * total * BLOCK),
        name="intra",
    )(side, recv, lc, lc_t, dt_t, skip, scale, gate, got)


def scan_kernel(recv, out):
    chunks, rows, width = recv.shape
    wide = out.shape[2]
    one_hot = spread(LANES, wide, 64)
    logs = jnp.concatenate([recv[k, 0:1, wide:width] for k in range(chunks)], axis=0)
    decay = jnp.dot(jnp.exp(logs), one_hot, precision=HIGH, preferred_element_type=F32)
    carry = jnp.zeros((rows, wide), F32)
    for k in range(chunks):
        out[k] = carry
        carry = decay[k : k + 1] * carry + recv[k, :, 0:wide]


def scan(recv):
    chunks, rows, width = recv.shape
    return pl.pallas_call(
        scan_kernel,
        out_shape=jax.ShapeDtypeStruct((chunks, rows, width - LANES), F32),
        in_specs=[VMEM],
        out_specs=VMEM,
        compiler_params=PARAMS,
        cost_estimate=cost(4 * chunks * rows * width, 4 * chunks * rows * width),
        name="scan",
    )(recv)


def finish_kernel(side_ref, carry, first_state, recv, last, mixed, factor, gain, out):
    b = pl.program_id(0)
    half, rows, width = recv.shape
    wide = mixed.shape[1]
    state_rows = first_state.shape[0]
    start = carry[...].reshape(state_rows, wide)
    decay = widen(jnp.exp(last[0]), spread(LANES, wide, 64))[0:1]
    start = jnp.where(b == 0, start, decay * start + first_state[...]).astype(BF16)
    read = recv[:, :, wide + LANES : wide + 2 * LANES].reshape(half * rows, LANES)
    carried = jnp.dot(read, start, preferred_element_type=F32)
    gated = mixed[...] + carried * factor[...]
    inv = lax.rsqrt(jnp.mean(gated * gated, axis=1, keepdims=True) + 1e-5)
    out[...] = (gated * inv * gain[...]).astype(BF16).reshape(out.shape)


def finish(side, carry, first_state, recv, last, mixed, factor, gain):
    total, wide = mixed.shape
    members, rows, width = recv.shape
    half = members // 2

    def whole(shape):
        return pl.BlockSpec(shape, lambda b, s: (0,) * len(shape))

    return pl.pallas_call(
        finish_kernel,
        out_shape=jax.ShapeDtypeStruct((members, rows, wide), BF16),
        grid_spec=pltpu.PrefetchScalarGridSpec(
            num_scalar_prefetch=1,
            grid=(2,),
            in_specs=[
                whole(carry.shape),
                whole(first_state.shape),
                pl.BlockSpec((half, rows, width), lambda b, s: (b, 0, 0)),
                whole(last.shape),
                pl.BlockSpec((BLOCK, wide), lambda b, s: (b, 0)),
                pl.BlockSpec((BLOCK, wide), lambda b, s: (b, 0)),
                pl.BlockSpec((1, wide), lambda b, s: (0, s[0])),
            ],
            out_specs=pl.BlockSpec((half, rows, wide), lambda b, s: (b, 0, 0)),
        ),
        compiler_params=PARAMS,
        cost_estimate=cost(2 * total * wide * 200, 10 * total * wide),
        name="finish",
    )(side, carry, first_state, recv, last, mixed, factor, gain)


def on_device(
    inner_raw,
    pairs_raw,
    gate_raw,
    step_raw,
    step_bias,
    rate_log,
    skip_gain,
    conv_inner,
    conv_pairs,
    norm_gain,
):
    places = lax.axis_size("context")
    shards = lax.axis_size("head")
    chunks = places // 2
    side = (lax.axis_index("context") % 2).astype(jnp.int32)
    side_arr = side.reshape(1)
    rows = inner_raw.shape[0]
    partner = [(c, c ^ 1) for c in range(places)]
    after = [(d, d + 1) for d in range(places * shards - 1)]
    teams = [list(range(8 * k, 8 * k + 8)) for k in range(places * shards // 8)]
    lines = [[2 * k + s for k in range(chunks)] for s in range(2)]

    halo_inner = lax.ppermute(inner_raw[rows - 8 :], ("context", "head"), after)
    pairs = pairs_raw.reshape(rows, -1)
    halo_pairs = lax.ppermute(pairs[rows - 8 :], ("context", "head"), after)
    step_got = lax.ppermute(step_raw, "context", partner)
    pair_taps = conv_pairs.reshape(conv_pairs.shape[0], -1)
    packed = conv(inner_raw, pairs, conv_inner, pair_taps)
    packed = fix(inner_raw, pairs, halo_inner, halo_pairs, conv_inner, pair_taps, packed)
    packed, step_got = lax.optimization_barrier((packed, step_got))
    recv = lax.all_to_all(
        packed, ("context", "head"), split_axis=0, concat_axis=0, axis_index_groups=teams
    )
    half = gate_raw.shape[1] // 2
    gate_out = lax.dynamic_slice_in_dim(gate_raw, (1 - side) * half, half, 1)
    gate_out, recv = lax.optimization_barrier((gate_out, recv))
    gate_got = lax.ppermute(gate_out, "context", partner)

    lc, lc_t, dt_t, tail, scale, last = prep(
        side_arr, step_raw, step_got, step_bias.reshape(1, -1), rate_log.reshape(1, -1), half
    )
    first_state, payload = state(recv, tail, last, chunks)
    states = lax.all_to_all(
        payload, "context", split_axis=0, concat_axis=0, axis_index_groups=lines
    )
    states, gate_got = lax.optimization_barrier((states, gate_got))
    carries = scan(states)
    carry = lax.all_to_all(
        carries, "context", split_axis=0, concat_axis=0, axis_index_groups=lines
    )
    mixed, factor = intra(
        side_arr, recv, lc, lc_t, dt_t, skip_gain.reshape(1, -1), scale, gate_raw, gate_got
    )
    slabs = finish(
        side_arr, carry, first_state, recv, last, mixed, factor, norm_gain.reshape(1, -1)
    )
    slabs = lax.all_to_all(
        slabs, ("context", "head"), split_axis=0, concat_axis=0, axis_index_groups=teams
    )
    return unpack(slabs)


def solution(mesh):
    placed = (
        P(("rollout", "context", "head"), None),
        P(("rollout", "context", "head"), None, None, None),
        P(("rollout", "context"), "head"),
        P(("rollout", "context"), "head"),
        P("head"),
        P("head"),
        P("head"),
        P(),
        P(),
        P("head"),
    )
    return jax.shard_map(
        on_device,
        mesh=mesh,
        in_specs=placed,
        out_specs=P(("rollout", "context", "head"), None),
        check_vma=False,
    )
```

```python
import functools

import jax
import jax.numpy as jnp
from jax import lax
from jax.experimental import pallas as pl
from jax.experimental.pallas import tpu as pltpu
from jax.sharding import PartitionSpec as P

BLOCK = 256
HIGH = lax.Precision.HIGHEST
F32 = jnp.float32
BF16 = jnp.bfloat16
LANES = 128
ANY = pl.BlockSpec(memory_space=pl.ANY)
VMEM = pl.BlockSpec(memory_space=pltpu.VMEM)
SMEM = pl.BlockSpec(memory_space=pltpu.SMEM)
HBM = pl.BlockSpec(memory_space=pltpu.HBM)
PARAMS = pltpu.CompilerParams(vmem_limit_bytes=24 * 1024 * 1024)
LARGE = pltpu.CompilerParams(vmem_limit_bytes=56 * 1024 * 1024)
TEAM = 16
EXTRA = 8


def cost(flops, bytes_accessed, transcendentals=0):
    return pl.CostEstimate(
        flops=flops, bytes_accessed=bytes_accessed, transcendentals=transcendentals
    )


def iota(shape, dim):
    return lax.broadcasted_iota(jnp.int32, shape, dim)


def spread(rows, channels):
    return (iota((rows, channels), 1) // 64 == iota((rows, channels), 0)).astype(F32)


def widen(value, one_hot):
    return jnp.dot(value, one_hot, precision=HIGH, preferred_element_type=F32)


def columns(value):
    padding = jnp.zeros((LANES - value.shape[0], value.shape[1]), F32)
    return jnp.concatenate([value, padding], axis=0).T


def silu(v):
    return v / (1.0 + jnp.exp(-v))


def pack_kernel(place, inner, pairs, steps, gain, out, extra, sem, pairs_sem, extra_sem):
    x = place[0]
    rows, full = inner.shape
    wide, narrow = full // TEAM, pairs.shape[1] // 8
    copies = []
    for member in range(TEAM):
        px, py = member // 4, member % 4
        copies.append(
            pltpu.make_async_copy(
                inner.at[:, pl.ds((4 * py + px) * wide, wide)],
                out.at[member, pl.ds(0, rows), pl.ds(0, wide)],
                sem.at[member],
            )
        )
        copies.append(
            pltpu.make_async_copy(
                pairs.at[:, pl.ds((2 * py + px // 2) * narrow, narrow)],
                out.at[member, pl.ds(0, rows), pl.ds(wide, narrow)],
                pairs_sem.at[member],
            )
        )
    for copy in copies:
        copy.start()
    mine = jnp.zeros((1, wide), F32)
    for px in range(4):
        mine = jnp.where(x == px, gain[:, px * wide : (px + 1) * wide], mine)
    top = mine.astype(BF16).astype(F32)
    mid = (mine - top).astype(BF16).astype(F32)
    low = (mine - top - mid).astype(BF16).astype(F32)
    row = iota((EXTRA, wide), 0)
    pieces = jnp.where(row == 0, top, jnp.where(row == 1, mid, jnp.where(row == 2, low, 0.0)))
    pieces = pieces.astype(BF16)
    span = steps.shape[1]
    for member in range(TEAM):
        px = member // 4
        extra[member, :, 0:span] = steps[8 * px : 8 * px + 8]
        extra[member, :, span:] = pieces
    last = pltpu.make_async_copy(extra, out.at[:, pl.ds(rows, EXTRA)], extra_sem)
    last.start()
    for copy in copies:
        copy.wait()
    last.wait()


def pack(place, inner, pairs, steps, gain):
    rows = inner.shape[0]
    width = inner.shape[1] // TEAM + pairs.shape[1] // 8
    return pl.pallas_call(
        pack_kernel,
        out_shape=jax.ShapeDtypeStruct((TEAM, rows + EXTRA, width), BF16),
        in_specs=[SMEM, HBM, ANY, VMEM, VMEM],
        out_specs=ANY,
        scratch_shapes=[
            pltpu.VMEM((TEAM, EXTRA, width), BF16),
            pltpu.SemaphoreType.DMA((TEAM,)),
            pltpu.SemaphoreType.DMA((TEAM,)),
            pltpu.SemaphoreType.DMA,
        ],
        compiler_params=PARAMS,
        cost_estimate=cost(0, 4 * TEAM * rows * width),
        name="pack",
    )(place, inner, pairs, steps, gain)


def taps(ext, row, rows, cols, weight):
    window = ext[pl.ds(row, rows + 8), cols]
    total = weight[4:5] + weight[0:1] * window[4 : 4 + rows]
    for k in range(1, 4):
        total = total + weight[k : k + 1] * window[4 + k : 4 + k + rows]
    return silu(total).astype(BF16)


def conv_kernel(
    place, recv, w_inner, w_pairs, bias, rate, xc, bc, lc_t, dt_t, tail, decay, logs, gains, ext
):
    x, y = place[0], place[1]
    members, tall, width = recv.shape
    rows = tall - EXTRA
    wide = xc.shape[1]
    ext[0:8] = jnp.zeros((8, width), F32)
    for m in range(members):
        ext[8 + m * rows : 8 + (m + 1) * rows] = recv[m, 0:rows].astype(F32)

    def chunk(m, _):
        row = pl.multiple_of(m * rows, rows)
        for start in range(0, wide, LANES):
            cols = slice(start, start + LANES)
            xc[pl.ds(row, rows), cols] = taps(ext, row, rows, cols, w_inner[:, cols])
        for start in range(0, width - wide, LANES):
            bc[pl.ds(row, rows), start : start + LANES] = taps(
                ext,
                row,
                rows,
                slice(wide + start, wide + start + LANES),
                w_pairs[:, start : start + LANES],
            )
        return 0

    lax.fori_loop(0, members, chunk, 0)

    own = bias.shape[1]
    mine = iota((8, own), 1) == 8 * x + iota((8, own), 0)
    shift = jnp.sum(jnp.where(mine, bias[...], 0.0), axis=1, keepdims=True)
    speed = jnp.sum(jnp.where(mine, -jnp.exp(rate[...]), 0.0), axis=1, keepdims=True)
    upper = (iota((BLOCK, BLOCK), 0) <= iota((BLOCK, BLOCK), 1)).astype(F32)
    one_hot = spread(LANES, wide)
    total = jnp.zeros((8, 1), F32)
    for b in range(4):
        v = recv[4 * b + y, rows:tall, 0:BLOCK].astype(F32) + shift
        step = jnp.maximum(v, 0.0) + jnp.log1p(jnp.exp(-jnp.abs(v)))
        cum = widen(step * speed, upper)
        end = cum[:, BLOCK - 1 : BLOCK]
        total = total + end
        lc_t[b] = cum
        dt_t[b] = step
        tail[b] = widen(columns(jnp.exp(end - cum) * step), one_hot)
        ends = columns(jnp.broadcast_to(end, (8, LANES)))
        decay[b] = widen(jnp.exp(ends[0:8]), one_hot)
    logs[...] = columns(jnp.broadcast_to(total, (8, LANES)))[0:8]
    for m in range(members):
        pieces = recv[m, rows:tall, BLOCK:].astype(F32)
        gains[m : m + 1] = pieces[0:1] + pieces[1:2] + pieces[2:3]


def whole(shape):
    return pl.BlockSpec(shape, lambda i, p: (0,) * len(shape))


def weight_specs(wide, narrow):
    return [
        pl.BlockSpec((5, wide), lambda i, p: (0, 4 * p[1] + p[0])),
        pl.BlockSpec((5, narrow), lambda i, p: (0, 2 * p[1] + lax.div(p[0], 2))),
    ]


def conv(place, recv, w_inner, w_pairs, bias, rate):
    members, tall, width = recv.shape
    wide = w_inner.shape[1] // TEAM
    narrow = width - wide
    total = members * (tall - EXTRA)
    shapes = (
        ((total, wide), BF16),
        ((total, narrow), BF16),
        ((4, 8, BLOCK), F32),
        ((4, 8, BLOCK), F32),
        ((4, BLOCK, wide), F32),
        ((4, 8, wide), F32),
        ((8, LANES), F32),
        ((members, wide), F32),
    )
    return pl.pallas_call(
        conv_kernel,
        out_shape=tuple(jax.ShapeDtypeStruct(*s) for s in shapes),
        grid_spec=pltpu.PrefetchScalarGridSpec(
            num_scalar_prefetch=1,
            grid=(1,),
            in_specs=[whole(recv.shape)]
            + weight_specs(wide, narrow)
            + [whole(bias.shape), whole(rate.shape)],
            out_specs=tuple(whole(s[0]) for s in shapes),
            scratch_shapes=[pltpu.VMEM((8 + total, width), F32)],
        ),
        compiler_params=PARAMS,
        cost_estimate=cost(20 * total * width, 4 * total * width, 2 * total * width),
        name="conv",
    )(place, recv, w_inner, w_pairs, bias, rate)


def state_kernel(
    place, first, halo, w_inner, w_pairs, xc0, bc0, tail, decay, logs, xc, bc, states, payload, ext
):
    count = first.shape[0]
    wide = xc.shape[1]
    narrow = bc.shape[1]
    ext[0:8] = halo[count - 8 : count].astype(F32)
    ext[8 : 8 + count] = first[...].astype(F32)
    xc[...] = xc0[...]
    bc[...] = bc0[...]
    for start in range(0, wide, LANES):
        cols = slice(start, start + LANES)
        xc[0:count, cols] = taps(ext, 0, count, cols, w_inner[:, cols])
    for start in range(0, narrow, LANES):
        bc[0:count, start : start + LANES] = taps(
            ext,
            0,
            count,
            slice(wide + start, wide + start + LANES),
            w_pairs[:, start : start + LANES],
        )
    total = jnp.zeros((LANES, wide), F32)
    for b in range(4):
        rows = slice(b * BLOCK, (b + 1) * BLOCK)
        weighted = (xc[rows].astype(F32) * tail[b]).astype(BF16)
        local = lax.dot_general(
            bc[rows, 0:LANES],
            weighted,
            (((0,), (0,)), ((), ())),
            preferred_element_type=F32,
        )
        states[b] = local
        total = decay[b, 0:1] * total + local
    parts, depth, _ = payload.shape
    payload[:, :, 0:wide] = total.reshape(parts, depth, wide)
    for part in range(parts):
        for row in range(0, depth, 8):
            payload[part, row : row + 8, wide : wide + LANES] = logs[...]


def state(place, first, halo, w_inner, w_pairs, xc0, bc0, tail, decay, logs, parts):
    count, width = first.shape
    total, wide = xc0.shape
    narrow = width - wide
    shapes = (
        ((total, wide), BF16),
        ((total, narrow), BF16),
        ((4, LANES, wide), F32),
        ((parts, LANES // parts, wide + LANES), F32),
    )
    return pl.pallas_call(
        state_kernel,
        out_shape=tuple(jax.ShapeDtypeStruct(*s) for s in shapes),
        grid_spec=pltpu.PrefetchScalarGridSpec(
            num_scalar_prefetch=1,
            grid=(1,),
            in_specs=[whole(first.shape), whole(halo.shape)]
            + weight_specs(wide, narrow)
            + [whole(a.shape) for a in (xc0, bc0, tail, decay, logs)],
            out_specs=tuple(whole(s[0]) for s in shapes),
            scratch_shapes=[pltpu.VMEM((8 + count, width), F32)],
        ),
        compiler_params=PARAMS,
        cost_estimate=cost(2 * total * wide * LANES, 8 * total * wide),
        name="state",
    )(place, first, halo, w_inner, w_pairs, xc0, bc0, tail, decay, logs)


def intra_kernel(place, xc, bc, lc_t, dt_t, skip, gate_rows, out, factor):
    wide = out.shape[1]
    heads = lc_t.shape[1]
    scores = lax.dot_general(
        bc[:, LANES:], bc[:, 0:LANES], (((1,), (1,)), ((), ())), preferred_element_type=F32
    )
    lower = iota((BLOCK, BLOCK), 0) >= iota((BLOCK, BLOCK), 1)
    own = skip.shape[1]
    gain = widen(
        jnp.broadcast_to(skip[...], (8, own)),
        (iota((own, wide), 1) // 64 + heads * place[0] == iota((own, wide), 0)).astype(F32),
    )[0:1]
    gate = silu(gate_rows[0].astype(F32))
    cum = columns(lc_t[0])
    factor[...] = gate * widen(jnp.exp(cum), spread(LANES, wide))
    for pair in range(heads // 2):
        outs = []
        for h in (2 * pair, 2 * pair + 1):
            gap = cum[:, h : h + 1] - lc_t[0, h : h + 1]
            decay = jnp.exp(jnp.where(lower, gap, -jnp.inf))
            weights = (scores * (decay * dt_t[0, h : h + 1])).astype(BF16)
            outs.append(
                jnp.dot(weights, xc[:, h * 64 : (h + 1) * 64], preferred_element_type=F32)
            )
        cols = slice(2 * pair * 64, 2 * (pair + 1) * 64)
        mixed = jnp.concatenate(outs, axis=1) + gain[:, cols] * xc[:, cols].astype(F32)
        out[:, cols] = mixed * gate[:, cols]


def intra(place, xc, bc, lc_t, dt_t, skip, gate_rows):
    total, wide = xc.shape
    narrow = bc.shape[1]
    heads = lc_t.shape[1]
    return pl.pallas_call(
        intra_kernel,
        out_shape=(jax.ShapeDtypeStruct((total, wide), F32),) * 2,
        grid_spec=pltpu.PrefetchScalarGridSpec(
            num_scalar_prefetch=1,
            grid=(4,),
            in_specs=[
                pl.BlockSpec((BLOCK, wide), lambda b, p: (b, 0)),
                pl.BlockSpec((BLOCK, narrow), lambda b, p: (b, 0)),
                pl.BlockSpec((1, heads, BLOCK), lambda b, p: (b, 0, 0)),
                pl.BlockSpec((1, heads, BLOCK), lambda b, p: (b, 0, 0)),
                whole(skip.shape),
                pl.BlockSpec((1, BLOCK, wide), lambda b, p: (b, 0, 0)),
            ],
            out_specs=(pl.BlockSpec((BLOCK, wide), lambda b, p: (b, 0)),) * 2,
        ),
        compiler_params=LARGE,
        cost_estimate=cost(2 * total * BLOCK * wide * 4, 12 * total * wide, heads * total * BLOCK),
        name="intra",
    )(place, xc, bc, lc_t, dt_t, skip, gate_rows)


def scan_kernel(recv, out):
    chunks, rows, width = recv.shape
    wide = out.shape[2]
    logs = jnp.concatenate([recv[k, 0:1, wide:width] for k in range(chunks)], axis=0)
    logs = jnp.where(iota(logs.shape, 1) < wide // 64, logs, 0.0)
    decay = widen(jnp.exp(logs), spread(LANES, wide))
    carry = jnp.zeros((rows, wide), F32)
    for k in range(chunks):
        out[k] = carry
        carry = decay[k : k + 1] * carry + recv[k, :, 0:wide]


def scan(recv):
    chunks, rows, width = recv.shape
    return pl.pallas_call(
        scan_kernel,
        out_shape=jax.ShapeDtypeStruct((chunks, rows, width - LANES), F32),
        in_specs=[VMEM],
        out_specs=VMEM,
        compiler_params=PARAMS,
        cost_estimate=cost(4 * chunks * rows * width, 8 * chunks * rows * width),
        name="scan",
    )(recv)


def finish_kernel(carry, states, decay, bc, mixed, factor, out, held):
    b = pl.program_id(0)

    @pl.when(b == 0)
    def _():
        held[...] = carry[...].reshape(held.shape)

    start = held[...]
    carried = jnp.dot(bc[:, LANES:], start.astype(BF16), preferred_element_type=F32)
    out[...] = (mixed[...] + carried * factor[...]).astype(BF16).reshape(out.shape)
    held[...] = decay[0, 0:1] * start + states[0]


def finish(carry, states, decay, bc, mixed, factor, rows):
    total, wide = mixed.shape
    narrow = bc.shape[1]
    return pl.pallas_call(
        finish_kernel,
        out_shape=jax.ShapeDtypeStruct((total // rows, rows, wide), BF16),
        grid=(4,),
        in_specs=[
            pl.BlockSpec(carry.shape, lambda b: (0, 0, 0)),
            pl.BlockSpec((1, LANES, wide), lambda b: (b, 0, 0)),
            pl.BlockSpec((1, 8, wide), lambda b: (b, 0, 0)),
            pl.BlockSpec((BLOCK, narrow), lambda b: (b, 0)),
            pl.BlockSpec((BLOCK, wide), lambda b: (b, 0)),
            pl.BlockSpec((BLOCK, wide), lambda b: (b, 0)),
        ],
        out_specs=pl.BlockSpec((BLOCK // rows, rows, wide), lambda b: (b, 0, 0)),
        scratch_shapes=[pltpu.VMEM((LANES, wide), F32)],
        compiler_params=LARGE,
        cost_estimate=cost(2 * total * wide * 200, 10 * total * wide),
        name="finish",
    )(carry, states, decay, bc, mixed, factor)


def post_kernel(slabs, gains, out):
    wide = slabs.shape[2]
    for y in range(4):
        for half in range(2):
            left, right = 8 * half + y, 8 * half + 4 + y
            a, b = slabs[left].astype(F32), slabs[right].astype(F32)
            mean = (
                jnp.sum(a * a, axis=1, keepdims=True) + jnp.sum(b * b, axis=1, keepdims=True)
            ) / (2 * wide)
            inv = lax.rsqrt(mean + 1e-5)
            at = (4 * y + 2 * half) * wide
            out[:, at : at + wide] = (a * inv * gains[left : left + 1]).astype(BF16)
            out[:, at + wide : at + 2 * wide] = (b * inv * gains[right : right + 1]).astype(BF16)


def post(slabs, gains):
    members, rows, wide = slabs.shape
    return pl.pallas_call(
        post_kernel,
        out_shape=jax.ShapeDtypeStruct((rows, members * wide), BF16),
        in_specs=[VMEM, VMEM],
        out_specs=VMEM,
        compiler_params=PARAMS,
        cost_estimate=cost(6 * members * rows * wide, 4 * members * rows * wide),
        name="post",
    )(slabs, gains)


def on_device(
    inner_raw,
    pairs_raw,
    gate_raw,
    step_raw,
    step_bias,
    rate_log,
    skip_gain,
    conv_inner,
    conv_pairs,
    norm_gain,
):
    places = lax.axis_size("context")
    shards = lax.axis_size("head")
    chunks = places // 4
    x = (lax.axis_index("context") % 4).astype(jnp.int32)
    place = jnp.stack([x, lax.axis_index("head").astype(jnp.int32)])
    rows = inner_raw.shape[0]
    after = [(c, c + 4) for c in range(places - 4)]
    teams = [list(range(TEAM * k, TEAM * (k + 1))) for k in range(places * shards // TEAM)]
    lines = [[4 * k + s for k in range(chunks)] for s in range(4)]
    rings = [[4 * k + s for s in range(4)] for k in range(chunks)]

    packed = pack(
        place, inner_raw, pairs_raw.reshape(rows, -1), step_raw.T, norm_gain.reshape(1, -1)
    )
    recv = lax.all_to_all(
        packed, ("context", "head"), split_axis=0, concat_axis=0, axis_index_groups=teams
    )
    gate_rows = gate_raw.reshape(gate_raw.shape[0], 4, -1).transpose(1, 0, 2)
    gate_rows, recv = lax.optimization_barrier((gate_rows, recv))
    halo = lax.ppermute(recv[TEAM - 1, rows - 16 : rows], "context", after)

    pair_taps = conv_pairs.reshape(conv_pairs.shape[0], -1)
    xc0, bc0, lc_t, dt_t, tail, decay, logs, gains = conv(
        place, recv, conv_inner, pair_taps, step_bias.reshape(1, -1), rate_log.reshape(1, -1)
    )
    xc, bc, states, payload = state(
        place, recv[0, :16], halo, conv_inner, pair_taps, xc0, bc0, tail, decay, logs, chunks
    )
    gate_rows = lax.all_to_all(
        gate_rows, "context", split_axis=0, concat_axis=0, axis_index_groups=rings
    )
    totals = lax.all_to_all(
        payload, "context", split_axis=0, concat_axis=0, axis_index_groups=lines
    )
    carry = lax.all_to_all(
        scan(totals), "context", split_axis=0, concat_axis=0, axis_index_groups=lines
    )
    mixed, factor = intra(place, xc, bc, lc_t, dt_t, skip_gain.reshape(1, -1), gate_rows)
    slabs = finish(carry, states, decay, bc, mixed, factor, rows)
    slabs = lax.all_to_all(
        slabs, ("context", "head"), split_axis=0, concat_axis=0, axis_index_groups=teams
    )
    return post(slabs, gains)


def solution(mesh):
    placed = (
        P(("rollout", "context", "head"), None),
        P(("rollout", "context", "head"), None, None, None),
        P(("rollout", "context"), "head"),
        P(("rollout", "context"), "head"),
        P("head"),
        P("head"),
        P("head"),
        P(),
        P(),
        P("head"),
    )
    return jax.shard_map(
        on_device,
        mesh=mesh,
        in_specs=placed,
        out_specs=P(("rollout", "context", "head"), None),
        check_vma=False,
    )
```

```python
import functools

import jax
import jax.numpy as jnp
from jax import lax
from jax.experimental import pallas as pl
from jax.experimental.pallas import tpu as pltpu
from jax.sharding import PartitionSpec as P

BLOCK = 256
HIGH = lax.Precision.HIGHEST
F32 = jnp.float32
BF16 = jnp.bfloat16
LANES = 128
ANY = pl.BlockSpec(memory_space=pl.ANY)
VMEM = pl.BlockSpec(memory_space=pltpu.VMEM)
SMEM = pl.BlockSpec(memory_space=pltpu.SMEM)
HBM = pl.BlockSpec(memory_space=pltpu.HBM)
PARAMS = pltpu.CompilerParams(vmem_limit_bytes=24 * 1024 * 1024)
LARGE = pltpu.CompilerParams(vmem_limit_bytes=56 * 1024 * 1024)
TEAM = 16
EXTRA = 8


def cost(flops, bytes_accessed, transcendentals=0):
    return pl.CostEstimate(
        flops=flops, bytes_accessed=bytes_accessed, transcendentals=transcendentals
    )


def keep(array):
    return pltpu.with_memory_space_constraint(array, pltpu.HBM)


def iota(shape, dim):
    return lax.broadcasted_iota(jnp.int32, shape, dim)


def spread(rows, channels):
    return (iota((rows, channels), 1) // 64 == iota((rows, channels), 0)).astype(F32)


def widen(value, one_hot):
    return jnp.dot(value, one_hot, precision=HIGH, preferred_element_type=F32)


def columns(value):
    padding = jnp.zeros((LANES - value.shape[0], value.shape[1]), F32)
    return jnp.concatenate([value, padding], axis=0).T


def split(value):
    top = value.astype(BF16).astype(F32)
    mid = (value - top).astype(BF16).astype(F32)
    return [top, mid, value - top - mid]


def spread_columns(value, channels):
    padding = jnp.zeros((LANES - 24, value.shape[1]), F32)
    left = jnp.concatenate(split(value) + [padding], axis=0).T.astype(BF16)
    row = iota((LANES, channels), 0)
    one_hot = (row % 8 == iota((LANES, channels), 1) // 64) & (row < 24)
    return jnp.dot(left, one_hot.astype(BF16), preferred_element_type=F32)


def silu(v):
    return v / (1.0 + jnp.exp(-v))


def pack_kernel(place, inner, pairs, steps, gain, out, extra, sem, pairs_sem, extra_sem):
    x = place[0]
    rows, full = inner.shape
    wide, narrow = full // TEAM, pairs.shape[1] // 8
    copies = []
    for member in range(TEAM):
        px, py = member // 4, member % 4
        copies.append(
            pltpu.make_async_copy(
                inner.at[:, pl.ds((4 * py + px) * wide, wide)],
                out.at[member, pl.ds(0, rows), pl.ds(0, wide)],
                sem.at[member],
            )
        )
        copies.append(
            pltpu.make_async_copy(
                pairs.at[:, pl.ds((2 * py + px // 2) * narrow, narrow)],
                out.at[member, pl.ds(0, rows), pl.ds(wide, narrow)],
                pairs_sem.at[member],
            )
        )
    for copy in copies:
        copy.start()
    mine = jnp.zeros((1, wide), F32)
    for px in range(4):
        mine = jnp.where(x == px, gain[:, px * wide : (px + 1) * wide], mine)
    top = mine.astype(BF16).astype(F32)
    mid = (mine - top).astype(BF16).astype(F32)
    low = (mine - top - mid).astype(BF16).astype(F32)
    row = iota((EXTRA, wide), 0)
    pieces = jnp.where(row == 0, top, jnp.where(row == 1, mid, jnp.where(row == 2, low, 0.0)))
    pieces = pieces.astype(BF16)
    span = steps.shape[1]
    for member in range(TEAM):
        px = member // 4
        extra[member, :, 0:span] = steps[8 * px : 8 * px + 8]
        extra[member, :, span:] = pieces
    last = pltpu.make_async_copy(extra, out.at[:, pl.ds(rows, EXTRA)], extra_sem)
    last.start()
    for copy in copies:
        copy.wait()
    last.wait()


def pack(place, inner, pairs, steps, gain):
    rows = inner.shape[0]
    width = inner.shape[1] // TEAM + pairs.shape[1] // 8
    return pl.pallas_call(
        pack_kernel,
        out_shape=jax.ShapeDtypeStruct((TEAM, rows + EXTRA, width), BF16),
        in_specs=[SMEM, HBM, ANY, VMEM, VMEM],
        out_specs=ANY,
        scratch_shapes=[
            pltpu.VMEM((TEAM, EXTRA, width), BF16),
            pltpu.SemaphoreType.DMA((TEAM,)),
            pltpu.SemaphoreType.DMA((TEAM,)),
            pltpu.SemaphoreType.DMA,
        ],
        compiler_params=PARAMS,
        cost_estimate=cost(0, 4 * TEAM * rows * width),
        name="pack",
    )(place, keep(inner), pairs, keep(steps), keep(gain))


def taps(ext, row, rows, cols, weight):
    window = ext[pl.ds(row, rows + 8), cols]
    total = weight[4:5] + weight[0:1] * window[4 : 4 + rows]
    for k in range(1, 4):
        total = total + weight[k : k + 1] * window[4 + k : 4 + k + rows]
    return silu(total).astype(BF16)


def conv_kernel(
    place, recv, w_inner, w_pairs, bias, rate, xc, bc, lc_t, dt_t, tail, decay, logs, gains, ext
):
    x, y = place[0], place[1]
    members, tall, width = recv.shape
    rows = tall - EXTRA
    wide = xc.shape[1]
    ext[0:8] = jnp.zeros((8, width), F32)
    for m in range(members):
        ext[8 + m * rows : 8 + (m + 1) * rows] = recv[m, 0:rows].astype(F32)

    def chunk(m, _):
        row = pl.multiple_of(m * rows, rows)
        for start in range(0, wide, LANES):
            cols = slice(start, start + LANES)
            xc[pl.ds(row, rows), cols] = taps(ext, row, rows, cols, w_inner[:, cols])
        for start in range(0, width - wide, LANES):
            bc[pl.ds(row, rows), start : start + LANES] = taps(
                ext,
                row,
                rows,
                slice(wide + start, wide + start + LANES),
                w_pairs[:, start : start + LANES],
            )
        return 0

    lax.fori_loop(0, members, chunk, 0)

    own = bias.shape[1]
    mine = iota((8, own), 1) == 8 * x + iota((8, own), 0)
    shift = jnp.sum(jnp.where(mine, bias[...], 0.0), axis=1, keepdims=True)
    speed = jnp.sum(jnp.where(mine, -jnp.exp(rate[...]), 0.0), axis=1, keepdims=True)
    upper = (iota((BLOCK, BLOCK), 0) <= iota((BLOCK, BLOCK), 1)).astype(BF16)
    steps = []
    for b in range(4):
        v = recv[4 * b + y, rows:tall, 0:BLOCK].astype(F32) + shift
        steps.append(jnp.maximum(v, 0.0) + jnp.log1p(jnp.exp(-jnp.abs(v))))
    parts = split(jnp.concatenate([step * speed for step in steps], axis=0))
    parts = jnp.concatenate(parts, axis=0).astype(BF16)
    sums = jnp.dot(parts, upper, preferred_element_type=F32)
    ends = jnp.zeros((8, LANES), F32)
    for b in range(4):
        cum = sums[8 * b : 8 * b + 8] + sums[8 * b + 32 : 8 * b + 40] + sums[8 * b + 64 : 8 * b + 72]
        end = cum[:, BLOCK - 1 : BLOCK]
        ends = jnp.where(iota((8, LANES), 1) == b, end, ends)
        lc_t[b] = cum
        dt_t[b] = steps[b]
        tail[b] = spread_columns(jnp.exp(end - cum) * steps[b], wide)
    decay[...] = spread_columns(jnp.exp(ends), wide)[0:8]
    by_block = columns(ends)
    logs[...] = jnp.broadcast_to(
        by_block[0:1] + by_block[1:2] + by_block[2:3] + by_block[3:4], (8, LANES)
    )
    for m in range(members):
        pieces = recv[m, rows:tall, BLOCK:].astype(F32)
        gains[m : m + 1] = pieces[0:1] + pieces[1:2] + pieces[2:3]


def whole(shape):
    return pl.BlockSpec(shape, lambda i, p: (0,) * len(shape))


def weight_specs(wide, narrow):
    return [
        pl.BlockSpec((5, wide), lambda i, p: (0, 4 * p[1] + p[0])),
        pl.BlockSpec((5, narrow), lambda i, p: (0, 2 * p[1] + lax.div(p[0], 2))),
    ]


def conv(place, recv, w_inner, w_pairs, bias, rate):
    members, tall, width = recv.shape
    wide = w_inner.shape[1] // TEAM
    narrow = width - wide
    total = members * (tall - EXTRA)
    shapes = (
        ((total, wide), BF16),
        ((total, narrow), BF16),
        ((4, 8, BLOCK), F32),
        ((4, 8, BLOCK), F32),
        ((4, BLOCK, wide), F32),
        ((8, wide), F32),
        ((8, LANES), F32),
        ((members, wide), F32),
    )
    return pl.pallas_call(
        conv_kernel,
        out_shape=tuple(jax.ShapeDtypeStruct(*s) for s in shapes),
        grid_spec=pltpu.PrefetchScalarGridSpec(
            num_scalar_prefetch=1,
            grid=(1,),
            in_specs=[whole(recv.shape)]
            + weight_specs(wide, narrow)
            + [whole(bias.shape), whole(rate.shape)],
            out_specs=tuple(whole(s[0]) for s in shapes),
            scratch_shapes=[pltpu.VMEM((8 + total, width), F32)],
        ),
        compiler_params=PARAMS,
        cost_estimate=cost(20 * total * width, 4 * total * width, 2 * total * width),
        name="conv",
    )(place, recv, w_inner, w_pairs, bias, rate)


def state_kernel(
    place, first, halo, w_inner, w_pairs, xc0, bc0, tail, decay, logs, xc, bc, states, payload, ext
):
    count = first.shape[0]
    wide = xc.shape[1]
    narrow = bc.shape[1]
    ext[0:8] = halo[count - 8 : count].astype(F32)
    ext[8 : 8 + count] = first[...].astype(F32)
    xc[...] = xc0[...]
    bc[...] = bc0[...]
    for start in range(0, wide, LANES):
        cols = slice(start, start + LANES)
        xc[0:count, cols] = taps(ext, 0, count, cols, w_inner[:, cols])
    for start in range(0, narrow, LANES):
        bc[0:count, start : start + LANES] = taps(
            ext,
            0,
            count,
            slice(wide + start, wide + start + LANES),
            w_pairs[:, start : start + LANES],
        )
    total = jnp.zeros((LANES, wide), F32)
    for b in range(4):
        rows = slice(b * BLOCK, (b + 1) * BLOCK)
        weighted = (xc[rows].astype(F32) * tail[b]).astype(BF16)
        local = lax.dot_general(
            bc[rows, 0:LANES],
            weighted,
            (((0,), (0,)), ((), ())),
            preferred_element_type=F32,
        )
        states[b] = local
        total = decay[b : b + 1] * total + local
    parts, depth, _ = payload.shape
    payload[:, :, 0:wide] = total.reshape(parts, depth, wide)
    for part in range(parts):
        for row in range(0, depth, 8):
            payload[part, row : row + 8, wide : wide + LANES] = logs[...]


def state(place, first, halo, w_inner, w_pairs, xc0, bc0, tail, decay, logs, parts):
    count, width = first.shape
    total, wide = xc0.shape
    narrow = width - wide
    shapes = (
        ((total, wide), BF16),
        ((total, narrow), BF16),
        ((4, LANES, wide), F32),
        ((parts, LANES // parts, wide + LANES), F32),
    )
    return pl.pallas_call(
        state_kernel,
        out_shape=tuple(pltpu.HBM(*s) for s in shapes),
        grid_spec=pltpu.PrefetchScalarGridSpec(
            num_scalar_prefetch=1,
            grid=(1,),
            in_specs=[whole(first.shape), whole(halo.shape)]
            + weight_specs(wide, narrow)
            + [whole(a.shape) for a in (xc0, bc0, tail, decay, logs)],
            out_specs=tuple(whole(s[0]) for s in shapes),
            scratch_shapes=[pltpu.VMEM((8 + count, width), F32)],
        ),
        compiler_params=PARAMS,
        cost_estimate=cost(2 * total * wide * LANES, 8 * total * wide),
        name="state",
    )(place, first, halo, w_inner, w_pairs, xc0, bc0, tail, decay, logs)


def intra_kernel(place, xc, bc, lc_t, dt_t, skip, own_gate, got_a, got_b, got_c, out, factor):
    wide = out.shape[1]
    heads = lc_t.shape[1]
    scores = lax.dot_general(
        bc[:, LANES:], bc[:, 0:LANES], (((1,), (1,)), ((), ())), preferred_element_type=F32
    )
    lower = iota((BLOCK, BLOCK), 0) >= iota((BLOCK, BLOCK), 1)
    own = skip.shape[1]
    gain = widen(
        jnp.broadcast_to(skip[...], (8, own)),
        (iota((own, wide), 1) // 64 + heads * place[0] == iota((own, wide), 0)).astype(F32),
    )[0:1]
    far = lax.rem(place[0] - pl.program_id(0) + 4, 4)
    gate = own_gate[...].astype(F32)
    for distance, got in ((1, got_a), (2, got_b), (3, got_c)):
        gate = jnp.where(far == distance, got[...].astype(F32), gate)
    gate = silu(gate)
    cum = columns(lc_t[0])
    factor[...] = (gate * spread_columns(jnp.exp(lc_t[0]), wide)).astype(BF16)
    for pair in range(heads // 2):
        outs = []
        for h in (2 * pair, 2 * pair + 1):
            gap = cum[:, h : h + 1] - lc_t[0, h : h + 1]
            decay = jnp.exp(jnp.where(lower, gap, -jnp.inf))
            weights = (scores * (decay * dt_t[0, h : h + 1])).astype(BF16)
            outs.append(
                jnp.dot(weights, xc[:, h * 64 : (h + 1) * 64], preferred_element_type=F32)
            )
        cols = slice(2 * pair * 64, 2 * (pair + 1) * 64)
        mixed = jnp.concatenate(outs, axis=1) + gain[:, cols] * xc[:, cols].astype(F32)
        out[:, cols] = (mixed * gate[:, cols]).astype(BF16)


def intra(place, xc, bc, lc_t, dt_t, skip, gate_raw, got):
    total, wide = xc.shape
    narrow = bc.shape[1]
    heads = lc_t.shape[1]
    return pl.pallas_call(
        intra_kernel,
        out_shape=(pltpu.HBM((total, wide), BF16),) * 2,
        grid_spec=pltpu.PrefetchScalarGridSpec(
            num_scalar_prefetch=1,
            grid=(4,),
            in_specs=[
                pl.BlockSpec((BLOCK, wide), lambda b, p: (b, 0)),
                pl.BlockSpec((BLOCK, narrow), lambda b, p: (b, 0)),
                pl.BlockSpec((1, heads, BLOCK), lambda b, p: (b, 0, 0)),
                pl.BlockSpec((1, heads, BLOCK), lambda b, p: (b, 0, 0)),
                whole(skip.shape),
                pl.BlockSpec((BLOCK, wide), lambda b, p: (0, p[0])),
            ]
            + [whole(a.shape) for a in got],
            out_specs=(pl.BlockSpec((BLOCK, wide), lambda b, p: (b, 0)),) * 2,
        ),
        compiler_params=PARAMS,
        cost_estimate=cost(2 * total * BLOCK * wide * 4, 12 * total * wide, heads * total * BLOCK),
        name="intra",
    )(place, xc, bc, lc_t, dt_t, skip, keep(gate_raw), *got)


def scan_kernel(recv, out):
    chunks, rows, width = recv.shape
    wide = out.shape[2]
    logs = jnp.concatenate([recv[k, 0:1, wide:width] for k in range(chunks)], axis=0)
    logs = jnp.where(iota(logs.shape, 1) < wide // 64, logs, 0.0)
    decay = widen(jnp.exp(logs), spread(LANES, wide))
    carry = jnp.zeros((rows, wide), F32)
    for k in range(chunks):
        out[k] = carry
        carry = decay[k : k + 1] * carry + recv[k, :, 0:wide]


def scan(recv):
    chunks, rows, width = recv.shape
    return pl.pallas_call(
        scan_kernel,
        out_shape=jax.ShapeDtypeStruct((chunks, rows, width - LANES), F32),
        in_specs=[VMEM],
        out_specs=VMEM,
        compiler_params=PARAMS,
        cost_estimate=cost(4 * chunks * rows * width, 8 * chunks * rows * width),
        name="scan",
    )(recv)


def finish_kernel(carry, states, decay, bc, mixed, factor, out, s_in, c_in, m_in, f_in, sem):
    wide = mixed.shape[1]
    copies = []
    for b in range(4):
        rows = pl.ds(b * BLOCK, BLOCK)
        copies.append(
            [
                pltpu.make_async_copy(bc.at[rows, pl.ds(LANES, LANES)], c_in.at[b], sem.at[b, 0]),
                pltpu.make_async_copy(mixed.at[rows], m_in.at[b], sem.at[b, 1]),
                pltpu.make_async_copy(factor.at[rows], f_in.at[b], sem.at[b, 2]),
                pltpu.make_async_copy(states.at[b], s_in.at[b], sem.at[b, 3]),
            ]
        )
    for group in copies:
        for copy in group:
            copy.start()
    start = carry[...].reshape(LANES, wide)
    for b in range(4):
        for copy in copies[b]:
            copy.wait()
        carried = jnp.dot(c_in[b], start.astype(BF16), preferred_element_type=F32)
        gated = m_in[b].astype(F32) + carried * f_in[b].astype(F32)
        count = BLOCK // out.shape[1]
        out[b * count : (b + 1) * count] = gated.astype(BF16).reshape(count, -1, wide)
        start = decay[b : b + 1] * start + s_in[b]


def finish(carry, states, decay, bc, mixed, factor, rows):
    total, wide = mixed.shape
    return pl.pallas_call(
        finish_kernel,
        out_shape=jax.ShapeDtypeStruct((total // rows, rows, wide), BF16),
        in_specs=[VMEM, ANY, VMEM, ANY, ANY, ANY],
        out_specs=VMEM,
        scratch_shapes=[
            pltpu.VMEM((4, LANES, wide), F32),
            pltpu.VMEM((4, BLOCK, LANES), BF16),
            pltpu.VMEM((4, BLOCK, wide), BF16),
            pltpu.VMEM((4, BLOCK, wide), BF16),
            pltpu.SemaphoreType.DMA((4, 4)),
        ],
        compiler_params=PARAMS,
        cost_estimate=cost(2 * total * wide * 200, 6 * total * wide),
        name="finish",
    )(carry, keep(states), decay, keep(bc), keep(mixed), keep(factor))


def post_kernel(slabs, gains, out):
    wide = slabs.shape[2]
    for y in range(4):
        for half in range(2):
            left, right = 8 * half + y, 8 * half + 4 + y
            a, b = slabs[left].astype(F32), slabs[right].astype(F32)
            mean = (
                jnp.sum(a * a, axis=1, keepdims=True) + jnp.sum(b * b, axis=1, keepdims=True)
            ) / (2 * wide)
            inv = lax.rsqrt(mean + 1e-5)
            at = (4 * y + 2 * half) * wide
            out[:, at : at + wide] = (a * inv * gains[left : left + 1]).astype(BF16)
            out[:, at + wide : at + 2 * wide] = (b * inv * gains[right : right + 1]).astype(BF16)


def post(slabs, gains):
    members, rows, wide = slabs.shape
    return pl.pallas_call(
        post_kernel,
        out_shape=jax.ShapeDtypeStruct((rows, members * wide), BF16),
        in_specs=[VMEM, VMEM],
        out_specs=VMEM,
        compiler_params=PARAMS,
        cost_estimate=cost(6 * members * rows * wide, 4 * members * rows * wide),
        name="post",
    )(slabs, gains)


def on_device(
    inner_raw,
    pairs_raw,
    gate_raw,
    step_raw,
    step_bias,
    rate_log,
    skip_gain,
    conv_inner,
    conv_pairs,
    norm_gain,
):
    places = lax.axis_size("context")
    shards = lax.axis_size("head")
    chunks = places // 4
    x = (lax.axis_index("context") % 4).astype(jnp.int32)
    place = jnp.stack([x, lax.axis_index("head").astype(jnp.int32)])
    rows = inner_raw.shape[0]
    after = [(c, c + 4) for c in range(places - 4)]
    teams = [list(range(TEAM * k, TEAM * (k + 1))) for k in range(places * shards // TEAM)]
    lines = [[4 * k + s for k in range(chunks)] for s in range(4)]
    rings = [[4 * k + s for s in range(4)] for k in range(chunks)]

    packed = pack(
        place, inner_raw, pairs_raw.reshape(rows, -1), step_raw.T, norm_gain.reshape(1, -1)
    )
    recv = lax.all_to_all(
        packed, ("context", "head"), split_axis=0, concat_axis=0, axis_index_groups=teams
    )
    width = gate_raw.shape[1] // 4
    gates = [
        lax.dynamic_slice_in_dim(gate_raw, (x + far) % 4 * width, width, 1) for far in (1, 2, 3)
    ]
    *gates, recv = lax.optimization_barrier((*gates, recv))
    halo = lax.ppermute(recv[TEAM - 1, rows - 16 : rows], "context", after)

    pair_taps = conv_pairs.reshape(conv_pairs.shape[0], -1)
    xc0, bc0, lc_t, dt_t, tail, decay, logs, gains = conv(
        place, recv, conv_inner, pair_taps, step_bias.reshape(1, -1), rate_log.reshape(1, -1)
    )
    xc, bc, states, payload = state(
        place, recv[0, :16], halo, conv_inner, pair_taps, xc0, bc0, tail, decay, logs, chunks
    )
    *gates, payload = lax.optimization_barrier((*gates, payload))
    gates = [
        lax.ppermute(gate, "context", [(c, c - c % 4 + (c + far) % 4) for c in range(places)])
        for far, gate in zip((1, 2, 3), gates)
    ]
    totals = lax.all_to_all(
        payload, "context", split_axis=0, concat_axis=0, axis_index_groups=lines
    )
    *gates, totals = lax.optimization_barrier((*gates, totals))
    carry = lax.all_to_all(
        scan(totals), "context", split_axis=0, concat_axis=0, axis_index_groups=lines
    )
    mixed, factor = intra(place, xc, bc, lc_t, dt_t, skip_gain.reshape(1, -1), gate_raw, gates)
    slabs = finish(carry, states, decay, bc, mixed, factor, rows)
    slabs = lax.all_to_all(
        slabs, ("context", "head"), split_axis=0, concat_axis=0, axis_index_groups=teams
    )
    return post(slabs, gains)


def solution(mesh):
    placed = (
        P(("rollout", "context", "head"), None),
        P(("rollout", "context", "head"), None, None, None),
        P(("rollout", "context"), "head"),
        P(("rollout", "context"), "head"),
        P("head"),
        P("head"),
        P("head"),
        P(),
        P(),
        P("head"),
    )
    return jax.shard_map(
        on_device,
        mesh=mesh,
        in_specs=placed,
        out_specs=P(("rollout", "context", "head"), None),
        check_vma=False,
    )
```

```python
import functools

import jax
import jax.numpy as jnp
from jax import lax
from jax.experimental import pallas as pl
from jax.experimental.pallas import tpu as pltpu
from jax.sharding import PartitionSpec as P

BLOCK = 256
HIGH = lax.Precision.HIGHEST
F32 = jnp.float32
BF16 = jnp.bfloat16
LANES = 128
ANY = pl.BlockSpec(memory_space=pl.ANY)
VMEM = pl.BlockSpec(memory_space=pltpu.VMEM)
SMEM = pl.BlockSpec(memory_space=pltpu.SMEM)
HBM = pl.BlockSpec(memory_space=pltpu.HBM)
PARAMS = pltpu.CompilerParams(vmem_limit_bytes=24 * 1024 * 1024)
LARGE = pltpu.CompilerParams(vmem_limit_bytes=56 * 1024 * 1024)
TEAM = 16
EXTRA = 8


def cost(flops, bytes_accessed, transcendentals=0):
    return pl.CostEstimate(
        flops=flops, bytes_accessed=bytes_accessed, transcendentals=transcendentals
    )


def keep(array):
    return pltpu.with_memory_space_constraint(array, pltpu.HBM)


def iota(shape, dim):
    return lax.broadcasted_iota(jnp.int32, shape, dim)


def spread(rows, channels):
    return (iota((rows, channels), 1) // 64 == iota((rows, channels), 0)).astype(F32)


def widen(value, one_hot):
    return jnp.dot(value, one_hot, precision=HIGH, preferred_element_type=F32)


def columns(value):
    padding = jnp.zeros((LANES - value.shape[0], value.shape[1]), F32)
    return jnp.concatenate([value, padding], axis=0).T


def split(value):
    top = value.astype(BF16).astype(F32)
    mid = (value - top).astype(BF16).astype(F32)
    return [top, mid, value - top - mid]


def spread_columns(value, channels):
    padding = jnp.zeros((LANES - 24, value.shape[1]), F32)
    left = jnp.concatenate(split(value) + [padding], axis=0).T.astype(BF16)
    row = iota((LANES, channels), 0)
    one_hot = (row % 8 == iota((LANES, channels), 1) // 64) & (row < 24)
    return jnp.dot(left, one_hot.astype(BF16), preferred_element_type=F32)


def silu(v):
    return v / (1.0 + jnp.exp(-v))


def pack_kernel(
    place, inner, pairs, steps, gain, out, staged, extra, stage_sem, sem, pairs_sem, extra_sem
):
    x = place[0]
    rows, full = inner.shape
    stages = [
        pltpu.make_async_copy(
            inner.at[pl.ds(8 * k, 8)], staged.at[pl.ds(8 * k, 8)], stage_sem.at[k]
        )
        for k in range(rows // 8)
    ]
    for copy in stages:
        copy.start()
    wide, narrow = full // TEAM, pairs.shape[1] // 8
    copies, more = [], []
    for member in range(TEAM):
        px, py = member // 4, member % 4
        copies.append(
            pltpu.make_async_copy(
                staged.at[:, pl.ds((4 * py + px) * wide, wide)],
                out.at[member, pl.ds(0, rows), pl.ds(0, wide)],
                sem.at[member],
            )
        )
        more.append(
            pltpu.make_async_copy(
                pairs.at[:, pl.ds((2 * py + px // 2) * narrow, narrow)],
                out.at[member, pl.ds(0, rows), pl.ds(wide, narrow)],
                pairs_sem.at[member],
            )
        )
    for copy in more:
        copy.start()
    mine = jnp.zeros((1, wide), F32)
    for px in range(4):
        mine = jnp.where(x == px, gain[:, px * wide : (px + 1) * wide], mine)
    top = mine.astype(BF16).astype(F32)
    mid = (mine - top).astype(BF16).astype(F32)
    low = (mine - top - mid).astype(BF16).astype(F32)
    row = iota((EXTRA, wide), 0)
    pieces = jnp.where(row == 0, top, jnp.where(row == 1, mid, jnp.where(row == 2, low, 0.0)))
    pieces = pieces.astype(BF16)
    span = steps.shape[1]
    for member in range(TEAM):
        px = member // 4
        extra[member, :, 0:span] = steps[8 * px : 8 * px + 8]
        extra[member, :, span:] = pieces
    last = pltpu.make_async_copy(extra, out.at[:, pl.ds(rows, EXTRA)], extra_sem)
    last.start()
    for copy in stages:
        copy.wait()
    for copy in copies:
        copy.start()
    for copy in copies + more:
        copy.wait()
    last.wait()


def pack(place, inner, pairs, steps, gain):
    rows = inner.shape[0]
    width = inner.shape[1] // TEAM + pairs.shape[1] // 8
    return pl.pallas_call(
        pack_kernel,
        out_shape=jax.ShapeDtypeStruct((TEAM, rows + EXTRA, width), BF16),
        in_specs=[SMEM, HBM, ANY, VMEM, VMEM],
        out_specs=ANY,
        scratch_shapes=[
            pltpu.VMEM(inner.shape, BF16),
            pltpu.VMEM((TEAM, EXTRA, width), BF16),
            pltpu.SemaphoreType.DMA((rows // 8,)),
            pltpu.SemaphoreType.DMA((TEAM,)),
            pltpu.SemaphoreType.DMA((TEAM,)),
            pltpu.SemaphoreType.DMA,
        ],
        compiler_params=PARAMS,
        cost_estimate=cost(0, 4 * TEAM * rows * width),
        name="pack",
    )(place, keep(inner), pairs, keep(steps), keep(gain))


def taps(ext, row, rows, cols, weight):
    window = ext[pl.ds(row, rows + 8), cols]
    total = weight[4:5] + weight[0:1] * window[4 : 4 + rows]
    for k in range(1, 4):
        total = total + weight[k : k + 1] * window[4 + k : 4 + k + rows]
    return silu(total).astype(BF16)


def conv_kernel(
    place, recv, w_inner, w_pairs, bias, rate, xc, bc, lc_t, dt_t, tail, decay, logs, gains, ext
):
    x, y = place[0], place[1]
    members, tall, width = recv.shape
    rows = tall - EXTRA
    wide = xc.shape[1]
    ext[0:8] = jnp.zeros((8, width), F32)
    for m in range(members):
        ext[8 + m * rows : 8 + (m + 1) * rows] = recv[m, 0:rows].astype(F32)

    def chunk(m, _):
        row = pl.multiple_of(m * rows, rows)
        for start in range(0, wide, LANES):
            cols = slice(start, start + LANES)
            xc[pl.ds(row, rows), cols] = taps(ext, row, rows, cols, w_inner[:, cols])
        for start in range(0, width - wide, LANES):
            bc[pl.ds(row, rows), start : start + LANES] = taps(
                ext,
                row,
                rows,
                slice(wide + start, wide + start + LANES),
                w_pairs[:, start : start + LANES],
            )
        return 0

    lax.fori_loop(0, members, chunk, 0)

    own = bias.shape[1]
    mine = iota((8, own), 1) == 8 * x + iota((8, own), 0)
    shift = jnp.sum(jnp.where(mine, bias[...], 0.0), axis=1, keepdims=True)
    speed = jnp.sum(jnp.where(mine, -jnp.exp(rate[...]), 0.0), axis=1, keepdims=True)
    upper = (iota((BLOCK, BLOCK), 0) <= iota((BLOCK, BLOCK), 1)).astype(BF16)
    steps = []
    for b in range(4):
        v = recv[4 * b + y, rows:tall, 0:BLOCK].astype(F32) + shift
        steps.append(jnp.maximum(v, 0.0) + jnp.log1p(jnp.exp(-jnp.abs(v))))
    parts = split(jnp.concatenate([step * speed for step in steps], axis=0))
    parts = jnp.concatenate(parts, axis=0).astype(BF16)
    sums = jnp.dot(parts, upper, preferred_element_type=F32)
    ends = jnp.zeros((8, LANES), F32)
    for b in range(4):
        cum = sums[8 * b : 8 * b + 8] + sums[8 * b + 32 : 8 * b + 40] + sums[8 * b + 64 : 8 * b + 72]
        end = cum[:, BLOCK - 1 : BLOCK]
        ends = jnp.where(iota((8, LANES), 1) == b, end, ends)
        lc_t[b] = cum
        dt_t[b] = steps[b]
        tail[b] = spread_columns(jnp.exp(end - cum) * steps[b], wide)
    decay[...] = spread_columns(jnp.exp(ends), wide)[0:8]
    by_block = columns(ends)
    logs[...] = jnp.broadcast_to(
        by_block[0:1] + by_block[1:2] + by_block[2:3] + by_block[3:4], (8, LANES)
    )
    for m in range(members):
        pieces = recv[m, rows:tall, BLOCK:].astype(F32)
        gains[m : m + 1] = pieces[0:1] + pieces[1:2] + pieces[2:3]


def whole(shape):
    return pl.BlockSpec(shape, lambda i, p: (0,) * len(shape))


def weight_specs(wide, narrow):
    return [
        pl.BlockSpec((5, wide), lambda i, p: (0, 4 * p[1] + p[0])),
        pl.BlockSpec((5, narrow), lambda i, p: (0, 2 * p[1] + lax.div(p[0], 2))),
    ]


def conv(place, recv, w_inner, w_pairs, bias, rate):
    members, tall, width = recv.shape
    wide = w_inner.shape[1] // TEAM
    narrow = width - wide
    total = members * (tall - EXTRA)
    shapes = (
        ((total, wide), BF16),
        ((total, narrow), BF16),
        ((4, 8, BLOCK), F32),
        ((4, 8, BLOCK), F32),
        ((4, BLOCK, wide), F32),
        ((8, wide), F32),
        ((8, LANES), F32),
        ((members, wide), F32),
    )
    return pl.pallas_call(
        conv_kernel,
        out_shape=tuple(jax.ShapeDtypeStruct(*s) for s in shapes),
        grid_spec=pltpu.PrefetchScalarGridSpec(
            num_scalar_prefetch=1,
            grid=(1,),
            in_specs=[whole(recv.shape)]
            + weight_specs(wide, narrow)
            + [whole(bias.shape), whole(rate.shape)],
            out_specs=tuple(whole(s[0]) for s in shapes),
            scratch_shapes=[pltpu.VMEM((8 + total, width), F32)],
        ),
        compiler_params=PARAMS,
        cost_estimate=cost(20 * total * width, 4 * total * width, 2 * total * width),
        name="conv",
    )(place, recv, w_inner, w_pairs, bias, rate)


def state_kernel(
    place,
    first,
    halo,
    w_inner,
    w_pairs,
    xc0,
    bc0,
    tail,
    decay,
    logs,
    xc,
    bc,
    states,
    payload,
    ext,
    head_x,
    head_b,
    local,
    sem,
):
    count = first.shape[0]
    total, wide = xc0.shape
    narrow = bc0.shape[1]
    rest = pl.ds(count, total - count)
    copies = [
        pltpu.make_async_copy(xc0.at[rest], xc.at[rest], sem.at[0]),
        pltpu.make_async_copy(bc0.at[rest], bc.at[rest], sem.at[1]),
        pltpu.make_async_copy(head_x, xc.at[pl.ds(0, count)], sem.at[2]),
        pltpu.make_async_copy(head_b, bc.at[pl.ds(0, count)], sem.at[3]),
    ]
    copies[0].start()
    copies[1].start()
    ext[0:8] = halo[count - 8 : count].astype(F32)
    ext[8 : 8 + count] = first[...].astype(F32)
    for start in range(0, wide, LANES):
        cols = slice(start, start + LANES)
        head_x[:, cols] = taps(ext, 0, count, cols, w_inner[:, cols])
    for start in range(0, narrow, LANES):
        head_b[:, start : start + LANES] = taps(
            ext,
            0,
            count,
            slice(wide + start, wide + start + LANES),
            w_pairs[:, start : start + LANES],
        )
    copies[2].start()
    copies[3].start()
    sum_state = jnp.zeros((LANES, wide), F32)
    for b in range(4):
        rows = slice(b * BLOCK, (b + 1) * BLOCK)
        if b == 0:
            block = jnp.concatenate([head_x[...], xc0[count:BLOCK]], axis=0)
            keys = jnp.concatenate([head_b[:, 0:LANES], bc0[count:BLOCK, 0:LANES]], axis=0)
        else:
            block, keys = xc0[rows], bc0[rows, 0:LANES]
        weighted = (block.astype(F32) * tail[b]).astype(BF16)
        one = lax.dot_general(
            keys, weighted, (((0,), (0,)), ((), ())), preferred_element_type=F32
        )
        local[b] = one
        copies.append(pltpu.make_async_copy(local.at[b], states.at[b], sem.at[4 + b]))
        copies[-1].start()
        sum_state = decay[b : b + 1] * sum_state + one
    parts, depth, _ = payload.shape
    payload[:, :, 0:wide] = sum_state.reshape(parts, depth, wide)
    for part in range(parts):
        for row in range(0, depth, 8):
            payload[part, row : row + 8, wide : wide + LANES] = logs[...]
    for copy in copies:
        copy.wait()


def state(place, first, halo, w_inner, w_pairs, xc0, bc0, tail, decay, logs, parts):
    count, width = first.shape
    total, wide = xc0.shape
    narrow = width - wide
    payload_shape = (parts, LANES // parts, wide + LANES)
    return pl.pallas_call(
        state_kernel,
        out_shape=(
            pltpu.HBM((total, wide), BF16),
            pltpu.HBM((total, narrow), BF16),
            pltpu.HBM((4, LANES, wide), F32),
            jax.ShapeDtypeStruct(payload_shape, F32),
        ),
        grid_spec=pltpu.PrefetchScalarGridSpec(
            num_scalar_prefetch=1,
            grid=(1,),
            in_specs=[whole(first.shape), whole(halo.shape)]
            + weight_specs(wide, narrow)
            + [whole(a.shape) for a in (xc0, bc0, tail, decay, logs)],
            out_specs=(ANY, ANY, ANY, whole(payload_shape)),
            scratch_shapes=[
                pltpu.VMEM((8 + count, width), F32),
                pltpu.VMEM((count, wide), BF16),
                pltpu.VMEM((count, narrow), BF16),
                pltpu.VMEM((4, LANES, wide), F32),
                pltpu.SemaphoreType.DMA((8,)),
            ],
        ),
        compiler_params=PARAMS,
        cost_estimate=cost(2 * total * wide * LANES, 8 * total * wide),
        name="state",
    )(place, first, halo, w_inner, w_pairs, xc0, bc0, tail, decay, logs)


def intra_kernel(place, xc, bc, lc_t, dt_t, skip, own_gate, got_a, got_b, got_c, out, factor):
    wide = out.shape[1]
    heads = lc_t.shape[1]
    scores = lax.dot_general(
        bc[:, LANES:], bc[:, 0:LANES], (((1,), (1,)), ((), ())), preferred_element_type=F32
    )
    half = BLOCK // 2
    lower = iota((half, half), 0) >= iota((half, half), 1)
    own = skip.shape[1]
    gain = widen(
        jnp.broadcast_to(skip[...], (8, own)),
        (iota((own, wide), 1) // 64 + heads * place[0] == iota((own, wide), 0)).astype(F32),
    )[0:1]
    far = lax.rem(place[0] - pl.program_id(0) + 4, 4)
    gate = own_gate[...].astype(F32)
    for distance, got in ((1, got_a), (2, got_b), (3, got_c)):
        gate = jnp.where(far == distance, got[...].astype(F32), gate)
    gate = silu(gate)
    cum = lc_t[0]
    factor[...] = (gate * spread_columns(jnp.exp(cum), wide)).astype(BF16)
    log2e = 1.4426950408889634
    late = cum * log2e
    early = late - jnp.log(dt_t[0]) * log2e
    late = columns(late)
    top = scores[0:half, 0:half]
    left, right = scores[half:, 0:half], scores[half:, half:]
    for pair in range(heads // 2):
        outs = []
        for h in (2 * pair, 2 * pair + 1):
            upper_col, lower_col = late[0:half, h : h + 1], late[half:, h : h + 1]
            first, second = early[h : h + 1, 0:half], early[h : h + 1, half:]
            values = xc[:, h * 64 : (h + 1) * 64]
            w_top = top * jnp.exp2(jnp.where(lower, upper_col - first, -jnp.inf))
            w_left = left * jnp.exp2(lower_col - first)
            w_right = right * jnp.exp2(jnp.where(lower, lower_col - second, -jnp.inf))
            w_low = jnp.concatenate([w_left, w_right], axis=1).astype(BF16)
            outs.append(
                jnp.concatenate(
                    [
                        jnp.dot(w_top.astype(BF16), values[0:half], preferred_element_type=F32),
                        jnp.dot(w_low, values, preferred_element_type=F32),
                    ],
                    axis=0,
                )
            )
        cols = slice(2 * pair * 64, 2 * (pair + 1) * 64)
        mixed = jnp.concatenate(outs, axis=1) + gain[:, cols] * xc[:, cols].astype(F32)
        out[:, cols] = (mixed * gate[:, cols]).astype(BF16)


def intra(place, xc, bc, lc_t, dt_t, skip, gate_raw, got):
    total, wide = xc.shape
    narrow = bc.shape[1]
    heads = lc_t.shape[1]
    return pl.pallas_call(
        intra_kernel,
        out_shape=(pltpu.HBM((total, wide), BF16),) * 2,
        grid_spec=pltpu.PrefetchScalarGridSpec(
            num_scalar_prefetch=1,
            grid=(4,),
            in_specs=[
                pl.BlockSpec((BLOCK, wide), lambda b, p: (b, 0)),
                pl.BlockSpec((BLOCK, narrow), lambda b, p: (b, 0)),
                pl.BlockSpec((1, heads, BLOCK), lambda b, p: (b, 0, 0)),
                pl.BlockSpec((1, heads, BLOCK), lambda b, p: (b, 0, 0)),
                whole(skip.shape),
                pl.BlockSpec((BLOCK, wide), lambda b, p: (0, p[0])),
            ]
            + [whole(a.shape) for a in got],
            out_specs=(pl.BlockSpec((BLOCK, wide), lambda b, p: (b, 0)),) * 2,
        ),
        compiler_params=PARAMS,
        cost_estimate=cost(2 * total * BLOCK * wide * 4, 12 * total * wide, heads * total * BLOCK),
        name="intra",
    )(place, xc, bc, lc_t, dt_t, skip, keep(gate_raw), *got)


def scan_kernel(recv, out):
    chunks, rows, width = recv.shape
    wide = out.shape[2]
    logs = jnp.concatenate([recv[k, 0:1, wide:width] for k in range(chunks)], axis=0)
    logs = jnp.where(iota(logs.shape, 1) < wide // 64, logs, 0.0)
    decay = widen(jnp.exp(logs), spread(LANES, wide))
    carry = jnp.zeros((rows, wide), F32)
    for k in range(chunks):
        out[k] = carry
        carry = decay[k : k + 1] * carry + recv[k, :, 0:wide]


def scan(recv):
    chunks, rows, width = recv.shape
    return pl.pallas_call(
        scan_kernel,
        out_shape=jax.ShapeDtypeStruct((chunks, rows, width - LANES), F32),
        in_specs=[VMEM],
        out_specs=VMEM,
        compiler_params=PARAMS,
        cost_estimate=cost(4 * chunks * rows * width, 8 * chunks * rows * width),
        name="scan",
    )(recv)


def finish_kernel(carry, states, decay, bc, mixed, factor, out, s_in, c_in, m_in, f_in, sem):
    wide = mixed.shape[1]
    copies = []
    for b in range(4):
        rows = pl.ds(b * BLOCK, BLOCK)
        copies.append(
            [
                pltpu.make_async_copy(bc.at[rows, pl.ds(LANES, LANES)], c_in.at[b], sem.at[b, 0]),
                pltpu.make_async_copy(mixed.at[rows], m_in.at[b], sem.at[b, 1]),
                pltpu.make_async_copy(factor.at[rows], f_in.at[b], sem.at[b, 2]),
                pltpu.make_async_copy(states.at[b], s_in.at[b], sem.at[b, 3]),
            ]
        )
    for group in copies:
        for copy in group:
            copy.start()
    start = carry[...].reshape(LANES, wide)
    for b in range(4):
        for copy in copies[b]:
            copy.wait()
        carried = jnp.dot(c_in[b], start.astype(BF16), preferred_element_type=F32)
        gated = m_in[b].astype(F32) + carried * f_in[b].astype(F32)
        count = BLOCK // out.shape[1]
        out[b * count : (b + 1) * count] = gated.astype(BF16).reshape(count, -1, wide)
        start = decay[b : b + 1] * start + s_in[b]


def finish(carry, states, decay, bc, mixed, factor, rows):
    total, wide = mixed.shape
    return pl.pallas_call(
        finish_kernel,
        out_shape=jax.ShapeDtypeStruct((total // rows, rows, wide), BF16),
        in_specs=[VMEM, ANY, VMEM, ANY, ANY, ANY],
        out_specs=VMEM,
        scratch_shapes=[
            pltpu.VMEM((4, LANES, wide), F32),
            pltpu.VMEM((4, BLOCK, LANES), BF16),
            pltpu.VMEM((4, BLOCK, wide), BF16),
            pltpu.VMEM((4, BLOCK, wide), BF16),
            pltpu.SemaphoreType.DMA((4, 4)),
        ],
        compiler_params=PARAMS,
        cost_estimate=cost(2 * total * wide * 200, 6 * total * wide),
        name="finish",
    )(carry, keep(states), decay, keep(bc), keep(mixed), keep(factor))


def post_kernel(slabs, gains, out):
    wide = slabs.shape[2]
    for y in range(4):
        for half in range(2):
            left, right = 8 * half + y, 8 * half + 4 + y
            a, b = slabs[left].astype(F32), slabs[right].astype(F32)
            mean = (
                jnp.sum(a * a, axis=1, keepdims=True) + jnp.sum(b * b, axis=1, keepdims=True)
            ) / (2 * wide)
            inv = lax.rsqrt(mean + 1e-5)
            at = (4 * y + 2 * half) * wide
            out[:, at : at + wide] = (a * inv * gains[left : left + 1]).astype(BF16)
            out[:, at + wide : at + 2 * wide] = (b * inv * gains[right : right + 1]).astype(BF16)


def post(slabs, gains):
    members, rows, wide = slabs.shape
    return pl.pallas_call(
        post_kernel,
        out_shape=jax.ShapeDtypeStruct((rows, members * wide), BF16),
        in_specs=[VMEM, VMEM],
        out_specs=VMEM,
        compiler_params=PARAMS,
        cost_estimate=cost(6 * members * rows * wide, 4 * members * rows * wide),
        name="post",
    )(slabs, gains)


def on_device(
    inner_raw,
    pairs_raw,
    gate_raw,
    step_raw,
    step_bias,
    rate_log,
    skip_gain,
    conv_inner,
    conv_pairs,
    norm_gain,
):
    places = lax.axis_size("context")
    shards = lax.axis_size("head")
    chunks = places // 4
    x = (lax.axis_index("context") % 4).astype(jnp.int32)
    place = jnp.stack([x, lax.axis_index("head").astype(jnp.int32)])
    rows = inner_raw.shape[0]
    after = [(c, c + 4) for c in range(places - 4)]
    teams = [list(range(TEAM * k, TEAM * (k + 1))) for k in range(places * shards // TEAM)]
    lines = [[4 * k + s for k in range(chunks)] for s in range(4)]
    rings = [[4 * k + s for s in range(4)] for k in range(chunks)]

    packed = pack(
        place, inner_raw, pairs_raw.reshape(rows, -1), step_raw.T, norm_gain.reshape(1, -1)
    )
    width = gate_raw.shape[1] // 4
    gate_later, packed = lax.optimization_barrier((gate_raw, packed))
    gates = [
        lax.dynamic_slice_in_dim(gate_later, (x + far) % 4 * width, width, 1) for far in (1, 2, 3)
    ]
    recv = lax.all_to_all(
        packed, ("context", "head"), split_axis=0, concat_axis=0, axis_index_groups=teams
    )
    gates = [
        lax.ppermute(gate, "context", [(c, c - c % 4 + (c + far) % 4) for c in range(places)])
        for far, gate in zip((1, 2, 3), gates)
    ]
    halo = lax.ppermute(recv[TEAM - 1, rows - 16 : rows], "context", after)

    pair_taps = conv_pairs.reshape(conv_pairs.shape[0], -1)
    xc0, bc0, lc_t, dt_t, tail, decay, logs, gains = conv(
        place, recv, conv_inner, pair_taps, step_bias.reshape(1, -1), rate_log.reshape(1, -1)
    )
    xc, bc, states, payload = state(
        place, recv[0, :16], halo, conv_inner, pair_taps, xc0, bc0, tail, decay, logs, chunks
    )
    *gates, payload = lax.optimization_barrier((*gates, payload))
    totals = lax.all_to_all(
        payload, "context", split_axis=0, concat_axis=0, axis_index_groups=lines
    )
    carry = lax.all_to_all(
        scan(totals), "context", split_axis=0, concat_axis=0, axis_index_groups=lines
    )
    mixed, factor = intra(place, xc, bc, lc_t, dt_t, skip_gain.reshape(1, -1), gate_raw, gates)
    slabs = finish(carry, states, decay, bc, mixed, factor, rows)
    slabs = lax.all_to_all(
        slabs, ("context", "head"), split_axis=0, concat_axis=0, axis_index_groups=teams
    )
    return post(slabs, gains)


def solution(mesh):
    placed = (
        P(("rollout", "context", "head"), None),
        P(("rollout", "context", "head"), None, None, None),
        P(("rollout", "context"), "head"),
        P(("rollout", "context"), "head"),
        P("head"),
        P("head"),
        P("head"),
        P(),
        P(),
        P("head"),
    )
    return jax.shard_map(
        on_device,
        mesh=mesh,
        in_specs=placed,
        out_specs=P(("rollout", "context", "head"), None),
        check_vma=False,
    )
```

```python
import functools

import jax
import jax.numpy as jnp
from jax import lax
from jax.experimental import pallas as pl
from jax.experimental.pallas import tpu as pltpu
from jax.sharding import PartitionSpec as P

BLOCK = 256
HIGH = lax.Precision.HIGHEST
F32 = jnp.float32
BF16 = jnp.bfloat16
LANES = 128
ANY = pl.BlockSpec(memory_space=pl.ANY)
VMEM = pl.BlockSpec(memory_space=pltpu.VMEM)
SMEM = pl.BlockSpec(memory_space=pltpu.SMEM)
HBM = pl.BlockSpec(memory_space=pltpu.HBM)
PARAMS = pltpu.CompilerParams(vmem_limit_bytes=24 * 1024 * 1024)
LARGE = pltpu.CompilerParams(vmem_limit_bytes=56 * 1024 * 1024)
TEAM = 16


def cost(flops, bytes_accessed, transcendentals=0):
    return pl.CostEstimate(
        flops=flops, bytes_accessed=bytes_accessed, transcendentals=transcendentals
    )


def keep(array):
    return pltpu.with_memory_space_constraint(array, pltpu.HBM)


def iota(shape, dim):
    return lax.broadcasted_iota(jnp.int32, shape, dim)


def spread(rows, channels):
    return (iota((rows, channels), 1) // 64 == iota((rows, channels), 0)).astype(F32)


def widen(value, one_hot):
    return jnp.dot(value, one_hot, precision=HIGH, preferred_element_type=F32)


def columns(value):
    padding = jnp.zeros((LANES - value.shape[0], value.shape[1]), F32)
    return jnp.concatenate([value, padding], axis=0).T


def split(value):
    top = value.astype(BF16).astype(F32)
    mid = (value - top).astype(BF16).astype(F32)
    return [top, mid, value - top - mid]


def spread_columns(value, channels):
    padding = jnp.zeros((LANES - 24, value.shape[1]), F32)
    left = jnp.concatenate(split(value) + [padding], axis=0).T.astype(BF16)
    row = iota((LANES, channels), 0)
    one_hot = (row % 8 == iota((LANES, channels), 1) // 64) & (row < 24)
    return jnp.dot(left, one_hot.astype(BF16), preferred_element_type=F32)


def silu(v):
    return v / (1.0 + jnp.exp(-v))


def pack_kernel(
    inner, pairs, out, staged, stage_sem, sem, pairs_sem
):
    rows, full = inner.shape
    wide, narrow = full // TEAM, pairs.shape[1] // 8
    stages, copies, more = [], [], []
    for member in range(TEAM):
        px, py = member // 4, member % 4
        part = pl.ds((4 * py + px) * wide, wide)
        stages.append(
            pltpu.make_async_copy(inner.at[:, part], staged.at[:, part], stage_sem.at[member])
        )
        copies.append(
            pltpu.make_async_copy(
                staged.at[:, part], out.at[member, pl.ds(0, rows), pl.ds(0, wide)], sem.at[member]
            )
        )
        more.append(
            pltpu.make_async_copy(
                pairs.at[:, pl.ds((2 * py + px // 2) * narrow, narrow)],
                out.at[member, pl.ds(0, rows), pl.ds(wide, narrow)],
                pairs_sem.at[member],
            )
        )
    for copy in stages:
        copy.start()
    for copy in more:
        copy.start()
    for stage, copy in zip(stages, copies):
        stage.wait()
        copy.start()
    for copy in copies + more:
        copy.wait()


def pack(inner, pairs):
    rows = inner.shape[0]
    width = inner.shape[1] // TEAM + pairs.shape[1] // 8
    return pl.pallas_call(
        pack_kernel,
        out_shape=jax.ShapeDtypeStruct((TEAM, rows, width), BF16),
        in_specs=[ANY, ANY],
        out_specs=ANY,
        scratch_shapes=[
            pltpu.VMEM(inner.shape, BF16),
            pltpu.SemaphoreType.DMA((TEAM,)),
            pltpu.SemaphoreType.DMA((TEAM,)),
            pltpu.SemaphoreType.DMA((TEAM,)),
        ],
        compiler_params=PARAMS,
        cost_estimate=cost(0, 4 * TEAM * rows * width),
        name="pack",
    )(keep(inner), pairs)


def taps(ext, row, rows, cols, weight):
    window = ext[pl.ds(row, rows + 8), cols]
    total = weight[4:5] + weight[0:1] * window[4 : 4 + rows]
    for k in range(1, 4):
        total = total + weight[k : k + 1] * window[4 + k : 4 + k + rows]
    return silu(total).astype(BF16)


def conv_kernel(
    place,
    recv,
    w_inner,
    w_pairs,
    bias,
    rate,
    own_steps,
    got_a,
    got_b,
    got_c,
    xc,
    bc,
    lc_t,
    dt_t,
    tail,
    decay,
    logs,
    ext,
):
    x = place[0]
    members, rows, width = recv.shape
    wide = xc.shape[1]
    ext[0:8] = jnp.zeros((8, width), F32)
    for m in range(members):
        ext[8 + m * rows : 8 + (m + 1) * rows] = recv[m].astype(F32)

    def chunk(m, _):
        row = pl.multiple_of(m * rows, rows)
        for start in range(0, wide, LANES):
            cols = slice(start, start + LANES)
            xc[pl.ds(row, rows), cols] = taps(ext, row, rows, cols, w_inner[:, cols])
        for start in range(0, width - wide, LANES):
            bc[pl.ds(row, rows), start : start + LANES] = taps(
                ext,
                row,
                rows,
                slice(wide + start, wide + start + LANES),
                w_pairs[:, start : start + LANES],
            )
        return 0

    lax.fori_loop(0, members, chunk, 0)

    own = bias.shape[1]
    mine = iota((8, own), 1) == 8 * x + iota((8, own), 0)
    shift = jnp.sum(jnp.where(mine, bias[...], 0.0), axis=1, keepdims=True)
    speed = jnp.sum(jnp.where(mine, -jnp.exp(rate[...]), 0.0), axis=1, keepdims=True)
    upper = (iota((BLOCK, BLOCK), 0) <= iota((BLOCK, BLOCK), 1)).astype(BF16)
    steps = []
    for b in range(4):
        far = lax.rem(x - b + 4, 4)
        v = own_steps[...].astype(F32)
        for distance, got in ((1, got_a), (2, got_b), (3, got_c)):
            v = jnp.where(far == distance, got[...].astype(F32), v)
        v = v + shift
        steps.append(jnp.maximum(v, 0.0) + jnp.log1p(jnp.exp(-jnp.abs(v))))
    parts = split(jnp.concatenate([step * speed for step in steps], axis=0))
    parts = jnp.concatenate(parts, axis=0).astype(BF16)
    sums = jnp.dot(parts, upper, preferred_element_type=F32)
    ends = jnp.zeros((8, LANES), F32)
    for b in range(4):
        cum = sums[8 * b : 8 * b + 8] + sums[8 * b + 32 : 8 * b + 40] + sums[8 * b + 64 : 8 * b + 72]
        end = cum[:, BLOCK - 1 : BLOCK]
        ends = jnp.where(iota((8, LANES), 1) == b, end, ends)
        lc_t[b] = cum
        dt_t[b] = steps[b]
        tail[b] = spread_columns(jnp.exp(end - cum) * steps[b], wide)
    decay[...] = spread_columns(jnp.exp(ends), wide)[0:8]
    by_block = columns(ends)
    logs[...] = jnp.broadcast_to(
        by_block[0:1] + by_block[1:2] + by_block[2:3] + by_block[3:4], (8, LANES)
    )


def whole(shape):
    return pl.BlockSpec(shape, lambda i, p: (0,) * len(shape))


def weight_specs(wide, narrow):
    return [
        pl.BlockSpec((5, wide), lambda i, p: (0, 4 * p[1] + p[0])),
        pl.BlockSpec((5, narrow), lambda i, p: (0, 2 * p[1] + lax.div(p[0], 2))),
    ]


def conv(place, recv, w_inner, w_pairs, bias, rate, steps):
    members, rows, width = recv.shape
    wide = w_inner.shape[1] // TEAM
    narrow = width - wide
    total = members * rows
    shapes = (
        ((total, wide), BF16),
        ((total, narrow), BF16),
        ((4, 8, BLOCK), F32),
        ((4, 8, BLOCK), F32),
        ((4, BLOCK, wide), F32),
        ((8, wide), F32),
        ((8, LANES), F32),
    )
    return pl.pallas_call(
        conv_kernel,
        out_shape=tuple(jax.ShapeDtypeStruct(*s) for s in shapes),
        grid_spec=pltpu.PrefetchScalarGridSpec(
            num_scalar_prefetch=1,
            grid=(1,),
            in_specs=[whole(recv.shape)]
            + weight_specs(wide, narrow)
            + [whole(a.shape) for a in (bias, rate, *steps)],
            out_specs=tuple(whole(s[0]) for s in shapes),
            scratch_shapes=[pltpu.VMEM((8 + total, width), F32)],
        ),
        compiler_params=PARAMS,
        cost_estimate=cost(20 * total * width, 4 * total * width, 2 * total * width),
        name="conv",
    )(place, recv, w_inner, w_pairs, bias, rate, *steps)


def state_kernel(
    place,
    first,
    halo,
    w_inner,
    w_pairs,
    xc0,
    bc0,
    tail,
    decay,
    logs,
    xc,
    bc,
    states,
    payload,
    ext,
    head_x,
    head_b,
    local,
    sem,
):
    count = first.shape[0]
    total, wide = xc0.shape
    narrow = bc0.shape[1]
    rest = pl.ds(count, total - count)
    copies = [
        pltpu.make_async_copy(xc0.at[rest], xc.at[rest], sem.at[0]),
        pltpu.make_async_copy(bc0.at[rest], bc.at[rest], sem.at[1]),
        pltpu.make_async_copy(head_x, xc.at[pl.ds(0, count)], sem.at[2]),
        pltpu.make_async_copy(head_b, bc.at[pl.ds(0, count)], sem.at[3]),
    ]
    copies[0].start()
    copies[1].start()
    ext[0:8] = halo[count - 8 : count].astype(F32)
    ext[8 : 8 + count] = first[...].astype(F32)
    for start in range(0, wide, LANES):
        cols = slice(start, start + LANES)
        head_x[:, cols] = taps(ext, 0, count, cols, w_inner[:, cols])
    for start in range(0, narrow, LANES):
        head_b[:, start : start + LANES] = taps(
            ext,
            0,
            count,
            slice(wide + start, wide + start + LANES),
            w_pairs[:, start : start + LANES],
        )
    copies[2].start()
    copies[3].start()
    sum_state = jnp.zeros((LANES, wide), F32)
    for b in range(4):
        rows = slice(b * BLOCK, (b + 1) * BLOCK)
        if b == 0:
            block = jnp.concatenate([head_x[...], xc0[count:BLOCK]], axis=0)
            keys = jnp.concatenate([head_b[:, 0:LANES], bc0[count:BLOCK, 0:LANES]], axis=0)
        else:
            block, keys = xc0[rows], bc0[rows, 0:LANES]
        weighted = (block.astype(F32) * tail[b]).astype(BF16)
        one = lax.dot_general(
            keys, weighted, (((0,), (0,)), ((), ())), preferred_element_type=F32
        )
        local[b] = one
        copies.append(pltpu.make_async_copy(local.at[b], states.at[b], sem.at[4 + b]))
        copies[-1].start()
        sum_state = decay[b : b + 1] * sum_state + one
    parts, depth, _ = payload.shape
    payload[:, :, 0:wide] = sum_state.reshape(parts, depth, wide)
    for part in range(parts):
        for row in range(0, depth, 8):
            payload[part, row : row + 8, wide : wide + LANES] = logs[...]
    for copy in copies:
        copy.wait()


def state(place, first, halo, w_inner, w_pairs, xc0, bc0, tail, decay, logs, parts):
    count, width = first.shape
    total, wide = xc0.shape
    narrow = width - wide
    payload_shape = (parts, LANES // parts, wide + LANES)
    return pl.pallas_call(
        state_kernel,
        out_shape=(
            pltpu.HBM((total, wide), BF16),
            pltpu.HBM((total, narrow), BF16),
            pltpu.HBM((4, LANES, wide), F32),
            jax.ShapeDtypeStruct(payload_shape, F32),
        ),
        grid_spec=pltpu.PrefetchScalarGridSpec(
            num_scalar_prefetch=1,
            grid=(1,),
            in_specs=[whole(first.shape), whole(halo.shape)]
            + weight_specs(wide, narrow)
            + [whole(a.shape) for a in (xc0, bc0, tail, decay, logs)],
            out_specs=(ANY, ANY, ANY, whole(payload_shape)),
            scratch_shapes=[
                pltpu.VMEM((8 + count, width), F32),
                pltpu.VMEM((count, wide), BF16),
                pltpu.VMEM((count, narrow), BF16),
                pltpu.VMEM((4, LANES, wide), F32),
                pltpu.SemaphoreType.DMA((8,)),
            ],
        ),
        compiler_params=PARAMS,
        cost_estimate=cost(2 * total * wide * LANES, 8 * total * wide),
        name="state",
    )(place, first, halo, w_inner, w_pairs, xc0, bc0, tail, decay, logs)


def intra_kernel(place, xc, bc, lc_t, dt_t, skip, own_gate, got_a, got_b, got_c, out, factor):
    wide = out.shape[1]
    heads = lc_t.shape[1]
    scores = lax.dot_general(
        bc[:, LANES:], bc[:, 0:LANES], (((1,), (1,)), ((), ())), preferred_element_type=F32
    )
    half = BLOCK // 2
    lower = iota((half, half), 0) >= iota((half, half), 1)
    own = skip.shape[1]
    gain = widen(
        jnp.broadcast_to(skip[...], (8, own)),
        (iota((own, wide), 1) // 64 + heads * place[0] == iota((own, wide), 0)).astype(F32),
    )[0:1]
    far = lax.rem(place[0] - pl.program_id(0) + 4, 4)
    gate = own_gate[...].astype(F32)
    for distance, got in ((1, got_a), (2, got_b), (3, got_c)):
        gate = jnp.where(far == distance, got[...].astype(F32), gate)
    gate = silu(gate)
    cum = lc_t[0]
    factor[...] = (gate * spread_columns(jnp.exp(cum), wide)).astype(BF16)
    log2e = 1.4426950408889634
    late = cum * log2e
    early = late - jnp.log(dt_t[0]) * log2e
    late = columns(late)
    top = scores[0:half, 0:half]
    left, right = scores[half:, 0:half], scores[half:, half:]
    for pair in range(heads // 2):
        outs = []
        for h in (2 * pair, 2 * pair + 1):
            upper_col, lower_col = late[0:half, h : h + 1], late[half:, h : h + 1]
            first, second = early[h : h + 1, 0:half], early[h : h + 1, half:]
            values = xc[:, h * 64 : (h + 1) * 64]
            w_top = top * jnp.exp2(jnp.where(lower, upper_col - first, -jnp.inf))
            w_left = left * jnp.exp2(lower_col - first)
            w_right = right * jnp.exp2(jnp.where(lower, lower_col - second, -jnp.inf))
            w_low = jnp.concatenate([w_left, w_right], axis=1).astype(BF16)
            outs.append(
                jnp.concatenate(
                    [
                        jnp.dot(w_top.astype(BF16), values[0:half], preferred_element_type=F32),
                        jnp.dot(w_low, values, preferred_element_type=F32),
                    ],
                    axis=0,
                )
            )
        cols = slice(2 * pair * 64, 2 * (pair + 1) * 64)
        mixed = jnp.concatenate(outs, axis=1) + gain[:, cols] * xc[:, cols].astype(F32)
        out[:, cols] = (mixed * gate[:, cols]).astype(BF16)


def intra(place, xc, bc, lc_t, dt_t, skip, gate_raw, got):
    total, wide = xc.shape
    narrow = bc.shape[1]
    heads = lc_t.shape[1]
    return pl.pallas_call(
        intra_kernel,
        out_shape=(pltpu.HBM((total, wide), BF16),) * 2,
        grid_spec=pltpu.PrefetchScalarGridSpec(
            num_scalar_prefetch=1,
            grid=(4,),
            in_specs=[
                pl.BlockSpec((BLOCK, wide), lambda b, p: (b, 0)),
                pl.BlockSpec((BLOCK, narrow), lambda b, p: (b, 0)),
                pl.BlockSpec((1, heads, BLOCK), lambda b, p: (b, 0, 0)),
                pl.BlockSpec((1, heads, BLOCK), lambda b, p: (b, 0, 0)),
                whole(skip.shape),
                pl.BlockSpec((BLOCK, wide), lambda b, p: (0, p[0])),
            ]
            + [whole(a.shape) for a in got],
            out_specs=(pl.BlockSpec((BLOCK, wide), lambda b, p: (b, 0)),) * 2,
        ),
        compiler_params=PARAMS,
        cost_estimate=cost(2 * total * BLOCK * wide * 4, 12 * total * wide, heads * total * BLOCK),
        name="intra",
    )(place, xc, bc, lc_t, dt_t, skip, keep(gate_raw), *got)


def scan_kernel(recv, out):
    chunks, rows, width = recv.shape
    wide = out.shape[2]
    logs = jnp.concatenate([recv[k, 0:1, wide:width] for k in range(chunks)], axis=0)
    logs = jnp.where(iota(logs.shape, 1) < wide // 64, logs, 0.0)
    decay = widen(jnp.exp(logs), spread(LANES, wide))
    carry = jnp.zeros((rows, wide), F32)
    for k in range(chunks):
        out[k] = carry
        carry = decay[k : k + 1] * carry + recv[k, :, 0:wide]


def scan(recv):
    chunks, rows, width = recv.shape
    return pl.pallas_call(
        scan_kernel,
        out_shape=jax.ShapeDtypeStruct((chunks, rows, width - LANES), F32),
        in_specs=[VMEM],
        out_specs=VMEM,
        compiler_params=PARAMS,
        cost_estimate=cost(4 * chunks * rows * width, 8 * chunks * rows * width),
        name="scan",
    )(recv)


def finish_kernel(carry, states, decay, bc, mixed, factor, out, s_in, c_in, m_in, f_in, sem):
    wide = mixed.shape[1]
    copies = []
    for b in range(4):
        rows = pl.ds(b * BLOCK, BLOCK)
        copies.append(
            [
                pltpu.make_async_copy(bc.at[rows, pl.ds(LANES, LANES)], c_in.at[b], sem.at[b, 0]),
                pltpu.make_async_copy(mixed.at[rows], m_in.at[b], sem.at[b, 1]),
                pltpu.make_async_copy(factor.at[rows], f_in.at[b], sem.at[b, 2]),
                pltpu.make_async_copy(states.at[b], s_in.at[b], sem.at[b, 3]),
            ]
        )
    for group in copies:
        for copy in group:
            copy.start()
    start = carry[...].reshape(LANES, wide)
    for b in range(4):
        for copy in copies[b]:
            copy.wait()
        carried = jnp.dot(c_in[b], start.astype(BF16), preferred_element_type=F32)
        gated = m_in[b].astype(F32) + carried * f_in[b].astype(F32)
        count = BLOCK // out.shape[1]
        out[b * count : (b + 1) * count] = gated.astype(BF16).reshape(count, -1, wide)
        start = decay[b : b + 1] * start + s_in[b]


def finish(carry, states, decay, bc, mixed, factor, rows):
    total, wide = mixed.shape
    return pl.pallas_call(
        finish_kernel,
        out_shape=jax.ShapeDtypeStruct((total // rows, rows, wide), BF16),
        in_specs=[VMEM, ANY, VMEM, ANY, ANY, ANY],
        out_specs=VMEM,
        scratch_shapes=[
            pltpu.VMEM((4, LANES, wide), F32),
            pltpu.VMEM((4, BLOCK, LANES), BF16),
            pltpu.VMEM((4, BLOCK, wide), BF16),
            pltpu.VMEM((4, BLOCK, wide), BF16),
            pltpu.SemaphoreType.DMA((4, 4)),
        ],
        compiler_params=PARAMS,
        cost_estimate=cost(2 * total * wide * 200, 6 * total * wide),
        name="finish",
    )(carry, keep(states), decay, keep(bc), keep(mixed), keep(factor))


def post_kernel(place, slabs, own_gain, got_a, got_b, got_c, out):
    wide = slabs.shape[2]
    for y in range(4):
        far = lax.rem(place[1] - y + 4, 4)
        gain = own_gain[...]
        for distance, got in ((1, got_a), (2, got_b), (3, got_c)):
            gain = jnp.where(far == distance, got[...], gain)
        for half in range(2):
            left, right = 8 * half + y, 8 * half + 4 + y
            a, b = slabs[left].astype(F32), slabs[right].astype(F32)
            mean = (
                jnp.sum(a * a, axis=1, keepdims=True) + jnp.sum(b * b, axis=1, keepdims=True)
            ) / (2 * wide)
            inv = lax.rsqrt(mean + 1e-5)
            at = 2 * half * wide
            low, high = gain[:, at : at + wide], gain[:, at + wide : at + 2 * wide]
            at = at + 4 * y * wide
            out[:, at : at + wide] = (a * inv * low).astype(BF16)
            out[:, at + wide : at + 2 * wide] = (b * inv * high).astype(BF16)


def post(place, slabs, gains):
    members, rows, wide = slabs.shape
    return pl.pallas_call(
        post_kernel,
        out_shape=jax.ShapeDtypeStruct((rows, members * wide), BF16),
        in_specs=[SMEM] + [VMEM] * 5,
        out_specs=VMEM,
        compiler_params=PARAMS,
        cost_estimate=cost(6 * members * rows * wide, 4 * members * rows * wide),
        name="post",
    )(place, slabs, *gains)


def on_device(
    inner_raw,
    pairs_raw,
    gate_raw,
    step_raw,
    step_bias,
    rate_log,
    skip_gain,
    conv_inner,
    conv_pairs,
    norm_gain,
):
    places = lax.axis_size("context")
    shards = lax.axis_size("head")
    chunks = places // 4
    x = (lax.axis_index("context") % 4).astype(jnp.int32)
    place = jnp.stack([x, lax.axis_index("head").astype(jnp.int32)])
    rows = inner_raw.shape[0]
    after = [(c, c + 4) for c in range(places - 4)]
    teams = [list(range(TEAM * k, TEAM * (k + 1))) for k in range(places * shards // TEAM)]
    lines = [[4 * k + s for k in range(chunks)] for s in range(4)]

    def around(axis, position, pick):
        count = lax.axis_size(axis)
        routes = [[(c, c - c % 4 + (c + far) % 4) for c in range(count)] for far in (1, 2, 3)]
        return [
            lax.ppermute(pick((position + far) % 4), axis, route)
            for far, route in zip((1, 2, 3), routes)
        ]

    packed = pack(inner_raw, pairs_raw.reshape(rows, -1))
    step_rows = step_raw.T
    gain_row = norm_gain.reshape(1, -1)
    gate_later, steps_later, gain_later, packed = lax.optimization_barrier(
        (gate_raw, step_rows, gain_row, packed)
    )
    recv = lax.all_to_all(
        packed, ("context", "head"), split_axis=0, concat_axis=0, axis_index_groups=teams
    )
    width = gate_raw.shape[1] // 4
    y = lax.axis_index("head").astype(jnp.int32)
    steps = around("context", x, lambda p: lax.dynamic_slice_in_dim(steps_later, 8 * p, 8, 0))
    gains = around("head", y, lambda p: gain_later)
    gates = around(
        "context", x, lambda p: lax.dynamic_slice_in_dim(gate_later, p * width, width, 1)
    )
    *steps, recv = lax.optimization_barrier((*steps, recv))
    halo = lax.ppermute(recv[TEAM - 1, rows - 16 : rows], "context", after)

    pair_taps = conv_pairs.reshape(conv_pairs.shape[0], -1)
    own_steps = lax.dynamic_slice_in_dim(step_rows, 8 * x, 8, 0)
    xc0, bc0, lc_t, dt_t, tail, decay, logs = conv(
        place,
        recv,
        conv_inner,
        pair_taps,
        step_bias.reshape(1, -1),
        rate_log.reshape(1, -1),
        [own_steps] + steps,
    )
    xc, bc, states, payload = state(
        place, recv[0, :16], halo, conv_inner, pair_taps, xc0, bc0, tail, decay, logs, chunks
    )
    *gates, payload = lax.optimization_barrier((*gates, payload))
    totals = lax.all_to_all(
        payload, "context", split_axis=0, concat_axis=0, axis_index_groups=lines
    )
    *gains, totals = lax.optimization_barrier((*gains, totals))
    carry = lax.all_to_all(
        scan(totals), "context", split_axis=0, concat_axis=0, axis_index_groups=lines
    )
    mixed, factor = intra(place, xc, bc, lc_t, dt_t, skip_gain.reshape(1, -1), gate_raw, gates)
    slabs = finish(carry, states, decay, bc, mixed, factor, rows)
    slabs = lax.all_to_all(
        slabs, ("context", "head"), split_axis=0, concat_axis=0, axis_index_groups=teams
    )
    return post(place, slabs, [gain_row] + gains)


def solution(mesh):
    placed = (
        P(("rollout", "context", "head"), None),
        P(("rollout", "context", "head"), None, None, None),
        P(("rollout", "context"), "head"),
        P(("rollout", "context"), "head"),
        P("head"),
        P("head"),
        P("head"),
        P(),
        P(),
        P("head"),
    )
    return jax.shard_map(
        on_device,
        mesh=mesh,
        in_specs=placed,
        out_specs=P(("rollout", "context", "head"), None),
        check_vma=False,
    )
```

```python
import functools

import jax
import jax.numpy as jnp
from jax import lax
from jax.experimental import pallas as pl
from jax.experimental.pallas import tpu as pltpu
from jax.sharding import PartitionSpec as P

BLOCK = 256
HIGH = lax.Precision.HIGHEST
F32 = jnp.float32
BF16 = jnp.bfloat16
LANES = 128
ANY = pl.BlockSpec(memory_space=pl.ANY)
VMEM = pl.BlockSpec(memory_space=pltpu.VMEM)
HBM = pl.BlockSpec(memory_space=pltpu.HBM)
PARAMS = pltpu.CompilerParams(vmem_limit_bytes=24 * 1024 * 1024)
LARGE = pltpu.CompilerParams(vmem_limit_bytes=56 * 1024 * 1024)
TEAM = 16


def cost(flops, bytes_accessed, transcendentals=0):
    return pl.CostEstimate(
        flops=flops, bytes_accessed=bytes_accessed, transcendentals=transcendentals
    )


def keep(array):
    return pltpu.with_memory_space_constraint(array, pltpu.HBM)


def iota(shape, dim):
    return lax.broadcasted_iota(jnp.int32, shape, dim)


def spread(rows, channels):
    return (iota((rows, channels), 1) // 64 == iota((rows, channels), 0)).astype(F32)


def widen(value, one_hot):
    return jnp.dot(value, one_hot, precision=HIGH, preferred_element_type=F32)


def columns(value):
    padding = jnp.zeros((LANES - value.shape[0], value.shape[1]), F32)
    return jnp.concatenate([value, padding], axis=0).T


def split(value):
    top = value.astype(BF16).astype(F32)
    mid = (value - top).astype(BF16).astype(F32)
    return [top, mid, value - top - mid]


def spread_columns(value, channels):
    padding = jnp.zeros((LANES - 24, value.shape[1]), F32)
    left = jnp.concatenate(split(value) + [padding], axis=0).T.astype(BF16)
    row = iota((LANES, channels), 0)
    one_hot = (row % 8 == iota((LANES, channels), 1) // 64) & (row < 24)
    return jnp.dot(left, one_hot.astype(BF16), preferred_element_type=F32)


def silu(v):
    half = 0.5 * v
    return half + half * jnp.tanh(half)


def pack_kernel(
    inner, pairs, out, staged, stage_sem, sem, pairs_sem
):
    rows, full = inner.shape
    wide, narrow = full // TEAM, pairs.shape[1] // 8
    stages, copies, more = [], [], []
    for member in range(TEAM):
        px, py = member // 4, member % 4
        part = pl.ds((4 * py + px) * wide, wide)
        stages.append(
            pltpu.make_async_copy(inner.at[:, part], staged.at[:, part], stage_sem.at[member])
        )
        copies.append(
            pltpu.make_async_copy(
                staged.at[:, part], out.at[member, pl.ds(0, rows), pl.ds(0, wide)], sem.at[member]
            )
        )
        more.append(
            pltpu.make_async_copy(
                pairs.at[:, pl.ds((2 * py + px // 2) * narrow, narrow)],
                out.at[member, pl.ds(0, rows), pl.ds(wide, narrow)],
                pairs_sem.at[member],
            )
        )
    for copy in stages:
        copy.start()
    for copy in more:
        copy.start()
    for stage, copy in zip(stages, copies):
        stage.wait()
        copy.start()
    for copy in copies + more:
        copy.wait()


def pack(inner, pairs):
    rows = inner.shape[0]
    width = inner.shape[1] // TEAM + pairs.shape[1] // 8
    return pl.pallas_call(
        pack_kernel,
        out_shape=jax.ShapeDtypeStruct((TEAM, rows, width), BF16),
        in_specs=[ANY, ANY],
        out_specs=ANY,
        scratch_shapes=[
            pltpu.VMEM(inner.shape, BF16),
            pltpu.SemaphoreType.DMA((TEAM,)),
            pltpu.SemaphoreType.DMA((TEAM,)),
            pltpu.SemaphoreType.DMA((TEAM,)),
        ],
        compiler_params=PARAMS,
        cost_estimate=cost(0, 4 * TEAM * rows * width),
        name="pack",
    )(keep(inner), pairs)


def taps(ext, row, rows, cols, weight):
    window = ext[pl.ds(row, rows + 8), cols]
    total = weight[4:5] + weight[0:1] * window[4 : 4 + rows]
    for k in range(1, 4):
        total = total + weight[k : k + 1] * window[4 + k : 4 + k + rows]
    return silu(total).astype(BF16)


def conv_kernel(
    recv,
    w_inner,
    w_pairs,
    bias,
    rate,
    own_steps,
    got_a,
    got_b,
    got_c,
    xc,
    bc,
    lc_t,
    dt_t,
    tail,
    decay,
    logs,
    ext,
):
    x = lax.rem(lax.axis_index("context"), 4)
    members, rows, width = recv.shape
    wide = xc.shape[1]
    ext[0:8] = jnp.zeros((8, width), F32)
    for m in range(members):
        ext[8 + m * rows : 8 + (m + 1) * rows] = recv[m].astype(F32)

    def chunk(m, _):
        row = pl.multiple_of(m * rows, rows)
        for start in range(0, wide, LANES):
            cols = slice(start, start + LANES)
            xc[pl.ds(row, rows), cols] = taps(ext, row, rows, cols, w_inner[:, cols])
        for start in range(0, width - wide, LANES):
            bc[pl.ds(row, rows), start : start + LANES] = taps(
                ext,
                row,
                rows,
                slice(wide + start, wide + start + LANES),
                w_pairs[:, start : start + LANES],
            )
        return 0

    lax.fori_loop(0, members, chunk, 0)

    own = bias.shape[1]
    mine = iota((8, own), 1) == 8 * x + iota((8, own), 0)
    shift = jnp.sum(jnp.where(mine, bias[...], 0.0), axis=1, keepdims=True)
    speed = jnp.sum(jnp.where(mine, -jnp.exp(rate[...]), 0.0), axis=1, keepdims=True)
    upper = (iota((BLOCK, BLOCK), 0) <= iota((BLOCK, BLOCK), 1)).astype(BF16)
    steps = []
    for b in range(4):
        far = lax.rem(x - b + 4, 4)
        v = own_steps[...].astype(F32)
        for distance, got in ((1, got_a), (2, got_b), (3, got_c)):
            v = jnp.where(far == distance, got[...].astype(F32), v)
        v = v + shift
        steps.append(jnp.maximum(v, 0.0) + jnp.log1p(jnp.exp(-jnp.abs(v))))
    parts = split(jnp.concatenate([step * speed for step in steps], axis=0))
    parts = jnp.concatenate(parts, axis=0).astype(BF16)
    sums = jnp.dot(parts, upper, preferred_element_type=F32)
    ends = jnp.zeros((8, LANES), F32)
    for b in range(4):
        cum = sums[8 * b : 8 * b + 8] + sums[8 * b + 32 : 8 * b + 40] + sums[8 * b + 64 : 8 * b + 72]
        end = cum[:, BLOCK - 1 : BLOCK]
        ends = jnp.where(iota((8, LANES), 1) == b, end, ends)
        lc_t[b] = cum
        dt_t[b] = steps[b]
        tail[b] = spread_columns(jnp.exp(end - cum) * steps[b], wide)
    decay[...] = spread_columns(jnp.exp(ends), wide)[0:8]
    by_block = columns(ends)
    logs[...] = jnp.broadcast_to(
        by_block[0:1] + by_block[1:2] + by_block[2:3] + by_block[3:4], (8, LANES)
    )


def conv(recv, w_inner, w_pairs, bias, rate, steps):
    members, rows, width = recv.shape
    wide, narrow = w_inner.shape[1], w_pairs.shape[1]
    total = members * rows
    shapes = (
        ((total, wide), BF16),
        ((total, narrow), BF16),
        ((4, 8, BLOCK), F32),
        ((4, 8, BLOCK), F32),
        ((4, BLOCK, wide), F32),
        ((8, wide), F32),
        ((8, LANES), F32),
    )
    return pl.pallas_call(
        conv_kernel,
        out_shape=tuple(jax.ShapeDtypeStruct(*s) for s in shapes),
        in_specs=[VMEM] * 9,
        out_specs=(VMEM,) * len(shapes),
        scratch_shapes=[pltpu.VMEM((8 + total, width), F32)],
        compiler_params=PARAMS,
        cost_estimate=cost(20 * total * width, 4 * total * width, 2 * total * width),
        name="conv",
    )(recv, w_inner, w_pairs, bias, rate, *steps)


def state_kernel(
    first,
    halo,
    w_inner,
    w_pairs,
    xc0,
    bc0,
    tail,
    decay,
    logs,
    xc,
    bc,
    states,
    payload,
    ext,
    head_x,
    head_b,
    local,
    sem,
):
    count = first.shape[0]
    total, wide = xc0.shape
    narrow = bc0.shape[1]
    rest = pl.ds(count, total - count)
    copies = [
        pltpu.make_async_copy(xc0.at[rest], xc.at[rest], sem.at[0]),
        pltpu.make_async_copy(bc0.at[rest], bc.at[rest], sem.at[1]),
        pltpu.make_async_copy(head_x, xc.at[pl.ds(0, count)], sem.at[2]),
        pltpu.make_async_copy(head_b, bc.at[pl.ds(0, count)], sem.at[3]),
    ]
    copies[0].start()
    copies[1].start()
    ext[0:8] = halo[count - 8 : count].astype(F32)
    ext[8 : 8 + count] = first[...].astype(F32)
    for start in range(0, wide, LANES):
        cols = slice(start, start + LANES)
        head_x[:, cols] = taps(ext, 0, count, cols, w_inner[:, cols])
    for start in range(0, narrow, LANES):
        head_b[:, start : start + LANES] = taps(
            ext,
            0,
            count,
            slice(wide + start, wide + start + LANES),
            w_pairs[:, start : start + LANES],
        )
    copies[2].start()
    copies[3].start()
    sum_state = jnp.zeros((LANES, wide), F32)
    for b in range(4):
        rows = slice(b * BLOCK, (b + 1) * BLOCK)
        if b == 0:
            block = jnp.concatenate([head_x[...], xc0[count:BLOCK]], axis=0)
            keys = jnp.concatenate([head_b[:, 0:LANES], bc0[count:BLOCK, 0:LANES]], axis=0)
        else:
            block, keys = xc0[rows], bc0[rows, 0:LANES]
        weighted = (block.astype(F32) * tail[b]).astype(BF16)
        one = lax.dot_general(
            keys, weighted, (((0,), (0,)), ((), ())), preferred_element_type=F32
        )
        local[b] = one
        copies.append(pltpu.make_async_copy(local.at[b], states.at[b], sem.at[4 + b]))
        copies[-1].start()
        sum_state = decay[b : b + 1] * sum_state + one
    parts, depth, _ = payload.shape
    payload[:, :, 0:wide] = sum_state.reshape(parts, depth, wide)
    for part in range(parts):
        for row in range(0, depth, 8):
            payload[part, row : row + 8, wide : wide + LANES] = logs[...]
    for copy in copies:
        copy.wait()


def state(first, halo, w_inner, w_pairs, xc0, bc0, tail, decay, logs, parts):
    count, width = first.shape
    total, wide = xc0.shape
    narrow = width - wide
    payload_shape = (parts, LANES // parts, wide + LANES)
    return pl.pallas_call(
        state_kernel,
        out_shape=(
            pltpu.HBM((total, wide), BF16),
            pltpu.HBM((total, narrow), BF16),
            pltpu.HBM((4, LANES, wide), F32),
            jax.ShapeDtypeStruct(payload_shape, F32),
        ),
        in_specs=[VMEM] * 9,
        out_specs=(ANY, ANY, ANY, VMEM),
        scratch_shapes=[
            pltpu.VMEM((8 + count, width), F32),
            pltpu.VMEM((count, wide), BF16),
            pltpu.VMEM((count, narrow), BF16),
            pltpu.VMEM((4, LANES, wide), F32),
            pltpu.SemaphoreType.DMA((8,)),
        ],
        compiler_params=PARAMS,
        cost_estimate=cost(2 * total * wide * LANES, 8 * total * wide),
        name="state",
    )(first, halo, w_inner, w_pairs, xc0, bc0, tail, decay, logs)


def intra_kernel(xc, bc, lc_t, dt_t, skip, own_gate, got_a, got_b, got_c, out, factor):
    x = lax.rem(lax.axis_index("context"), 4)
    wide = out.shape[1]
    heads = lc_t.shape[1]
    scores = lax.dot_general(
        bc[:, LANES:], bc[:, 0:LANES], (((1,), (1,)), ((), ())), preferred_element_type=F32
    )
    half = BLOCK // 2
    lower = iota((half, half), 0) >= iota((half, half), 1)
    own = skip.shape[1]
    gain = widen(
        jnp.broadcast_to(skip[...], (8, own)),
        (iota((own, wide), 1) // 64 + heads * x == iota((own, wide), 0)).astype(F32),
    )[0:1]
    far = lax.rem(x - pl.program_id(0) + 4, 4)
    gate = own_gate[...].astype(F32)
    for distance, got in ((1, got_a), (2, got_b), (3, got_c)):
        gate = jnp.where(far == distance, got[...].astype(F32), gate)
    gate = silu(gate)
    cum = lc_t[0]
    factor[...] = (gate * spread_columns(jnp.exp(cum), wide)).astype(BF16)
    log2e = 1.4426950408889634
    late = cum * log2e
    early = late - jnp.log(dt_t[0]) * log2e
    late = columns(late)
    top = scores[0:half, 0:half]
    left, right = scores[half:, 0:half], scores[half:, half:]
    for pair in range(heads // 2):
        outs = []
        for h in (2 * pair, 2 * pair + 1):
            upper_col, lower_col = late[0:half, h : h + 1], late[half:, h : h + 1]
            first, second = early[h : h + 1, 0:half], early[h : h + 1, half:]
            values = xc[:, h * 64 : (h + 1) * 64]
            w_top = top * jnp.exp2(jnp.where(lower, upper_col - first, -jnp.inf))
            w_left = left * jnp.exp2(lower_col - first)
            w_right = right * jnp.exp2(jnp.where(lower, lower_col - second, -jnp.inf))
            w_low = jnp.concatenate([w_left, w_right], axis=1).astype(BF16)
            outs.append(
                jnp.concatenate(
                    [
                        jnp.dot(w_top.astype(BF16), values[0:half], preferred_element_type=F32),
                        jnp.dot(w_low, values, preferred_element_type=F32),
                    ],
                    axis=0,
                )
            )
        cols = slice(2 * pair * 64, 2 * (pair + 1) * 64)
        mixed = jnp.concatenate(outs, axis=1) + gain[:, cols] * xc[:, cols].astype(F32)
        out[:, cols] = (mixed * gate[:, cols]).astype(BF16)


def intra(xc, bc, lc_t, dt_t, skip, gates):
    total, wide = xc.shape
    narrow = bc.shape[1]
    heads = lc_t.shape[1]
    return pl.pallas_call(
        intra_kernel,
        out_shape=(pltpu.HBM((total, wide), BF16),) * 2,
        grid=(4,),
        in_specs=[
            pl.BlockSpec((BLOCK, wide), lambda b: (b, 0)),
            pl.BlockSpec((BLOCK, narrow), lambda b: (b, 0)),
            pl.BlockSpec((1, heads, BLOCK), lambda b: (b, 0, 0)),
            pl.BlockSpec((1, heads, BLOCK), lambda b: (b, 0, 0)),
            pl.BlockSpec(skip.shape, lambda b: (0, 0)),
        ]
        + [pl.BlockSpec(gate.shape, lambda b: (0, 0)) for gate in gates],
        out_specs=(pl.BlockSpec((BLOCK, wide), lambda b: (b, 0)),) * 2,
        compiler_params=PARAMS,
        cost_estimate=cost(2 * total * BLOCK * wide * 4, 12 * total * wide, heads * total * BLOCK),
        name="intra",
    )(xc, bc, lc_t, dt_t, skip, *gates)


def scan_kernel(recv, out):
    chunks, rows, width = recv.shape
    wide = out.shape[2]
    logs = jnp.concatenate([recv[k, 0:1, wide:width] for k in range(chunks)], axis=0)
    logs = jnp.where(iota(logs.shape, 1) < wide // 64, logs, 0.0)
    decay = widen(jnp.exp(logs), spread(LANES, wide))
    carry = jnp.zeros((rows, wide), F32)
    for k in range(chunks):
        out[k] = carry
        carry = decay[k : k + 1] * carry + recv[k, :, 0:wide]


def scan(recv):
    chunks, rows, width = recv.shape
    return pl.pallas_call(
        scan_kernel,
        out_shape=jax.ShapeDtypeStruct((chunks, rows, width - LANES), F32),
        in_specs=[VMEM],
        out_specs=VMEM,
        compiler_params=PARAMS,
        cost_estimate=cost(4 * chunks * rows * width, 8 * chunks * rows * width),
        name="scan",
    )(recv)


def finish_kernel(carry, states, decay, bc, mixed, factor, out, s_in, c_in, m_in, f_in, sem):
    wide = mixed.shape[1]
    copies = []
    for b in range(4):
        rows = pl.ds(b * BLOCK, BLOCK)
        copies.append(
            [
                pltpu.make_async_copy(bc.at[rows, pl.ds(LANES, LANES)], c_in.at[b], sem.at[b, 0]),
                pltpu.make_async_copy(mixed.at[rows], m_in.at[b], sem.at[b, 1]),
                pltpu.make_async_copy(factor.at[rows], f_in.at[b], sem.at[b, 2]),
                pltpu.make_async_copy(states.at[b], s_in.at[b], sem.at[b, 3]),
            ]
        )
    for group in copies:
        for copy in group:
            copy.start()
    start = carry[...].reshape(LANES, wide)
    for b in range(4):
        for copy in copies[b]:
            copy.wait()
        carried = jnp.dot(c_in[b], start.astype(BF16), preferred_element_type=F32)
        gated = m_in[b].astype(F32) + carried * f_in[b].astype(F32)
        count = BLOCK // out.shape[1]
        out[b * count : (b + 1) * count] = gated.astype(BF16).reshape(count, -1, wide)
        start = decay[b : b + 1] * start + s_in[b]


def finish(carry, states, decay, bc, mixed, factor, rows):
    total, wide = mixed.shape
    return pl.pallas_call(
        finish_kernel,
        out_shape=jax.ShapeDtypeStruct((total // rows, rows, wide), BF16),
        in_specs=[VMEM, ANY, VMEM, ANY, ANY, ANY],
        out_specs=VMEM,
        scratch_shapes=[
            pltpu.VMEM((4, LANES, wide), F32),
            pltpu.VMEM((4, BLOCK, LANES), BF16),
            pltpu.VMEM((4, BLOCK, wide), BF16),
            pltpu.VMEM((4, BLOCK, wide), BF16),
            pltpu.SemaphoreType.DMA((4, 4)),
        ],
        compiler_params=PARAMS,
        cost_estimate=cost(2 * total * wide * 200, 6 * total * wide),
        name="finish",
    )(carry, keep(states), decay, keep(bc), keep(mixed), keep(factor))


def post_kernel(slabs, own_gain, got_a, got_b, got_c, out):
    wide = slabs.shape[2]
    for y in range(4):
        far = lax.rem(lax.axis_index("head") - y + 4, 4)
        gain = own_gain[...]
        for distance, got in ((1, got_a), (2, got_b), (3, got_c)):
            gain = jnp.where(far == distance, got[...], gain)
        for half in range(2):
            left, right = 8 * half + y, 8 * half + 4 + y
            a, b = slabs[left].astype(F32), slabs[right].astype(F32)
            mean = (
                jnp.sum(a * a, axis=1, keepdims=True) + jnp.sum(b * b, axis=1, keepdims=True)
            ) / (2 * wide)
            inv = lax.rsqrt(mean + 1e-5)
            at = 2 * half * wide
            low, high = gain[:, at : at + wide], gain[:, at + wide : at + 2 * wide]
            at = at + 4 * y * wide
            out[:, at : at + wide] = (a * inv * low).astype(BF16)
            out[:, at + wide : at + 2 * wide] = (b * inv * high).astype(BF16)


def post(slabs, gains):
    members, rows, wide = slabs.shape
    return pl.pallas_call(
        post_kernel,
        out_shape=jax.ShapeDtypeStruct((rows, members * wide), BF16),
        in_specs=[VMEM] * 5,
        out_specs=VMEM,
        compiler_params=PARAMS,
        cost_estimate=cost(6 * members * rows * wide, 4 * members * rows * wide),
        name="post",
    )(slabs, *gains)


def on_device(
    inner_raw,
    pairs_raw,
    gate_raw,
    step_raw,
    step_bias,
    rate_log,
    skip_gain,
    conv_inner,
    conv_pairs,
    norm_gain,
):
    places = lax.axis_size("context")
    shards = lax.axis_size("head")
    chunks = places // 4
    x = (lax.axis_index("context") % 4).astype(jnp.int32)
    rows = inner_raw.shape[0]
    after = [(c, c + 4) for c in range(places - 4)]
    teams = [list(range(TEAM * k, TEAM * (k + 1))) for k in range(places * shards // TEAM)]
    lines = [[4 * k + s for k in range(chunks)] for s in range(4)]

    def around(axis, position, pick):
        count = lax.axis_size(axis)
        routes = [[(c, c - c % 4 + (c + far) % 4) for c in range(count)] for far in (1, 2, 3)]
        return [
            lax.ppermute(pick((position + far) % 4), axis, route)
            for far, route in zip((1, 2, 3), routes)
        ]

    packed = pack(inner_raw, pairs_raw.reshape(rows, -1))
    step_rows = step_raw.T
    gain_row = norm_gain.reshape(1, -1)
    gate_later, steps_later, gain_later, w_inner, w_pairs, packed = lax.optimization_barrier(
        (gate_raw, step_rows, gain_row, conv_inner, conv_pairs, packed)
    )
    recv = lax.all_to_all(
        packed, ("context", "head"), split_axis=0, concat_axis=0, axis_index_groups=teams
    )
    width = gate_raw.shape[1] // 4
    y = lax.axis_index("head").astype(jnp.int32)
    steps = around("context", x, lambda p: lax.dynamic_slice_in_dim(steps_later, 8 * p, 8, 0))
    gains = around("head", y, lambda p: gain_later)
    gates = around(
        "context", x, lambda p: lax.dynamic_slice_in_dim(gate_later, p * width, width, 1)
    )
    *steps, recv = lax.optimization_barrier((*steps, recv))
    halo = lax.ppermute(recv[TEAM - 1, rows - 16 : rows], "context", after)

    own_steps = lax.dynamic_slice_in_dim(steps_later, 8 * x, 8, 0)
    own_gate = lax.dynamic_slice_in_dim(gate_later, x * width, width, 1)
    w_pairs = w_pairs.reshape(w_pairs.shape[0], -1)
    wide, narrow = w_inner.shape[1] // TEAM, w_pairs.shape[1] // 8
    w_inner = lax.dynamic_slice_in_dim(w_inner, (4 * y + x) * wide, wide, 1)
    w_pairs = lax.dynamic_slice_in_dim(w_pairs, (2 * y + x // 2) * narrow, narrow, 1)
    xc0, bc0, lc_t, dt_t, tail, decay, logs = conv(
        recv,
        w_inner,
        w_pairs,
        step_bias.reshape(1, -1),
        rate_log.reshape(1, -1),
        [own_steps] + steps,
    )
    xc, bc, states, payload = state(
        recv[0, :16], halo, w_inner, w_pairs, xc0, bc0, tail, decay, logs, chunks
    )
    gates[0], gates[1], payload = lax.optimization_barrier((gates[0], gates[1], payload))
    totals = lax.all_to_all(
        payload, "context", split_axis=0, concat_axis=0, axis_index_groups=lines
    )
    gates[2], *gains, totals = lax.optimization_barrier((gates[2], *gains, totals))
    carry = lax.all_to_all(
        scan(totals), "context", split_axis=0, concat_axis=0, axis_index_groups=lines
    )
    mixed, factor = intra(xc, bc, lc_t, dt_t, skip_gain.reshape(1, -1), [own_gate] + gates)
    slabs = finish(carry, states, decay, bc, mixed, factor, rows)
    slabs = lax.all_to_all(
        slabs, ("context", "head"), split_axis=0, concat_axis=0, axis_index_groups=teams
    )
    return post(slabs, [gain_row] + gains)


def solution(mesh):
    placed = (
        P(("rollout", "context", "head"), None),
        P(("rollout", "context", "head"), None, None, None),
        P(("rollout", "context"), "head"),
        P(("rollout", "context"), "head"),
        P("head"),
        P("head"),
        P("head"),
        P(),
        P(),
        P("head"),
    )
    return jax.shard_map(
        on_device,
        mesh=mesh,
        in_specs=placed,
        out_specs=P(("rollout", "context", "head"), None),
        check_vma=False,
    )
```

```python
import functools

import jax
import jax.numpy as jnp
from jax import lax
from jax.experimental import pallas as pl
from jax.experimental.pallas import tpu as pltpu
from jax.sharding import PartitionSpec as P

BLOCK = 256
HIGH = lax.Precision.HIGHEST
F32 = jnp.float32
BF16 = jnp.bfloat16
LANES = 128
ANY = pl.BlockSpec(memory_space=pl.ANY)
VMEM = pl.BlockSpec(memory_space=pltpu.VMEM)
HBM = pl.BlockSpec(memory_space=pltpu.HBM)
PARAMS = pltpu.CompilerParams(vmem_limit_bytes=24 * 1024 * 1024)
LARGE = pltpu.CompilerParams(vmem_limit_bytes=56 * 1024 * 1024)
TEAM = 16


def cost(flops, bytes_accessed, transcendentals=0):
    return pl.CostEstimate(
        flops=flops, bytes_accessed=bytes_accessed, transcendentals=transcendentals
    )


def keep(array):
    return pltpu.with_memory_space_constraint(array, pltpu.HBM)


def iota(shape, dim):
    return lax.broadcasted_iota(jnp.int32, shape, dim)


def spread(rows, channels):
    return (iota((rows, channels), 1) // 64 == iota((rows, channels), 0)).astype(F32)


def widen(value, one_hot):
    return jnp.dot(value, one_hot, precision=HIGH, preferred_element_type=F32)


def columns(value):
    padding = jnp.zeros((LANES - value.shape[0], value.shape[1]), F32)
    return jnp.concatenate([value, padding], axis=0).T


def split(value):
    top = value.astype(BF16).astype(F32)
    mid = (value - top).astype(BF16).astype(F32)
    return [top, mid, value - top - mid]


def spread_columns(value, channels):
    padding = jnp.zeros((LANES - 24, value.shape[1]), F32)
    left = jnp.concatenate(split(value) + [padding], axis=0).T.astype(BF16)
    row = iota((LANES, channels), 0)
    one_hot = (row % 8 == iota((LANES, channels), 1) // 64) & (row < 24)
    return jnp.dot(left, one_hot.astype(BF16), preferred_element_type=F32)


def silu(v):
    half = 0.5 * v
    return half + half * jnp.tanh(half)


def pack_kernel(
    inner, pairs, out, staged, local, flat, stage_sem, sem, pairs_sem, local_sem
):
    rows, full = inner.shape
    wide, narrow = full // TEAM, 2 * pairs.shape[3]
    stages, copies, more = [], [], []
    for member in range(TEAM):
        px, py = member // 4, member % 4
        part = pl.ds((4 * py + px) * wide, wide)
        stages.append(
            pltpu.make_async_copy(inner.at[:, part], staged.at[:, part], stage_sem.at[member])
        )
        copies.append(
            pltpu.make_async_copy(
                staged.at[:, part], out.at[member, pl.ds(0, rows), pl.ds(0, wide)], sem.at[member]
            )
        )
        more.append(
            pltpu.make_async_copy(
                flat.at[:, pl.ds((2 * py + px // 2) * narrow, narrow)],
                out.at[member, pl.ds(0, rows), pl.ds(wide, narrow)],
                pairs_sem.at[member],
            )
        )
    fetch = pltpu.make_async_copy(pairs, local, local_sem)
    fetch.start()
    for copy in stages:
        copy.start()
    fetch.wait()
    half = pairs.shape[3]
    for group in range(pairs.shape[1]):
        both = local[:, group].astype(F32)
        for k in range(2):
            at = group * narrow + k * half
            flat[:, at : at + half] = both[:, k].astype(BF16)
    for copy in more:
        copy.start()
    for stage, copy in zip(stages, copies):
        stage.wait()
        copy.start()
    for copy in copies + more:
        copy.wait()


def pack(inner, pairs):
    rows = inner.shape[0]
    width = inner.shape[1] // TEAM + 2 * pairs.shape[3]
    return pl.pallas_call(
        pack_kernel,
        out_shape=jax.ShapeDtypeStruct((TEAM, rows, width), BF16),
        in_specs=[ANY, ANY],
        out_specs=ANY,
        scratch_shapes=[
            pltpu.VMEM(inner.shape, BF16),
            pltpu.VMEM(pairs.shape, BF16),
            pltpu.VMEM((rows, pairs.shape[1] * 2 * pairs.shape[3]), BF16),
            pltpu.SemaphoreType.DMA((TEAM,)),
            pltpu.SemaphoreType.DMA((TEAM,)),
            pltpu.SemaphoreType.DMA((TEAM,)),
            pltpu.SemaphoreType.DMA,
        ],
        compiler_params=PARAMS,
        cost_estimate=cost(0, 4 * TEAM * rows * width),
        name="pack",
    )(keep(inner), keep(pairs))


def taps(ext, row, rows, cols, weight):
    window = ext[pl.ds(row, rows + 8), cols]
    total = weight[4:5] + weight[0:1] * window[4 : 4 + rows]
    for k in range(1, 4):
        total = total + weight[k : k + 1] * window[4 + k : 4 + k + rows]
    return silu(total).astype(BF16)


def conv_kernel(
    recv,
    w_inner,
    w_pairs,
    bias,
    rate,
    own_steps,
    got_a,
    got_b,
    got_c,
    xc,
    bc,
    lc_t,
    dt_t,
    tail,
    decay,
    logs,
    ext,
):
    x = lax.rem(lax.axis_index("context"), 4)
    members, rows, width = recv.shape
    wide = xc.shape[1]
    ext[0:8] = jnp.zeros((8, width), F32)
    for m in range(members):
        ext[8 + m * rows : 8 + (m + 1) * rows] = recv[m].astype(F32)

    def chunk(m, _):
        row = pl.multiple_of(m * rows, rows)
        for start in range(0, wide, LANES):
            cols = slice(start, start + LANES)
            xc[pl.ds(row, rows), cols] = taps(ext, row, rows, cols, w_inner[:, cols])
        for start in range(0, width - wide, LANES):
            bc[pl.ds(row, rows), start : start + LANES] = taps(
                ext,
                row,
                rows,
                slice(wide + start, wide + start + LANES),
                w_pairs[:, start : start + LANES],
            )
        return 0

    lax.fori_loop(0, members, chunk, 0)

    own = bias.shape[1]
    mine = iota((8, own), 1) == 8 * x + iota((8, own), 0)
    shift = jnp.sum(jnp.where(mine, bias[...], 0.0), axis=1, keepdims=True)
    speed = jnp.sum(jnp.where(mine, -jnp.exp(rate[...]), 0.0), axis=1, keepdims=True)
    upper = (iota((BLOCK, BLOCK), 0) <= iota((BLOCK, BLOCK), 1)).astype(BF16)
    steps = []
    for b in range(4):
        far = lax.rem(x - b + 4, 4)
        v = own_steps[...].astype(F32)
        for distance, got in ((1, got_a), (2, got_b), (3, got_c)):
            v = jnp.where(far == distance, got[...].astype(F32), v)
        v = v + shift
        steps.append(jnp.maximum(v, 0.0) + jnp.log1p(jnp.exp(-jnp.abs(v))))
    parts = split(jnp.concatenate([step * speed for step in steps], axis=0))
    parts = jnp.concatenate(parts, axis=0).astype(BF16)
    sums = jnp.dot(parts, upper, preferred_element_type=F32)
    ends = jnp.zeros((8, LANES), F32)
    for b in range(4):
        cum = sums[8 * b : 8 * b + 8] + sums[8 * b + 32 : 8 * b + 40] + sums[8 * b + 64 : 8 * b + 72]
        end = cum[:, BLOCK - 1 : BLOCK]
        ends = jnp.where(iota((8, LANES), 1) == b, end, ends)
        lc_t[b] = cum
        dt_t[b] = steps[b]
        tail[b] = spread_columns(jnp.exp(end - cum) * steps[b], wide)
    decay[...] = spread_columns(jnp.exp(ends), wide)[0:8]
    by_block = columns(ends)
    logs[...] = jnp.broadcast_to(
        by_block[0:1] + by_block[1:2] + by_block[2:3] + by_block[3:4], (8, LANES)
    )


def conv(recv, w_inner, w_pairs, bias, rate, steps):
    members, rows, width = recv.shape
    wide, narrow = w_inner.shape[1], w_pairs.shape[1]
    total = members * rows
    shapes = (
        ((total, wide), BF16),
        ((total, narrow), BF16),
        ((4, 8, BLOCK), F32),
        ((4, 8, BLOCK), F32),
        ((4, BLOCK, wide), F32),
        ((8, wide), F32),
        ((8, LANES), F32),
    )
    return pl.pallas_call(
        conv_kernel,
        out_shape=tuple(jax.ShapeDtypeStruct(*s) for s in shapes),
        in_specs=[VMEM] * 9,
        out_specs=(VMEM,) * len(shapes),
        scratch_shapes=[pltpu.VMEM((8 + total, width), F32)],
        compiler_params=PARAMS,
        cost_estimate=cost(20 * total * width, 4 * total * width, 2 * total * width),
        name="conv",
    )(recv, w_inner, w_pairs, bias, rate, *steps)


def state_kernel(
    first,
    halo,
    w_inner,
    w_pairs,
    xc0,
    bc0,
    tail,
    decay,
    logs,
    xc,
    bc,
    states,
    payload,
    ext,
    head_x,
    head_b,
    local,
    sem,
):
    count = first.shape[0]
    total, wide = xc0.shape
    narrow = bc0.shape[1]
    rest = pl.ds(count, total - count)
    copies = [
        pltpu.make_async_copy(xc0.at[rest], xc.at[rest], sem.at[0]),
        pltpu.make_async_copy(bc0.at[rest], bc.at[rest], sem.at[1]),
        pltpu.make_async_copy(head_x, xc.at[pl.ds(0, count)], sem.at[2]),
        pltpu.make_async_copy(head_b, bc.at[pl.ds(0, count)], sem.at[3]),
    ]
    copies[0].start()
    copies[1].start()
    ext[0:8] = halo[count - 8 : count].astype(F32)
    ext[8 : 8 + count] = first[...].astype(F32)
    for start in range(0, wide, LANES):
        cols = slice(start, start + LANES)
        head_x[:, cols] = taps(ext, 0, count, cols, w_inner[:, cols])
    for start in range(0, narrow, LANES):
        head_b[:, start : start + LANES] = taps(
            ext,
            0,
            count,
            slice(wide + start, wide + start + LANES),
            w_pairs[:, start : start + LANES],
        )
    copies[2].start()
    copies[3].start()
    sum_state = jnp.zeros((LANES, wide), F32)
    for b in range(4):
        rows = slice(b * BLOCK, (b + 1) * BLOCK)
        if b == 0:
            block = jnp.concatenate([head_x[...], xc0[count:BLOCK]], axis=0)
            keys = jnp.concatenate([head_b[:, 0:LANES], bc0[count:BLOCK, 0:LANES]], axis=0)
        else:
            block, keys = xc0[rows], bc0[rows, 0:LANES]
        weighted = (block.astype(F32) * tail[b]).astype(BF16)
        one = lax.dot_general(
            keys, weighted, (((0,), (0,)), ((), ())), preferred_element_type=F32
        )
        local[b] = one
        copies.append(pltpu.make_async_copy(local.at[b], states.at[b], sem.at[4 + b]))
        copies[-1].start()
        sum_state = decay[b : b + 1] * sum_state + one
    parts, depth, _ = payload.shape
    payload[:, :, 0:wide] = sum_state.reshape(parts, depth, wide)
    for part in range(parts):
        for row in range(0, depth, 8):
            payload[part, row : row + 8, wide : wide + LANES] = logs[...]
    for copy in copies:
        copy.wait()


def state(first, halo, w_inner, w_pairs, xc0, bc0, tail, decay, logs, parts):
    count, width = first.shape
    total, wide = xc0.shape
    narrow = width - wide
    payload_shape = (parts, LANES // parts, wide + LANES)
    return pl.pallas_call(
        state_kernel,
        out_shape=(
            pltpu.HBM((total, wide), BF16),
            pltpu.HBM((total, narrow), BF16),
            pltpu.HBM((4, LANES, wide), F32),
            jax.ShapeDtypeStruct(payload_shape, F32),
        ),
        in_specs=[VMEM] * 9,
        out_specs=(ANY, ANY, ANY, VMEM),
        scratch_shapes=[
            pltpu.VMEM((8 + count, width), F32),
            pltpu.VMEM((count, wide), BF16),
            pltpu.VMEM((count, narrow), BF16),
            pltpu.VMEM((4, LANES, wide), F32),
            pltpu.SemaphoreType.DMA((8,)),
        ],
        compiler_params=PARAMS,
        cost_estimate=cost(2 * total * wide * LANES, 8 * total * wide),
        name="state",
    )(first, halo, w_inner, w_pairs, xc0, bc0, tail, decay, logs)


def intra_kernel(xc, bc, lc_t, dt_t, skip, own_gate, got_a, got_b, got_c, out, factor):
    x = lax.rem(lax.axis_index("context"), 4)
    wide = out.shape[1]
    heads = lc_t.shape[1]
    scores = lax.dot_general(
        bc[:, LANES:], bc[:, 0:LANES], (((1,), (1,)), ((), ())), preferred_element_type=F32
    )
    half = BLOCK // 2
    lower = iota((half, half), 0) >= iota((half, half), 1)
    own = skip.shape[1]
    gain = widen(
        jnp.broadcast_to(skip[...], (8, own)),
        (iota((own, wide), 1) // 64 + heads * x == iota((own, wide), 0)).astype(F32),
    )[0:1]
    far = lax.rem(x - pl.program_id(0) + 4, 4)
    gate = own_gate[...].astype(F32)
    for distance, got in ((1, got_a), (2, got_b), (3, got_c)):
        gate = jnp.where(far == distance, got[...].astype(F32), gate)
    gate = silu(gate)
    cum = lc_t[0]
    factor[...] = (gate * spread_columns(jnp.exp(cum), wide)).astype(BF16)
    log2e = 1.4426950408889634
    late = cum * log2e
    early = late - jnp.log(dt_t[0]) * log2e
    late = columns(late)
    top = scores[0:half, 0:half]
    left, right = scores[half:, 0:half], scores[half:, half:]
    for pair in range(heads // 2):
        outs = []
        for h in (2 * pair, 2 * pair + 1):
            upper_col, lower_col = late[0:half, h : h + 1], late[half:, h : h + 1]
            first, second = early[h : h + 1, 0:half], early[h : h + 1, half:]
            values = xc[:, h * 64 : (h + 1) * 64]
            w_top = top * jnp.exp2(jnp.where(lower, upper_col - first, -jnp.inf))
            w_left = left * jnp.exp2(lower_col - first)
            w_right = right * jnp.exp2(jnp.where(lower, lower_col - second, -jnp.inf))
            w_low = jnp.concatenate([w_left, w_right], axis=1).astype(BF16)
            outs.append(
                jnp.concatenate(
                    [
                        jnp.dot(w_top.astype(BF16), values[0:half], preferred_element_type=F32),
                        jnp.dot(w_low, values, preferred_element_type=F32),
                    ],
                    axis=0,
                )
            )
        cols = slice(2 * pair * 64, 2 * (pair + 1) * 64)
        mixed = jnp.concatenate(outs, axis=1) + gain[:, cols] * xc[:, cols].astype(F32)
        out[:, cols] = (mixed * gate[:, cols]).astype(BF16)


def intra(xc, bc, lc_t, dt_t, skip, gates):
    total, wide = xc.shape
    narrow = bc.shape[1]
    heads = lc_t.shape[1]
    return pl.pallas_call(
        intra_kernel,
        out_shape=(jax.ShapeDtypeStruct((total, wide), BF16),) * 2,
        grid=(4,),
        in_specs=[
            pl.BlockSpec((BLOCK, wide), lambda b: (b, 0)),
            pl.BlockSpec((BLOCK, narrow), lambda b: (b, 0)),
            pl.BlockSpec((1, heads, BLOCK), lambda b: (b, 0, 0)),
            pl.BlockSpec((1, heads, BLOCK), lambda b: (b, 0, 0)),
            pl.BlockSpec(skip.shape, lambda b: (0, 0)),
        ]
        + [pl.BlockSpec(gate.shape, lambda b: (0, 0)) for gate in gates],
        out_specs=(pl.BlockSpec((BLOCK, wide), lambda b: (b, 0)),) * 2,
        compiler_params=PARAMS,
        cost_estimate=cost(2 * total * BLOCK * wide * 4, 12 * total * wide, heads * total * BLOCK),
        name="intra",
    )(keep(xc), keep(bc), lc_t, dt_t, skip, *[keep(gate) for gate in gates])


def scan_kernel(recv, out):
    chunks, rows, width = recv.shape
    wide = out.shape[2]
    logs = jnp.concatenate([recv[k, 0:1, wide:width] for k in range(chunks)], axis=0)
    logs = jnp.where(iota(logs.shape, 1) < wide // 64, logs, 0.0)
    decay = widen(jnp.exp(logs), spread(LANES, wide))
    carry = jnp.zeros((rows, wide), F32)
    for k in range(chunks):
        out[k] = carry
        carry = decay[k : k + 1] * carry + recv[k, :, 0:wide]


def scan(recv):
    chunks, rows, width = recv.shape
    return pl.pallas_call(
        scan_kernel,
        out_shape=jax.ShapeDtypeStruct((chunks, rows, width - LANES), F32),
        in_specs=[VMEM],
        out_specs=VMEM,
        compiler_params=PARAMS,
        cost_estimate=cost(4 * chunks * rows * width, 8 * chunks * rows * width),
        name="scan",
    )(recv)


def finish_kernel(carry, states, decay, bc, mixed, factor, out, s_in, c_in, sem):
    wide = mixed.shape[1]
    copies = []
    for b in range(4):
        rows = pl.ds(b * BLOCK, BLOCK)
        copies.append(
            [
                pltpu.make_async_copy(bc.at[rows, pl.ds(LANES, LANES)], c_in.at[b], sem.at[b, 0]),
                pltpu.make_async_copy(states.at[b], s_in.at[b], sem.at[b, 1]),
            ]
        )
    for group in copies:
        for copy in group:
            copy.start()
    start = carry[...].reshape(LANES, wide)
    for b in range(4):
        for copy in copies[b]:
            copy.wait()
        carried = jnp.dot(c_in[b], start.astype(BF16), preferred_element_type=F32)
        rows = slice(b * BLOCK, (b + 1) * BLOCK)
        gated = mixed[rows].astype(F32) + carried * factor[rows].astype(F32)
        count = BLOCK // out.shape[1]
        out[b * count : (b + 1) * count] = gated.astype(BF16).reshape(count, -1, wide)
        start = decay[b : b + 1] * start + s_in[b]


def finish(carry, states, decay, bc, mixed, factor, rows):
    total, wide = mixed.shape
    return pl.pallas_call(
        finish_kernel,
        out_shape=jax.ShapeDtypeStruct((total // rows, rows, wide), BF16),
        in_specs=[VMEM, ANY, VMEM, ANY, VMEM, VMEM],
        out_specs=VMEM,
        scratch_shapes=[
            pltpu.VMEM((4, LANES, wide), F32),
            pltpu.VMEM((4, BLOCK, LANES), BF16),
            pltpu.SemaphoreType.DMA((4, 2)),
        ],
        compiler_params=PARAMS,
        cost_estimate=cost(2 * total * wide * 200, 6 * total * wide),
        name="finish",
    )(carry, keep(states), decay, keep(bc), mixed, factor)


def post_kernel(slabs, own_gain, got_a, got_b, got_c, out):
    wide = slabs.shape[2]
    for y in range(4):
        far = lax.rem(lax.axis_index("head") - y + 4, 4)
        gain = own_gain[...]
        for distance, got in ((1, got_a), (2, got_b), (3, got_c)):
            gain = jnp.where(far == distance, got[...], gain)
        for half in range(2):
            left, right = 8 * half + y, 8 * half + 4 + y
            a, b = slabs[left].astype(F32), slabs[right].astype(F32)
            mean = (
                jnp.sum(a * a, axis=1, keepdims=True) + jnp.sum(b * b, axis=1, keepdims=True)
            ) / (2 * wide)
            inv = lax.rsqrt(mean + 1e-5)
            at = 2 * half * wide
            low, high = gain[:, at : at + wide], gain[:, at + wide : at + 2 * wide]
            at = at + 4 * y * wide
            out[:, at : at + wide] = (a * inv * low).astype(BF16)
            out[:, at + wide : at + 2 * wide] = (b * inv * high).astype(BF16)


def post(slabs, gains):
    members, rows, wide = slabs.shape
    return pl.pallas_call(
        post_kernel,
        out_shape=jax.ShapeDtypeStruct((rows, members * wide), BF16),
        in_specs=[VMEM] * 5,
        out_specs=VMEM,
        compiler_params=PARAMS,
        cost_estimate=cost(6 * members * rows * wide, 4 * members * rows * wide),
        name="post",
    )(slabs, *gains)


def on_device(
    inner_raw,
    pairs_raw,
    gate_raw,
    step_raw,
    step_bias,
    rate_log,
    skip_gain,
    conv_inner,
    conv_pairs,
    norm_gain,
):
    places = lax.axis_size("context")
    shards = lax.axis_size("head")
    chunks = places // 4
    x = (lax.axis_index("context") % 4).astype(jnp.int32)
    rows = inner_raw.shape[0]
    after = [(c, c + 4) for c in range(places - 4)]
    teams = [list(range(TEAM * k, TEAM * (k + 1))) for k in range(places * shards // TEAM)]
    lines = [[4 * k + s for k in range(chunks)] for s in range(4)]

    def around(axis, position, pick):
        count = lax.axis_size(axis)
        routes = [[(c, c - c % 4 + (c + far) % 4) for c in range(count)] for far in (1, 2, 3)]
        return [
            lax.ppermute(pick((position + far) % 4), axis, route)
            for far, route in zip((1, 2, 3), routes)
        ]

    packed = pack(inner_raw, pairs_raw)
    step_rows = step_raw.T
    gain_row = norm_gain.reshape(1, -1)
    gate_later, steps_later, gain_later, w_inner, w_pairs, packed = lax.optimization_barrier(
        (gate_raw, step_rows, gain_row, conv_inner, conv_pairs, packed)
    )
    recv = lax.all_to_all(
        packed, ("context", "head"), split_axis=0, concat_axis=0, axis_index_groups=teams
    )
    width = gate_raw.shape[1] // 4
    y = lax.axis_index("head").astype(jnp.int32)
    steps = around("context", x, lambda p: lax.dynamic_slice_in_dim(steps_later, 8 * p, 8, 0))
    gains = around("head", y, lambda p: gain_later)
    gates = around(
        "context", x, lambda p: lax.dynamic_slice_in_dim(gate_later, p * width, width, 1)
    )
    *steps, recv = lax.optimization_barrier((*steps, recv))
    halo = lax.ppermute(recv[TEAM - 1, rows - 16 : rows], "context", after)

    own_steps = lax.dynamic_slice_in_dim(steps_later, 8 * x, 8, 0)
    own_gate = lax.dynamic_slice_in_dim(gate_later, x * width, width, 1)
    w_pairs = w_pairs.reshape(w_pairs.shape[0], -1)
    wide, narrow = w_inner.shape[1] // TEAM, w_pairs.shape[1] // 8
    w_inner = lax.dynamic_slice_in_dim(w_inner, (4 * y + x) * wide, wide, 1)
    w_pairs = lax.dynamic_slice_in_dim(w_pairs, (2 * y + x // 2) * narrow, narrow, 1)
    xc0, bc0, lc_t, dt_t, tail, decay, logs = conv(
        recv,
        w_inner,
        w_pairs,
        step_bias.reshape(1, -1),
        rate_log.reshape(1, -1),
        [own_steps] + steps,
    )
    xc, bc, states, payload = state(
        recv[0, :16], halo, w_inner, w_pairs, xc0, bc0, tail, decay, logs, chunks
    )
    gates[0], gates[1], payload = lax.optimization_barrier((gates[0], gates[1], payload))
    totals = lax.all_to_all(
        payload, "context", split_axis=0, concat_axis=0, axis_index_groups=lines
    )
    gates[2], *gains, totals = lax.optimization_barrier((gates[2], *gains, totals))
    carry = lax.all_to_all(
        scan(totals), "context", split_axis=0, concat_axis=0, axis_index_groups=lines
    )
    mixed, factor = intra(xc, bc, lc_t, dt_t, skip_gain.reshape(1, -1), [own_gate] + gates)
    slabs = finish(carry, states, decay, bc, mixed, factor, rows)
    slabs = lax.all_to_all(
        slabs, ("context", "head"), split_axis=0, concat_axis=0, axis_index_groups=teams
    )
    return post(slabs, [gain_row] + gains)


def solution(mesh):
    placed = (
        P(("rollout", "context", "head"), None),
        P(("rollout", "context", "head"), None, None, None),
        P(("rollout", "context"), "head"),
        P(("rollout", "context"), "head"),
        P("head"),
        P("head"),
        P("head"),
        P(),
        P(),
        P("head"),
    )
    return jax.shard_map(
        on_device,
        mesh=mesh,
        in_specs=placed,
        out_specs=P(("rollout", "context", "head"), None),
        check_vma=False,
    )
```

```python
import functools

import jax
import jax.numpy as jnp
from jax import lax
from jax.experimental import pallas as pl
from jax.experimental.pallas import tpu as pltpu
from jax.sharding import PartitionSpec as P

BLOCK = 256
HIGH = lax.Precision.HIGHEST
F32 = jnp.float32
BF16 = jnp.bfloat16
LANES = 128
ANY = pl.BlockSpec(memory_space=pl.ANY)
VMEM = pl.BlockSpec(memory_space=pltpu.VMEM)
HBM = pl.BlockSpec(memory_space=pltpu.HBM)
PARAMS = pltpu.CompilerParams(vmem_limit_bytes=24 * 1024 * 1024)
LARGE = pltpu.CompilerParams(vmem_limit_bytes=56 * 1024 * 1024)
TEAM = 16


def cost(flops, bytes_accessed, transcendentals=0):
    return pl.CostEstimate(
        flops=flops, bytes_accessed=bytes_accessed, transcendentals=transcendentals
    )


def keep(array):
    return pltpu.with_memory_space_constraint(array, pltpu.HBM)


def iota(shape, dim):
    return lax.broadcasted_iota(jnp.int32, shape, dim)


def spread(rows, channels):
    return (iota((rows, channels), 1) // 64 == iota((rows, channels), 0)).astype(F32)


def widen(value, one_hot):
    return jnp.dot(value, one_hot, precision=HIGH, preferred_element_type=F32)


def columns(value):
    padding = jnp.zeros((LANES - value.shape[0], value.shape[1]), F32)
    return jnp.concatenate([value, padding], axis=0).T


def split(value):
    top = value.astype(BF16).astype(F32)
    mid = (value - top).astype(BF16).astype(F32)
    return [top, mid, value - top - mid]


def spread_columns(value, channels):
    padding = jnp.zeros((LANES - 24, value.shape[1]), F32)
    left = jnp.concatenate(split(value) + [padding], axis=0).T.astype(BF16)
    row = iota((LANES, channels), 0)
    one_hot = (row % 8 == iota((LANES, channels), 1) // 64) & (row < 24)
    return jnp.dot(left, one_hot.astype(BF16), preferred_element_type=F32)


def silu(v):
    half = 0.5 * v
    return half + half * jnp.tanh(half)


def pack_kernel(
    inner, pairs, out, staged, local, flat, stage_sem, sem, pairs_sem, local_sem
):
    rows, full = inner.shape
    wide, narrow = full // TEAM, 2 * pairs.shape[3]
    stages, copies, more = [], [], []
    for member in range(TEAM):
        px, py = member // 4, member % 4
        part = pl.ds((4 * py + px) * wide, wide)
        stages.append(
            pltpu.make_async_copy(inner.at[:, part], staged.at[:, part], stage_sem.at[member])
        )
        copies.append(
            pltpu.make_async_copy(
                staged.at[:, part], out.at[member, pl.ds(0, rows), pl.ds(0, wide)], sem.at[member]
            )
        )
        more.append(
            pltpu.make_async_copy(
                flat.at[:, pl.ds((2 * py + px // 2) * narrow, narrow)],
                out.at[member, pl.ds(0, rows), pl.ds(wide, narrow)],
                pairs_sem.at[member],
            )
        )
    fetch = pltpu.make_async_copy(pairs, local, local_sem)
    fetch.start()
    for copy in stages:
        copy.start()
    fetch.wait()
    half = pairs.shape[3]
    for group in range(pairs.shape[1]):
        both = local[:, group].astype(F32)
        for k in range(2):
            at = group * narrow + k * half
            flat[:, at : at + half] = both[:, k].astype(BF16)
    for copy in more:
        copy.start()
    for stage, copy in zip(stages, copies):
        stage.wait()
        copy.start()
    for copy in copies + more:
        copy.wait()


def pack(inner, pairs):
    rows = inner.shape[0]
    width = inner.shape[1] // TEAM + 2 * pairs.shape[3]
    return pl.pallas_call(
        pack_kernel,
        out_shape=jax.ShapeDtypeStruct((TEAM, rows, width), BF16),
        in_specs=[ANY, ANY],
        out_specs=ANY,
        scratch_shapes=[
            pltpu.VMEM(inner.shape, BF16),
            pltpu.VMEM(pairs.shape, BF16),
            pltpu.VMEM((rows, pairs.shape[1] * 2 * pairs.shape[3]), BF16),
            pltpu.SemaphoreType.DMA((TEAM,)),
            pltpu.SemaphoreType.DMA((TEAM,)),
            pltpu.SemaphoreType.DMA((TEAM,)),
            pltpu.SemaphoreType.DMA,
        ],
        compiler_params=PARAMS,
        cost_estimate=cost(0, 4 * TEAM * rows * width),
        name="pack",
    )(keep(inner), keep(pairs))


def taps(ext, row, rows, cols, weight):
    window = ext[pl.ds(row, rows + 8), cols]
    total = weight[4:5] + weight[0:1] * window[4 : 4 + rows]
    for k in range(1, 4):
        total = total + weight[k : k + 1] * window[4 + k : 4 + k + rows]
    return silu(total).astype(BF16)


def conv_kernel(
    recv,
    w_inner,
    w_pairs,
    bias,
    rate,
    own_steps,
    got_a,
    got_b,
    got_c,
    xc,
    bc,
    lc_t,
    dt_t,
    tail,
    decay,
    logs,
    ext,
):
    x = lax.rem(lax.axis_index("context"), 4)
    members, rows, width = recv.shape
    wide = xc.shape[1]
    ext[0:8] = jnp.zeros((8, width), F32)
    for m in range(members):
        ext[8 + m * rows : 8 + (m + 1) * rows] = recv[m].astype(F32)

    def chunk(m, _):
        row = pl.multiple_of(m * rows, rows)
        for start in range(0, wide, LANES):
            cols = slice(start, start + LANES)
            xc[pl.ds(row, rows), cols] = taps(ext, row, rows, cols, w_inner[:, cols])
        for start in range(0, width - wide, LANES):
            bc[pl.ds(row, rows), start : start + LANES] = taps(
                ext,
                row,
                rows,
                slice(wide + start, wide + start + LANES),
                w_pairs[:, start : start + LANES],
            )
        return 0

    lax.fori_loop(0, members, chunk, 0)

    own = bias.shape[1]
    mine = iota((8, own), 1) == 8 * x + iota((8, own), 0)
    shift = jnp.sum(jnp.where(mine, bias[...], 0.0), axis=1, keepdims=True)
    speed = jnp.sum(jnp.where(mine, -jnp.exp(rate[...]), 0.0), axis=1, keepdims=True)
    upper = (iota((BLOCK, BLOCK), 0) <= iota((BLOCK, BLOCK), 1)).astype(BF16)
    steps = []
    for b in range(4):
        far = lax.rem(x - b + 4, 4)
        v = own_steps[...].astype(F32)
        for distance, got in ((1, got_a), (2, got_b), (3, got_c)):
            v = jnp.where(far == distance, got[...].astype(F32), v)
        v = v + shift
        steps.append(jnp.maximum(v, 0.0) + jnp.log1p(jnp.exp(-jnp.abs(v))))
    parts = split(jnp.concatenate([step * speed for step in steps], axis=0))
    parts = jnp.concatenate(parts, axis=0).astype(BF16)
    sums = jnp.dot(parts, upper, preferred_element_type=F32)
    ends = jnp.zeros((8, LANES), F32)
    for b in range(4):
        cum = sums[8 * b : 8 * b + 8] + sums[8 * b + 32 : 8 * b + 40] + sums[8 * b + 64 : 8 * b + 72]
        end = cum[:, BLOCK - 1 : BLOCK]
        ends = jnp.where(iota((8, LANES), 1) == b, end, ends)
        lc_t[b] = cum
        dt_t[b] = steps[b]
        tail[b] = spread_columns(jnp.exp(end - cum) * steps[b], wide)
    decay[...] = spread_columns(jnp.exp(ends), wide)[0:8]
    by_block = columns(ends)
    logs[...] = jnp.broadcast_to(
        by_block[0:1] + by_block[1:2] + by_block[2:3] + by_block[3:4], (8, LANES)
    )


def conv(recv, w_inner, w_pairs, bias, rate, steps):
    members, rows, width = recv.shape
    wide, narrow = w_inner.shape[1], w_pairs.shape[1]
    total = members * rows
    shapes = (
        ((total, wide), BF16),
        ((total, narrow), BF16),
        ((4, 8, BLOCK), F32),
        ((4, 8, BLOCK), F32),
        ((4, BLOCK, wide), F32),
        ((8, wide), F32),
        ((8, LANES), F32),
    )
    return pl.pallas_call(
        conv_kernel,
        out_shape=tuple(jax.ShapeDtypeStruct(*s) for s in shapes),
        in_specs=[VMEM] * 9,
        out_specs=(VMEM,) * len(shapes),
        scratch_shapes=[pltpu.VMEM((8 + total, width), F32)],
        compiler_params=PARAMS,
        cost_estimate=cost(20 * total * width, 4 * total * width, 2 * total * width),
        name="conv",
    )(recv, w_inner, w_pairs, bias, rate, *steps)


def state_kernel(
    first,
    halo,
    w_inner,
    w_pairs,
    xc0,
    bc0,
    tail,
    decay,
    logs,
    xc,
    bc,
    states,
    payload,
    ext,
    head_x,
    head_b,
    local,
    sem,
):
    count = first.shape[0]
    total, wide = xc0.shape
    narrow = bc0.shape[1]
    rest = pl.ds(count, total - count)
    copies = [
        pltpu.make_async_copy(xc0.at[rest], xc.at[rest], sem.at[0]),
        pltpu.make_async_copy(bc0.at[rest], bc.at[rest], sem.at[1]),
        pltpu.make_async_copy(head_x, xc.at[pl.ds(0, count)], sem.at[2]),
        pltpu.make_async_copy(head_b, bc.at[pl.ds(0, count)], sem.at[3]),
    ]
    copies[0].start()
    copies[1].start()
    ext[0:8] = halo[count - 8 : count].astype(F32)
    ext[8 : 8 + count] = first[...].astype(F32)
    for start in range(0, wide, LANES):
        cols = slice(start, start + LANES)
        head_x[:, cols] = taps(ext, 0, count, cols, w_inner[:, cols])
    for start in range(0, narrow, LANES):
        head_b[:, start : start + LANES] = taps(
            ext,
            0,
            count,
            slice(wide + start, wide + start + LANES),
            w_pairs[:, start : start + LANES],
        )
    copies[2].start()
    copies[3].start()
    sum_state = jnp.zeros((LANES, wide), F32)
    for b in range(4):
        rows = slice(b * BLOCK, (b + 1) * BLOCK)
        if b == 0:
            block = jnp.concatenate([head_x[...], xc0[count:BLOCK]], axis=0)
            keys = jnp.concatenate([head_b[:, 0:LANES], bc0[count:BLOCK, 0:LANES]], axis=0)
        else:
            block, keys = xc0[rows], bc0[rows, 0:LANES]
        weighted = (block.astype(F32) * tail[b]).astype(BF16)
        one = lax.dot_general(
            keys, weighted, (((0,), (0,)), ((), ())), preferred_element_type=F32
        )
        local[b] = one
        copies.append(pltpu.make_async_copy(local.at[b], states.at[b], sem.at[4 + b]))
        copies[-1].start()
        sum_state = decay[b : b + 1] * sum_state + one
    parts, depth, _ = payload.shape
    payload[:, :, 0:wide] = sum_state.reshape(parts, depth, wide)
    for part in range(parts):
        for row in range(0, depth, 8):
            payload[part, row : row + 8, wide : wide + LANES] = logs[...]
    for copy in copies:
        copy.wait()


def state(first, halo, w_inner, w_pairs, xc0, bc0, tail, decay, logs, parts):
    count, width = first.shape
    total, wide = xc0.shape
    narrow = width - wide
    payload_shape = (parts, LANES // parts, wide + LANES)
    return pl.pallas_call(
        state_kernel,
        out_shape=(
            pltpu.HBM((total, wide), BF16),
            pltpu.HBM((total, narrow), BF16),
            pltpu.HBM((4, LANES, wide), F32),
            jax.ShapeDtypeStruct(payload_shape, F32),
        ),
        in_specs=[VMEM] * 9,
        out_specs=(ANY, ANY, ANY, VMEM),
        scratch_shapes=[
            pltpu.VMEM((8 + count, width), F32),
            pltpu.VMEM((count, wide), BF16),
            pltpu.VMEM((count, narrow), BF16),
            pltpu.VMEM((4, LANES, wide), F32),
            pltpu.SemaphoreType.DMA((8,)),
        ],
        compiler_params=PARAMS,
        cost_estimate=cost(2 * total * wide * LANES, 8 * total * wide),
        name="state",
    )(first, halo, w_inner, w_pairs, xc0, bc0, tail, decay, logs)


def intra_kernel(xc, bc, lc_t, dt_t, skip, own_gate, got_a, got_b, got_c, out, factor):
    x = lax.rem(lax.axis_index("context"), 4)
    wide = out.shape[1]
    heads = lc_t.shape[1]
    scores = lax.dot_general(
        bc[:, LANES:], bc[:, 0:LANES], (((1,), (1,)), ((), ())), preferred_element_type=F32
    )
    half = BLOCK // 2
    lower = iota((half, half), 0) >= iota((half, half), 1)
    own = skip.shape[1]
    gain = widen(
        jnp.broadcast_to(skip[...], (8, own)),
        (iota((own, wide), 1) // 64 + heads * x == iota((own, wide), 0)).astype(F32),
    )[0:1]
    far = lax.rem(x - pl.program_id(0) + 4, 4)
    gate = own_gate[...].astype(F32)
    for distance, got in ((1, got_a), (2, got_b), (3, got_c)):
        gate = jnp.where(far == distance, got[...].astype(F32), gate)
    gate = silu(gate)
    cum = lc_t[0]
    factor[...] = (gate * spread_columns(jnp.exp(cum), wide)).astype(BF16)
    log2e = 1.4426950408889634
    late = cum * log2e
    early = late - jnp.log(dt_t[0]) * log2e
    late = columns(late)
    top = scores[0:half, 0:half]
    left, right = scores[half:, 0:half], scores[half:, half:]
    for pair in range(heads // 2):
        outs = []
        for h in (2 * pair, 2 * pair + 1):
            upper_col, lower_col = late[0:half, h : h + 1], late[half:, h : h + 1]
            first, second = early[h : h + 1, 0:half], early[h : h + 1, half:]
            values = xc[:, h * 64 : (h + 1) * 64]
            w_top = top * jnp.exp2(jnp.where(lower, upper_col - first, -jnp.inf))
            w_left = left * jnp.exp2(lower_col - first)
            w_right = right * jnp.exp2(jnp.where(lower, lower_col - second, -jnp.inf))
            w_low = jnp.concatenate([w_left, w_right], axis=1).astype(BF16)
            outs.append(
                jnp.concatenate(
                    [
                        jnp.dot(w_top.astype(BF16), values[0:half], preferred_element_type=F32),
                        jnp.dot(w_low, values, preferred_element_type=F32),
                    ],
                    axis=0,
                )
            )
        cols = slice(2 * pair * 64, 2 * (pair + 1) * 64)
        mixed = jnp.concatenate(outs, axis=1) + gain[:, cols] * xc[:, cols].astype(F32)
        out[:, cols] = (mixed * gate[:, cols]).astype(BF16)


def intra(xc, bc, lc_t, dt_t, skip, gates):
    total, wide = xc.shape
    narrow = bc.shape[1]
    heads = lc_t.shape[1]
    return pl.pallas_call(
        intra_kernel,
        out_shape=(jax.ShapeDtypeStruct((total, wide), BF16),) * 2,
        grid=(4,),
        in_specs=[
            pl.BlockSpec((BLOCK, wide), lambda b: (b, 0)),
            pl.BlockSpec((BLOCK, narrow), lambda b: (b, 0)),
            pl.BlockSpec((1, heads, BLOCK), lambda b: (b, 0, 0)),
            pl.BlockSpec((1, heads, BLOCK), lambda b: (b, 0, 0)),
            pl.BlockSpec(skip.shape, lambda b: (0, 0)),
        ]
        + [pl.BlockSpec(gate.shape, lambda b: (0, 0)) for gate in gates],
        out_specs=(pl.BlockSpec((BLOCK, wide), lambda b: (b, 0)),) * 2,
        compiler_params=PARAMS,
        cost_estimate=cost(2 * total * BLOCK * wide * 4, 12 * total * wide, heads * total * BLOCK),
        name="intra",
    )(keep(xc), keep(bc), lc_t, dt_t, skip, *[keep(gate) for gate in gates])


def scan_kernel(recv, out):
    chunks, rows, width = recv.shape
    wide = out.shape[2]
    logs = jnp.concatenate([recv[k, 0:1, wide:width] for k in range(chunks)], axis=0)
    heads = wide // 64
    top, mid, low = split(jnp.where(iota(logs.shape, 1) < heads, jnp.exp(logs), 0.0))
    pieces = top + pltpu.roll(mid, heads, 1) + pltpu.roll(low, 2 * heads, 1)
    row = iota((LANES, wide), 0)
    one_hot = (row % heads == iota((LANES, wide), 1) // 64) & (row < 3 * heads)
    decay = jnp.dot(pieces.astype(BF16), one_hot.astype(BF16), preferred_element_type=F32)
    carry = jnp.zeros((rows, wide), F32)
    for k in range(chunks):
        out[k] = carry
        carry = decay[k : k + 1] * carry + recv[k, :, 0:wide]


def scan(recv):
    chunks, rows, width = recv.shape
    return pl.pallas_call(
        scan_kernel,
        out_shape=jax.ShapeDtypeStruct((chunks, rows, width - LANES), F32),
        in_specs=[VMEM],
        out_specs=VMEM,
        compiler_params=PARAMS,
        cost_estimate=cost(4 * chunks * rows * width, 8 * chunks * rows * width),
        name="scan",
    )(recv)


def finish_kernel(carry, states, decay, bc, mixed, factor, out, s_in, c_in, sem):
    wide = mixed.shape[1]
    copies = []
    for b in range(4):
        rows = pl.ds(b * BLOCK, BLOCK)
        copies.append(
            [
                pltpu.make_async_copy(bc.at[rows, pl.ds(LANES, LANES)], c_in.at[b], sem.at[b, 0]),
                pltpu.make_async_copy(states.at[b], s_in.at[b], sem.at[b, 1]),
            ]
        )
    for group in copies:
        for copy in group:
            copy.start()
    start = carry[...].reshape(LANES, wide)
    for b in range(4):
        for copy in copies[b]:
            copy.wait()
        carried = jnp.dot(c_in[b], start.astype(BF16), preferred_element_type=F32)
        rows = slice(b * BLOCK, (b + 1) * BLOCK)
        gated = mixed[rows].astype(F32) + carried * factor[rows].astype(F32)
        count = BLOCK // out.shape[1]
        out[b * count : (b + 1) * count] = gated.astype(BF16).reshape(count, -1, wide)
        start = decay[b : b + 1] * start + s_in[b]


def finish(carry, states, decay, bc, mixed, factor, rows):
    total, wide = mixed.shape
    return pl.pallas_call(
        finish_kernel,
        out_shape=jax.ShapeDtypeStruct((total // rows, rows, wide), BF16),
        in_specs=[VMEM, ANY, VMEM, ANY, VMEM, VMEM],
        out_specs=VMEM,
        scratch_shapes=[
            pltpu.VMEM((4, LANES, wide), F32),
            pltpu.VMEM((4, BLOCK, LANES), BF16),
            pltpu.SemaphoreType.DMA((4, 2)),
        ],
        compiler_params=PARAMS,
        cost_estimate=cost(2 * total * wide * 200, 6 * total * wide),
        name="finish",
    )(carry, keep(states), decay, keep(bc), mixed, factor)


def post_kernel(slabs, own_gain, got_a, got_b, got_c, out):
    wide = slabs.shape[2]
    for y in range(4):
        far = lax.rem(lax.axis_index("head") - y + 4, 4)
        gain = own_gain[...]
        for distance, got in ((1, got_a), (2, got_b), (3, got_c)):
            gain = jnp.where(far == distance, got[...], gain)
        for half in range(2):
            left, right = 8 * half + y, 8 * half + 4 + y
            a, b = slabs[left].astype(F32), slabs[right].astype(F32)
            mean = (
                jnp.sum(a * a, axis=1, keepdims=True) + jnp.sum(b * b, axis=1, keepdims=True)
            ) / (2 * wide)
            inv = lax.rsqrt(mean + 1e-5)
            at = 2 * half * wide
            low, high = gain[:, at : at + wide], gain[:, at + wide : at + 2 * wide]
            at = at + 4 * y * wide
            out[:, at : at + wide] = (a * inv * low).astype(BF16)
            out[:, at + wide : at + 2 * wide] = (b * inv * high).astype(BF16)


def post(slabs, gains):
    members, rows, wide = slabs.shape
    return pl.pallas_call(
        post_kernel,
        out_shape=jax.ShapeDtypeStruct((rows, members * wide), BF16),
        in_specs=[VMEM] * 5,
        out_specs=VMEM,
        compiler_params=PARAMS,
        cost_estimate=cost(6 * members * rows * wide, 4 * members * rows * wide),
        name="post",
    )(slabs, *gains)


def on_device(
    inner_raw,
    pairs_raw,
    gate_raw,
    step_raw,
    step_bias,
    rate_log,
    skip_gain,
    conv_inner,
    conv_pairs,
    norm_gain,
):
    places = lax.axis_size("context")
    shards = lax.axis_size("head")
    chunks = places // 4
    x = (lax.axis_index("context") % 4).astype(jnp.int32)
    rows = inner_raw.shape[0]
    after = [(c, c + 4) for c in range(places - 4)]
    teams = [list(range(TEAM * k, TEAM * (k + 1))) for k in range(places * shards // TEAM)]
    lines = [[4 * k + s for k in range(chunks)] for s in range(4)]

    def around(axis, position, pick):
        count = lax.axis_size(axis)
        routes = [[(c, c - c % 4 + (c + far) % 4) for c in range(count)] for far in (1, 2, 3)]
        return [
            lax.ppermute(pick((position + far) % 4), axis, route)
            for far, route in zip((1, 2, 3), routes)
        ]

    packed = pack(inner_raw, pairs_raw)
    step_rows = step_raw.T
    gain_row = norm_gain.reshape(1, -1)
    gate_later, steps_later, gain_later, w_inner, w_pairs, packed = lax.optimization_barrier(
        (gate_raw, step_rows, gain_row, conv_inner, conv_pairs, packed)
    )
    recv = lax.all_to_all(
        packed, ("context", "head"), split_axis=0, concat_axis=0, axis_index_groups=teams
    )
    width = gate_raw.shape[1] // 4
    y = lax.axis_index("head").astype(jnp.int32)
    steps = around("context", x, lambda p: lax.dynamic_slice_in_dim(steps_later, 8 * p, 8, 0))
    gains = around("head", y, lambda p: gain_later)
    gates = around(
        "context", x, lambda p: lax.dynamic_slice_in_dim(gate_later, p * width, width, 1)
    )
    *steps, recv = lax.optimization_barrier((*steps, recv))
    halo = lax.ppermute(recv[TEAM - 1, rows - 16 : rows], "context", after)

    own_steps = lax.dynamic_slice_in_dim(steps_later, 8 * x, 8, 0)
    own_gate = lax.dynamic_slice_in_dim(gate_later, x * width, width, 1)
    w_pairs = w_pairs.reshape(w_pairs.shape[0], -1)
    wide, narrow = w_inner.shape[1] // TEAM, w_pairs.shape[1] // 8
    w_inner = lax.dynamic_slice_in_dim(w_inner, (4 * y + x) * wide, wide, 1)
    w_pairs = lax.dynamic_slice_in_dim(w_pairs, (2 * y + x // 2) * narrow, narrow, 1)
    xc0, bc0, lc_t, dt_t, tail, decay, logs = conv(
        recv,
        w_inner,
        w_pairs,
        step_bias.reshape(1, -1),
        rate_log.reshape(1, -1),
        [own_steps] + steps,
    )
    xc, bc, states, payload = state(
        recv[0, :16], halo, w_inner, w_pairs, xc0, bc0, tail, decay, logs, chunks
    )
    gates[0], gates[1], payload = lax.optimization_barrier((gates[0], gates[1], payload))
    totals = lax.all_to_all(
        payload, "context", split_axis=0, concat_axis=0, axis_index_groups=lines
    )
    gates[2], *gains, totals = lax.optimization_barrier((gates[2], *gains, totals))
    carry = lax.all_to_all(
        scan(totals), "context", split_axis=0, concat_axis=0, axis_index_groups=lines
    )
    mixed, factor = intra(xc, bc, lc_t, dt_t, skip_gain.reshape(1, -1), [own_gate] + gates)
    slabs = finish(carry, states, decay, bc, mixed, factor, rows)
    slabs = lax.all_to_all(
        slabs, ("context", "head"), split_axis=0, concat_axis=0, axis_index_groups=teams
    )
    return post(slabs, [gain_row] + gains)


def solution(mesh):
    placed = (
        P(("rollout", "context", "head"), None),
        P(("rollout", "context", "head"), None, None, None),
        P(("rollout", "context"), "head"),
        P(("rollout", "context"), "head"),
        P("head"),
        P("head"),
        P("head"),
        P(),
        P(),
        P("head"),
    )
    return jax.shard_map(
        on_device,
        mesh=mesh,
        in_specs=placed,
        out_specs=P(("rollout", "context", "head"), None),
        check_vma=False,
    )
```
